32 devices in a mesh: dp: 8 (over y, x, core), tensor: 4 (over z).
Axes of the slice: x: 2, y: 2, z: 4, core: 2. Of those that a mesh axis runs over, the one named last changes fastest.
Arguments:
- word_in: bfloat16 [16384, 768], P('dp'), may hold values from -6 to 6
- entity_in: bfloat16 [4096, 768], P('dp'), may hold values from -6 to 6
- entity_spans: int32 [32, 128, 2], P('dp'), may hold values from 0 to 512, as said below
- word_mask: int32 [32, 512], P('dp'), may hold values 0 or 1
- entity_mask: int32 [32, 128], P('dp'), may hold values 0 or 1
- pos_table: bfloat16 [512, 768], replicated, may hold values from -6 to 6
- query_w: bfloat16 [4, 768, 768], P(None, None, 'tensor'), may hold values from -0.21875 to 0.21875
- query_b: bfloat16 [4, 768], P(None, 'tensor'), may hold values from -3 to 3
- key_w: bfloat16 [768, 768], P(None, 'tensor'), may hold values from -0.21875 to 0.21875
- value_w: bfloat16 [768, 768], P(None, 'tensor'), may hold values from -0.21875 to 0.21875
- value_b: bfloat16 [768], P('tensor'), may hold values from -0.29882812 to 0.29882812
- out_w: bfloat16 [768, 768], P('tensor'), may hold values from -3.5 to 3.5
- out_b: bfloat16 [768], replicated, may hold values from -3 to 3
- norm1_gain: bfloat16 [768], replicated, may hold values from 0.099609375 to 1.8984375
- norm1_bias: bfloat16 [768], replicated, may hold values from -2 to 2
- up_w: bfloat16 [768, 3072], P(None, 'tensor'), may hold values from -0.21875 to 0.21875
- up_b: bfloat16 [3072], P('tensor'), may hold values from -3 to 3
- down_w: bfloat16 [3072, 768], P('tensor'), may hold values from -0.109375 to 0.109375
- down_b: bfloat16 [768], replicated, may hold values from -3 to 3
- norm2_gain: bfloat16 [768], replicated, may hold values from 0.099609375 to 1.8984375
- norm2_bias: bfloat16 [768], replicated, may hold values from -2 to 2
- cot_words: bfloat16 [16384, 768], P(('dp', 'tensor')), may hold values from -6 to 6
- cot_entities: bfloat16 [4096, 768], P(('dp', 'tensor')), may hold values from -6 to 6
Outputs:
- out_words: bfloat16 [16384, 768], P(('dp', 'tensor'))
- out_entities: bfloat16 [4096, 768], P(('dp', 'tensor'))
- grad_words: float32 [16384, 768], P(('dp', 'tensor'))
- grad_entities: float32 [4096, 768], P(('dp', 'tensor'))
- grad_pos: float32 [512, 768], replicated
- grad_query_w: float32 [4, 768, 768], P(None, None, 'tensor')
- grad_query_b: float32 [4, 768], P(None, 'tensor')
- grad_key_w: float32 [768, 768], P(None, 'tensor')
- grad_value_w: float32 [768, 768], P(None, 'tensor')
- grad_value_b: float32 [768], P('tensor')
- grad_out_w: float32 [768, 768], P('tensor')
- grad_out_b: float32 [768], replicated
- grad_norm1_gain: float32 [768], replicated
- grad_norm1_bias: float32 [768], replicated
- grad_up_w: float32 [768, 3072], P(None, 'tensor')
- grad_up_b: float32 [3072], P('tensor')
- grad_down_w: float32 [3072, 768], P('tensor')
- grad_down_b: float32 [768], replicated
- grad_norm2_gain: float32 [768], replicated
- grad_norm2_bias: float32 [768], replicated
The draws below stay inside these ranges and needn't reach their ends.
Inputs may be any that keep to these rules, and one draw needn't show every extreme that they name: entity_spans[s, e] = (start, end): entity e of sequence s covers words start to end - 1, 1 to 30 words; in every sequence entity 0 covers words 0 to 29 and entity 1 ends at the last word.
All inputs are finite; a program needn't handle non-finite values. No bound on the sum of `word_mask` or of `entity_mask` on one device may be relied on, other than what follows from the above.
Results may differ from the reference program's by a relative error of at most 0.015.
The reference program's roundings to bfloat16 on the way count: a program that leaves them out, or rounds other values in their place, can miss the bound.
Values may be sent and summed in bfloat16 or wider, within the bound.
No kernel may reach another device: no remote copies, remote signals or barrier semaphores. Data moves between devices by JAX's collectives and lax.ppermute only.
A program may use at most 128 MiB of HBM per device.

```python
import jax
import jax.numpy as jnp
from jax import lax

D = 768
HEADS = 12
HEAD_DIM = 64
FF = 3072
LW = 512
NE = 128
SPAN_MAX = 30
SEQS = 32


def draw_entity_spans(key, part):
    key_length = jax.random.fold_in(key, 31)
    key_start = jax.random.fold_in(key, 37)
    lengths = jax.random.randint(key_length, (SEQS, NE), 1, SPAN_MAX + 1)
    starts_drawn = jax.random.randint(key_start, (SEQS, NE), 0, LW - SPAN_MAX + 1)
    column = jnp.arange(NE)[None, :]
    lengths = jnp.where(column == 0, SPAN_MAX, lengths)
    starts = jnp.where(column == 0, 0, jnp.where(column == 1, LW - lengths, starts_drawn))
    return jnp.stack([starts, starts + lengths], -1).astype(jnp.int32)


def place_ends(drawn, stream_key, smallest, largest):
    dims = drawn.shape
    place = [jax.random.randint(jax.random.fold_in(stream_key, axis), (), 0, dims[axis]) for axis in range(len(dims))]
    drawn = drawn.at[tuple(place)].set(smallest)
    longest = dims.index(max(dims))
    place[longest] = (place[longest] + 1) % dims[longest]
    return drawn.at[tuple(place)].set(largest)


def levels(own_key, dims, shards, least, high):
    def one(axis_at, parts):
        heights = jax.random.uniform(jax.random.fold_in(jax.random.fold_in(own_key, 6), axis_at), (parts,), jnp.float32, least / len(shards), high / len(shards))
        return jnp.repeat(jnp.exp(heights), dims[axis_at] // parts).reshape((-1,) + (1,) * (len(dims) - axis_at - 1))

    level = one(*shards[0])
    for cut in shards[1:]:
        level = level * one(*cut)
    return level


def bell_draw(key, dims, spread, limit, pieces=(), kind=jnp.bfloat16):
    level = levels(key, dims, pieces, -0.22, 0.18) if pieces else 1.0
    entries = jax.random.normal(key, dims, jnp.float32) * spread * level
    return jnp.minimum(jnp.maximum(entries, -limit), limit).astype(kind)


def setup_inputs(seed: int = 0) -> dict:
    keys = jax.random.split(jax.random.key(seed), 24)
    return {
        "word_in": bell_draw(keys[0], (SEQS * LW, D), 1.0, 6.0, ((0, 8),)),
        "entity_in": bell_draw(keys[1], (SEQS * NE, D), 1.0, 6.0, ((0, 8),)),
        "entity_spans": draw_entity_spans(jax.random.fold_in(keys[23], 71), 0),
        "word_mask": place_ends((jax.random.randint(keys[3], (SEQS, LW), 0, 100) < 15).astype(jnp.int32), jax.random.fold_in(keys[3], 1), 0, 1),
        "entity_mask": place_ends((jax.random.randint(keys[4], (SEQS, NE), 0, 100) < 15).astype(jnp.int32), jax.random.fold_in(keys[4], 1), 0, 1),
        "pos_table": bell_draw(keys[5], (LW, D), 1.0, 6.0),
        "query_w": bell_draw(keys[6], (4, D, D), D ** -0.5, 0.21875, ((2, 4),)),
        "query_b": bell_draw(keys[7], (4, D), 0.5, 3.0, ((1, 4),)),
        "key_w": bell_draw(keys[8], (D, D), D ** -0.5, 0.21875, ((1, 4),)),
        "value_w": bell_draw(keys[9], (D, D), D ** -0.5, 0.21875, ((1, 4),)),
        "value_b": bell_draw(keys[10], (D,), 0.05, 0.29882812, ((0, 4),)),
        "out_w": bell_draw(keys[11], (D, D), (max(1, 3 * D // (LW + NE))) ** -0.5, 3.5, ((0, 4),)),
        "out_b": bell_draw(keys[12], (D,), 0.5, 3.0),
        "norm1_gain": jnp.clip(1.0 + 0.18 * jax.random.normal(keys[13], (D,), jnp.float32), 0.099609375, 1.8984375).astype(jnp.bfloat16),
        "norm1_bias": bell_draw(keys[14], (D,), 0.3, 2.0),
        "up_w": bell_draw(keys[15], (D, FF), D ** -0.5, 0.21875, ((1, 4),)),
        "up_b": bell_draw(keys[16], (FF,), 0.5, 3.0, ((0, 4),)),
        "down_w": bell_draw(keys[17], (FF, D), FF ** -0.5, 0.109375, ((0, 4),)),
        "down_b": bell_draw(keys[18], (D,), 0.5, 3.0),
        "norm2_gain": jnp.clip(1.0 + 0.18 * jax.random.normal(keys[19], (D,), jnp.float32), 0.099609375, 1.8984375).astype(jnp.bfloat16),
        "norm2_bias": bell_draw(keys[20], (D,), 0.3, 2.0),
        "cot_words": bell_draw(keys[21], (SEQS * LW, D), 1.0, 6.0, ((0, 32),)),
        "cot_entities": bell_draw(keys[22], (SEQS * NE, D), 1.0, 6.0, ((0, 32),)),
    }


norm_epsilon = 1e-12
highest = lax.Precision.HIGHEST

@jax.custom_vjp
def low(v):
    return lax.optimization_barrier(v.astype(jnp.bfloat16)).astype(jnp.float32)

@jax.custom_vjp
def low_back(v):
    return v

def low_keep(v):
    return (low(v), None)

def low_pass(kept, grad):
    return (grad,)

def back_keep(v):
    return (v, None)

def back_low(kept, grad):
    return (low(grad),)
low.defvjp(low_keep, low_pass)
low_back.defvjp(back_keep, back_low)

def matmul_high(left, right):
    return jnp.dot(left, right, precision=highest, preferred_element_type=jnp.float32)

def span_weights(entity_spans, word_count):
    word_pos = lax.broadcasted_iota(jnp.int32, (entity_spans.shape[0], entity_spans.shape[1], word_count), 2)
    span_start = entity_spans[:, :, 0:1]
    span_end = entity_spans[:, :, 1:2]
    inside = jnp.logical_and(word_pos >= span_start, word_pos < span_end)
    return jnp.where(inside, 1.0, 0.0).astype(jnp.float32) / (span_end - span_start).astype(jnp.float32)

def layer_norm(values, gain_row, shift_row):
    row_mean = lax.optimization_barrier(jnp.mean(values, axis=-1, keepdims=True))
    centered = values - row_mean
    row_var = lax.optimization_barrier(jnp.mean(centered * centered, axis=-1, keepdims=True))
    return centered * lax.rsqrt(row_var + norm_epsilon) * gain_row + shift_row

def sequence_loss(params, word_rows, ent_input, member, row_mask, cotangent):
    pos_table, query_w, query_b, key_w, value_w, value_b, out_w, out_b, norm1_gain, norm1_bias, up_w, up_b, down_w, down_b, norm2_gain, norm2_bias = params
    word_count = word_rows.shape[0]
    ent_rows = ent_input + matmul_high(member, pos_table)
    layer_rows = jnp.concatenate([word_rows, ent_rows], 0)
    seq_len = layer_rows.shape[0]
    rows_low = low(layer_rows)
    words_low = rows_low[:word_count]
    ents_low = rows_low[word_count:]
    to_words = jnp.concatenate([matmul_high(words_low, query_w[0]) + query_b[0], matmul_high(ents_low, query_w[2]) + query_b[2]], 0)
    to_entities = jnp.concatenate([matmul_high(words_low, query_w[1]) + query_b[1], matmul_high(ents_low, query_w[3]) + query_b[3]], 0)
    to_words = low_back(low(to_words))
    to_entities = low_back(low(to_entities))
    key_rows = low_back(low(matmul_high(rows_low, key_w)))
    value_rows = low_back(low(matmul_high(rows_low, value_w) + value_b))

    def split_heads(values):
        return values.reshape(seq_len, HEADS, HEAD_DIM)
    key_heads = split_heads(key_rows)
    score_words = jnp.einsum('qhd,khd->hqk', split_heads(to_words), key_heads[:word_count], precision=highest)
    score_ents = jnp.einsum('qhd,khd->hqk', split_heads(to_entities), key_heads[word_count:], precision=highest)
    scores = low_back(jnp.concatenate([score_words, score_ents], 2) * HEAD_DIM ** (-0.5))
    row_max = lax.optimization_barrier(jnp.max(scores, axis=2, keepdims=True))
    exp_scores = jnp.exp(scores - row_max)
    prob_low = low(exp_scores / lax.optimization_barrier(jnp.sum(exp_scores, axis=2, keepdims=True)))
    context = jnp.einsum('hqk,khd->qhd', prob_low, split_heads(value_rows), precision=highest)
    context = low_back(low(context.reshape(seq_len, HEADS * HEAD_DIM)))
    attended = layer_rows + low_back(matmul_high(context, out_w)) + out_b
    normed = layer_norm(attended, norm1_gain, norm1_bias)
    hidden_pre = low_back(matmul_high(low(normed), up_w) + up_b)
    activation = low(jax.nn.gelu(hidden_pre, approximate=False))
    mixed_rows = normed + low_back(matmul_high(activation, down_w)) + down_b
    output = layer_norm(mixed_rows, norm2_gain, norm2_bias)
    return (jnp.sum(row_mask[:, None] * cotangent * output), output)

def reference(word_in, entity_in, entity_spans, word_mask, entity_mask, pos_table, query_w, query_b, key_w, value_w, value_b, out_w, out_b, norm1_gain, norm1_bias, up_w, up_b, down_w, down_b, norm2_gain, norm2_bias, cot_words, cot_entities):
    params = tuple((item.astype(jnp.float32) for item in (pos_table, query_w, query_b, key_w, value_w, value_b, out_w, out_b, norm1_gain, norm1_bias, up_w, up_b, down_w, down_b, norm2_gain, norm2_bias)))
    seq_total = entity_spans.shape[0]
    word_seq = word_in.astype(jnp.float32).reshape(seq_total, LW, D)
    ent_seq = entity_in.astype(jnp.float32).reshape(seq_total, NE, D)
    cot_seq = jnp.concatenate([cot_words.astype(jnp.float32).reshape(seq_total, LW, D), cot_entities.astype(jnp.float32).reshape(seq_total, NE, D)], 1)
    mask_seq = jnp.concatenate([word_mask, entity_mask], 1).astype(jnp.float32)
    member_seq = span_weights(entity_spans, LW)

    def per_sequence(grad_total, inputs):
        word_rows, ent_input, member, row_mask, cotangent = inputs

        def loss_of(params_in, words_in, ents_in):
            return sequence_loss(params_in, words_in, ents_in, member, row_mask, cotangent)
        loss_value, back_fn, output = jax.vjp(loss_of, params, word_rows, ent_input, has_aux=True)
        grad_params, grad_word_rows, grad_ent_rows = back_fn(jnp.ones_like(loss_value))
        grad_total = jax.tree.map(lambda running, adding: running + adding, grad_total, grad_params)
        return (grad_total, (output, grad_word_rows, grad_ent_rows))
    zero_grads = jax.tree.map(jnp.zeros_like, params)
    grad_params, (outputs, grad_word_seq, grad_ent_seq) = lax.scan(per_sequence, zero_grads, (word_seq, ent_seq, member_seq, mask_seq, cot_seq))
    out_words = outputs[:, :LW].reshape(seq_total * LW, D).astype(jnp.bfloat16)
    out_entities = outputs[:, LW:].reshape(seq_total * NE, D).astype(jnp.bfloat16)
    grad_words = grad_word_seq.reshape(seq_total * LW, D)
    grad_entities = grad_ent_seq.reshape(seq_total * NE, D)
    return (out_words, out_entities, grad_words, grad_entities, grad_params[0], grad_params[1], grad_params[2], grad_params[3], grad_params[4], grad_params[5], grad_params[6], grad_params[7], grad_params[8], grad_params[9], grad_params[10], grad_params[11], grad_params[12], grad_params[13], grad_params[14], grad_params[15])
```

```python
from functools import partial

import jax
import jax.numpy as jnp
from jax import lax
from jax.experimental import pallas as pl
from jax.experimental.pallas import tpu as pltpu
from jax.sharding import PartitionSpec as P

HEAD_DIM = 64
norm_epsilon = 1e-12
F32 = jnp.float32
BF16 = jnp.bfloat16
NT = (((1,), (1,)), ((), ()))
TN = (((0,), (0,)), ((), ()))


def mm(a, b):
    return jnp.dot(a, b, preferred_element_type=F32)


def mm_nt(a, b):
    return lax.dot_general(a, b, NT, preferred_element_type=F32)


def mm_tn(a, b):
    return lax.dot_general(a, b, TN, preferred_element_type=F32)


def attn_forward_kernel(
    words, ents, gw, heads, rows_ref, w_ref, b_ref, pw_ref, pe_ref, ctx_ref, lt_ref, qw_s, qe_s, k_s, v_s
):
    half = 2 * gw
    pw_ref[...] = (mm(rows_ref[:words], w_ref[:, : 4 * gw]) + b_ref[:, : 4 * gw]).astype(BF16)
    pe_ref[...] = (mm(rows_ref[words:], w_ref[:, half:]) + b_ref[:, half:]).astype(BF16)
    for h in range(heads):
        o = h * HEAD_DIM
        e = o + HEAD_DIM
        qw_s[h, :words] = pw_ref[:, o:e]
        qw_s[h, words:] = pe_ref[:, half + o : half + e]
        qe_s[h, :words] = pw_ref[:, gw + o : gw + e]
        qe_s[h, words:] = pe_ref[:, half + gw + o : half + gw + e]
        k_s[h, :words] = pw_ref[:, half + o : half + e]
        k_s[h, words:] = pe_ref[:, o:e]
        v_s[h, :words] = pw_ref[:, half + gw + o : half + gw + e]
        v_s[h, words:] = pe_ref[:, gw + o : gw + e]

    scale = HEAD_DIM**-0.5
    block = 128

    def step(qb, carry):
        rows = pl.ds(pl.multiple_of(qb * block, block), block)
        parts = []
        for h in range(heads):
            sw = mm_nt(qw_s[h, rows], k_s[h, :words])
            se = mm_nt(qe_s[h, rows], k_s[h, words:])
            top = jnp.maximum(jnp.max(sw, 1, keepdims=True), jnp.max(se, 1, keepdims=True))
            ew = jnp.exp((sw - top) * scale)
            ee = jnp.exp((se - top) * scale)
            total = jnp.sum(ew, 1, keepdims=True) + jnp.sum(ee, 1, keepdims=True)
            inv = 1.0 / total
            ctx = mm((ew * inv).astype(BF16), v_s[h, :words]) + mm(
                (ee * inv).astype(BF16), v_s[h, words:]
            )
            parts.append(ctx)
            logt = top * scale + jnp.log(total)
            lt_ref[h : h + 1, rows] = jnp.broadcast_to(logt, (block, block)).T[0:1]
        ctx_ref[rows, :] = jnp.concatenate(parts, 1).astype(BF16)
        return carry

    lax.fori_loop(0, rows_ref.shape[0] // block, step, 0)


def attn_forward(rows_low, weight, bias, words, heads):
    total, width = rows_low.shape
    ents = total - words
    gw = heads * HEAD_DIM
    return pl.pallas_call(
        partial(attn_forward_kernel, words, ents, gw, heads),
        out_shape=(
            jax.ShapeDtypeStruct((words, 4 * gw), BF16),
            jax.ShapeDtypeStruct((ents, 4 * gw), BF16),
            jax.ShapeDtypeStruct((total, gw), BF16),
            jax.ShapeDtypeStruct((8, total), F32),
        ),
        scratch_shapes=[pltpu.VMEM((heads, total, HEAD_DIM), BF16) for _ in range(4)],
        compiler_params=pltpu.CompilerParams(vmem_limit_bytes=24 << 20),
        cost_estimate=pl.CostEstimate(
            flops=2 * total * width * 4 * gw + 4 * total * total * 256 * heads,
            bytes_accessed=6 << 20,
            transcendentals=heads * total * total,
        ),
    )(rows_low, weight, bias)


def attn_backward_kernel(
    words,
    gw,
    heads,
    rt_ref,
    pw_ref,
    pe_ref,
    lt_ref,
    dctx_ref,
    w_ref,
    acc_ref,
    dw_ref,
    out_ref,
    db_ref,
    qw_s,
    qe_s,
    k_s,
    v_s,
    dc_s,
    p_s,
    ds_s,
    dpw_s,
    dpe_s,
):
    half = 2 * gw
    total = rt_ref.shape[1]
    for h in range(heads):
        o = h * HEAD_DIM
        e = o + HEAD_DIM
        qw_s[h, :words] = pw_ref[:, o:e]
        qw_s[h, words:] = pe_ref[:, half + o : half + e]
        qe_s[h, :words] = pw_ref[:, gw + o : gw + e]
        qe_s[h, words:] = pe_ref[:, half + gw + o : half + gw + e]
        k_s[h, :words] = pw_ref[:, half + o : half + e]
        k_s[h, words:] = pe_ref[:, o:e]
        v_s[h, :words] = pw_ref[:, half + gw + o : half + gw + e]
        v_s[h, words:] = pe_ref[:, gw + o : gw + e]
        dc_s[h] = dctx_ref[:, o:e]
    scale = HEAD_DIM**-0.5
    block = 128
    for h in range(heads):
        o = h * HEAD_DIM
        e = o + HEAD_DIM

        def step(qb, carry):
            rows = pl.ds(pl.multiple_of(qb * block, block), block)
            logt = lt_ref[h : h + 1, rows]
            pw = jnp.exp(mm_nt(k_s[h, :words], qw_s[h, rows]) * scale - logt)
            pe = jnp.exp(mm_nt(k_s[h, words:], qe_s[h, rows]) * scale - logt)
            gw_ = mm_nt(v_s[h, :words], dc_s[h, rows])
            ge_ = mm_nt(v_s[h, words:], dc_s[h, rows])
            p_s[:words, rows] = pw.astype(BF16)
            p_s[words:, rows] = pe.astype(BF16)
            dot = jnp.sum(pw * gw_, 0, keepdims=True) + jnp.sum(pe * ge_, 0, keepdims=True)
            ds_s[:words, rows] = (pw * (gw_ - dot)).astype(BF16)
            ds_s[words:, rows] = (pe * (ge_ - dot)).astype(BF16)
            return carry

        lax.fori_loop(0, total // block, step, 0)
        dv = mm(p_s[...], dc_s[h]).astype(BF16)
        dkw = (mm(ds_s[:words], qw_s[h]) * scale).astype(BF16)
        dke = (mm(ds_s[words:], qe_s[h]) * scale).astype(BF16)
        dqw = (mm_tn(ds_s[:words], k_s[h, :words]) * scale).astype(BF16)
        dqe = (mm_tn(ds_s[words:], k_s[h, words:]) * scale).astype(BF16)
        dpw_s[:, o:e] = dqw[:words]
        dpw_s[:, gw + o : gw + e] = dqe[:words]
        dpw_s[:, half + o : half + e] = dkw
        dpw_s[:, half + gw + o : half + gw + e] = dv[:words]
        dpe_s[:, o:e] = dke
        dpe_s[:, gw + o : gw + e] = dv[words:]
        dpe_s[:, half + o : half + e] = dqw[words:]
        dpe_s[:, half + gw + o : half + gw + e] = dqe[words:]
    dpw = dpw_s[...]
    dpe = dpe_s[...]
    dw_ref[:, :half] = mm(rt_ref[:, :words], dpw[:, :half]).astype(BF16)
    dw_ref[:, half : 2 * half] = (
        mm(rt_ref[:, :words], dpw[:, half:]) + mm(rt_ref[:, words:], dpe[:, :half])
    ).astype(BF16)
    dw_ref[:, 2 * half :] = mm(rt_ref[:, words:], dpe[:, half:]).astype(BF16)
    out_ref[:words] = acc_ref[:words] + mm_nt(dpw, w_ref[:, : 2 * half])
    out_ref[words:] = acc_ref[words:] + mm_nt(dpe, w_ref[:, half:])
    sw = jnp.sum(dpw.astype(F32), 0, keepdims=True)
    se = jnp.sum(dpe.astype(F32), 0, keepdims=True)
    db_ref[0:1, :half] = sw[:, :half]
    db_ref[0:1, half : 2 * half] = sw[:, half:] + se[:, :half]
    db_ref[0:1, 2 * half :] = se[:, half:]


def attn_backward(rows_t, proj_w, proj_e, log_total, grad_ctx, weight, acc, heads):
    width, total = rows_t.shape
    words = proj_w.shape[0]
    ents = total - words
    gw = heads * HEAD_DIM
    return pl.pallas_call(
        partial(attn_backward_kernel, words, gw, heads),
        out_shape=(
            jax.ShapeDtypeStruct((width, 6 * gw), BF16),
            jax.ShapeDtypeStruct((total, width), F32),
            jax.ShapeDtypeStruct((8, 6 * gw), F32),
        ),
        scratch_shapes=[pltpu.VMEM((heads, total, HEAD_DIM), BF16) for _ in range(5)]
        + [
            pltpu.VMEM((total, total), BF16),
            pltpu.VMEM((total, total), BF16),
            pltpu.VMEM((words, 4 * gw), BF16),
            pltpu.VMEM((ents, 4 * gw), BF16),
        ],
        input_output_aliases={6: 1},
        compiler_params=pltpu.CompilerParams(vmem_limit_bytes=40 << 20),
        cost_estimate=pl.CostEstimate(
            flops=4 * total * width * 4 * gw + 10 * total * total * 256 * heads,
            bytes_accessed=12 << 20,
            transcendentals=heads * total * total,
        ),
    )(rows_t, proj_w, proj_e, log_total, grad_ctx, weight, acc)


def norm_forward(values, gain_row, shift_row):
    row_mean = jnp.mean(values, axis=-1, keepdims=True)
    centered = values - row_mean
    row_var = jnp.mean(centered * centered, axis=-1, keepdims=True)
    inv_std = lax.rsqrt(row_var + norm_epsilon)
    scaled = centered * inv_std
    return (scaled * gain_row + shift_row, scaled, inv_std)


def norm_backward(grad_in, scaled, inv_std, gain_row):
    grad_gain = jnp.sum(grad_in * scaled, axis=0)
    grad_shift = jnp.sum(grad_in, axis=0)
    grad_scaled = grad_in * gain_row
    mean_first = jnp.mean(grad_scaled, axis=-1, keepdims=True)
    mean_second = jnp.mean(grad_scaled * scaled, axis=-1, keepdims=True)
    return (inv_std * (grad_scaled - mean_first - scaled * mean_second), grad_gain, grad_shift)


def exact_gelu(values):
    return jax.nn.gelu(values, approximate=False)


class Links:
    def __init__(self):
        self.dp = lax.axis_size("dp")
        self.ring = lax.axis_size("tensor")
        dp_index = lax.axis_index("dp")
        self.z = lax.axis_index("tensor")
        self.core = dp_index % 2
        self.bits = (self.dp // 2).bit_length() - 1
        self.bit = [(dp_index // (2 << k)) % 2 for k in range(self.bits)]

    def next_z(self, v):
        n = self.ring
        return lax.ppermute(v, "tensor", [(i, (i + 1) % n) for i in range(n)])

    def shift_z(self, v, by):
        n = self.ring
        return lax.ppermute(v, "tensor", [(i, (i + by) % n) for i in range(n)])

    def swap_z(self, v, mask):
        return lax.ppermute(v, "tensor", [(i, i ^ mask) for i in range(self.ring)])

    def swap_core(self, v):
        return lax.ppermute(v, "dp", [(i, i ^ 1) for i in range(self.dp)])

    def swap_bit(self, v, k):
        return lax.ppermute(v, "dp", [(i, i ^ (2 << k)) for i in range(self.dp)])


def take_rows(v, start, size):
    return lax.dynamic_slice_in_dim(v, start, size, 0)


def gather_stage(links, own, k):
    quarter = own.shape[0] // 4
    part = 2 * links.core + links.bit[k]
    cur = take_rows(own, part * quarter, quarter)
    groups = []
    for _ in range(links.ring - 1):
        cur = links.next_z(cur)
        other = links.swap_bit(cur, k)
        groups.append((cur, other, links.swap_core(cur), links.swap_core(other)))
    return groups


def assemble(links, pieces, k):
    part = 2 * links.core + links.bit[k]
    quarter = pieces[0].shape[0]
    buf = jnp.zeros((4 * quarter,) + pieces[0].shape[1:], pieces[0].dtype)
    for i, piece in enumerate(pieces):
        buf = lax.dynamic_update_slice_in_dim(buf, piece, (part ^ i) * quarter, 0)
    return buf


def add_low(a, b):
    return (a.astype(F32) + b.astype(F32)).astype(BF16)


def join_rows(mine, other, flag):
    return jnp.where(flag == 0, jnp.concatenate([mine, other], 0), jnp.concatenate([other, mine], 0))


def reduce_group(links, grad, k):
    half = grad.shape[0] // 2
    c = links.core
    kept = add_low(take_rows(grad, c * half, half), links.swap_core(take_rows(grad, (1 - c) * half, half)))
    b = links.bit[k]
    quarter = half // 2
    return add_low(
        take_rows(kept, b * quarter, quarter),
        links.swap_bit(take_rows(kept, (1 - b) * quarter, quarter), k),
    )


def reduce_stage(links, grads, k):
    n = links.ring
    order = list(range(1, n)) + [0]
    acc = None
    for r in order:
        quarter = reduce_group(links, grads[r], k)
        acc = quarter if acc is None else add_low(quarter, links.next_z(acc))
    for j in range(links.bits):
        if j != k:
            acc = add_low(acc, links.swap_bit(acc, j))
    other = links.swap_bit(acc, k)
    return assemble(links, (acc, other, links.swap_core(acc), links.swap_core(other)), k)


def reduce_everywhere(links, v):
    v = v + links.swap_core(v)
    for j in range(links.bits):
        v = v + links.swap_bit(v, j)
    mask = 1
    while mask < links.ring:
        v = v + links.swap_z(v, mask)
        mask *= 2
    return v


def reduce_pos(links, v):
    flags = [(links.core, links.swap_core)] + [
        (links.bit[j], partial(links.swap_bit, k=j)) for j in range(min(2, links.bits))
    ]
    for flag, swap in flags:
        half = v.shape[0] // 2
        v = add_low(take_rows(v, flag * half, half), swap(take_rows(v, (1 - flag) * half, half)))
    for j in range(2, links.bits):
        v = add_low(v, links.swap_bit(v, j))
    mask = 1
    while mask < links.ring:
        v = add_low(v, links.swap_z(v, mask))
        mask *= 2
    for flag, swap in reversed(flags):
        v = join_rows(v, swap(v), flag)
    return v


def shards(
    word_in,
    entity_in,
    entity_spans,
    word_mask,
    entity_mask,
    pos_table,
    query_w,
    query_b,
    key_w,
    value_w,
    value_b,
    out_w,
    out_b,
    norm1_gain,
    norm1_bias,
    up_w,
    up_b,
    down_w,
    down_b,
    norm2_gain,
    norm2_bias,
    cot_words,
    cot_entities,
):
    links = Links()
    n = links.ring
    z = links.z
    words = cot_words.shape[0]
    ents = cot_entities.shape[0]
    width = word_in.shape[1]
    gw = key_w.shape[1]
    heads = gw // HEAD_DIM
    ff = up_w.shape[1]

    qkv_own = jnp.concatenate([query_w[0], query_w[1], key_w, value_w, query_w[2], query_w[3]], 1)
    ffn_own = jnp.concatenate([out_w, up_w, down_w], 0)
    bias_own = jnp.concatenate(
        [query_b[0], query_b[1], jnp.zeros((gw,), BF16), value_b, query_b[2], query_b[3], up_b]
    )[None]
    biases = [bias_own] + [links.shift_z(bias_own, r) for r in range(1, n)]
    qkv_parts = gather_stage(links, qkv_own, 0)
    ffn_start, _ = lax.optimization_barrier((ffn_own, qkv_parts[-1][0]))
    ffn_parts = gather_stage(links, ffn_start, 1)
    qkv = [qkv_own] + [assemble(links, p, 0) for p in qkv_parts]
    ffn = [ffn_own] + [assemble(links, p, 1) for p in ffn_parts]

    words_own = take_rows(word_in, z * words, words)
    ents_own = take_rows(entity_in, z * ents, ents)
    spans = lax.dynamic_index_in_dim(entity_spans, z, 0, keepdims=False)
    position = lax.broadcasted_iota(jnp.int32, (ents, words), 1)
    inside = jnp.logical_and(position >= spans[:, 0:1], position < spans[:, 1:2])
    inside_low = jnp.where(inside, 1.0, 0.0).astype(BF16)
    share = 1.0 / (spans[:, 1:2] - spans[:, 0:1]).astype(F32)
    ent_rows = ents_own.astype(F32) + mm(inside_low, pos_table) * share
    rows_low = jnp.concatenate([words_own, ent_rows.astype(BF16)], 0)
    rows_t = rows_low.T

    saved = []
    for r in range(n):
        saved.append(attn_forward(rows_low, qkv[r], biases[r][:, : 6 * gw].astype(F32), words, heads))

    out_parts = [g[:gw] for g in ffn]
    up_parts = [g[gw : gw + width] for g in ffn]
    down_parts = [g[gw + width :] for g in ffn]
    attn = sum(mm(saved[r][2], out_parts[r]) for r in range(n))
    resid = jnp.concatenate([words_own.astype(F32), ent_rows], 0)
    attended = resid + attn + out_b.astype(F32)
    gain_one = norm1_gain.astype(F32)
    normed, scaled_one, inv_one = norm_forward(attended, gain_one, norm1_bias.astype(F32))
    normed_low = normed.astype(BF16)
    hidden = [mm(normed_low, up_parts[r]) + biases[r][:, 6 * gw :].astype(F32) for r in range(n)]
    activ = [exact_gelu(v).astype(BF16) for v in hidden]
    ffn_out = sum(mm(activ[r], down_parts[r]) for r in range(n))
    mixed = normed + ffn_out + down_b.astype(F32)
    gain_two = norm2_gain.astype(F32)
    output, scaled_two, inv_two = norm_forward(mixed, gain_two, norm2_bias.astype(F32))
    out_low = output.astype(BF16)
    mask_row = jnp.concatenate(
        [
            lax.dynamic_index_in_dim(word_mask, z, 0, keepdims=False),
            lax.dynamic_index_in_dim(entity_mask, z, 0, keepdims=False),
        ]
    ).astype(F32)[:, None]
    grad_output = mask_row * jnp.concatenate([cot_words, cot_entities], 0).astype(F32)
    grad_mixed, grad_gain_two, grad_bias_two = norm_backward(grad_output, scaled_two, inv_two, gain_two)
    grad_down_b = jnp.sum(grad_mixed, axis=0)
    mixed_low = grad_mixed.astype(BF16)
    grad_normed = grad_mixed
    grad_up_b = []
    up_grads = []
    down_grads = []
    for r in range(n):
        grad_activ = mm_nt(mixed_low, down_parts[r])
        _, gelu_back = jax.vjp(exact_gelu, hidden[r])
        pre_low = gelu_back(grad_activ)[0].astype(BF16)
        down_grads.append(mm_tn(activ[r], mixed_low).astype(BF16))
        up_grads.append(mm_tn(normed_low, pre_low).astype(BF16))
        grad_up_b.append(jnp.sum(pre_low.astype(F32), 0))
        grad_normed = grad_normed + mm_nt(pre_low, up_parts[r])
    grad_attended, grad_gain_one, grad_bias_one = norm_backward(grad_normed, scaled_one, inv_one, gain_one)
    grad_out_b = jnp.sum(grad_attended, axis=0)
    attended_low = grad_attended.astype(BF16)
    out_grads = [mm_tn(saved[r][2], attended_low).astype(BF16) for r in range(n)]
    ffn_grads = [jnp.concatenate([out_grads[r], up_grads[r], down_grads[r]], 0) for r in range(n)]
    ffn_sum = reduce_stage(links, ffn_grads, 1).astype(F32)

    acc = grad_attended
    qkv_grads = [None] * n
    qkv_bias = [None] * n
    for r in list(range(1, n)) + [0]:
        grad_ctx = mm_nt(attended_low, out_parts[r]).astype(BF16)
        proj_w, proj_e, _, log_total = saved[r]
        qkv_grads[r], acc, bias_sum = attn_backward(
            rows_t, proj_w, proj_e, log_total, grad_ctx, qkv[r], acc, heads
        )
        qkv_bias[r] = bias_sum[0]
    qkv_sum = reduce_stage(links, qkv_grads, 0).astype(F32)
    grad_ents = acc[words:]
    scaled_ents = grad_ents * share
    ents_high = scaled_ents.astype(BF16)
    ents_rest = (scaled_ents - ents_high.astype(F32)).astype(BF16)
    grad_pos = mm_tn(inside_low, ents_high) + mm_tn(inside_low, ents_rest)
    pos_sum = reduce_pos(links, grad_pos.astype(BF16)).astype(F32)

    group_vec = jnp.stack([jnp.concatenate([qkv_bias[r], grad_up_b[r]]) for r in range(n)])
    group_abs = jnp.take(group_vec, (z - jnp.arange(n)) % n, axis=0)
    flat = jnp.concatenate(
        [
            grad_gain_one,
            grad_bias_one,
            grad_out_b,
            grad_gain_two,
            grad_bias_two,
            grad_down_b,
            group_abs.reshape(-1),
        ]
    )
    vec = reduce_everywhere(links, flat.reshape(-1, width))
    own_vec = lax.dynamic_index_in_dim(
        vec[6:].reshape(n, 6 * gw + ff), z, 0, keepdims=False
    )
    grad_query_w = jnp.stack(
        [
            qkv_sum[:, :gw],
            qkv_sum[:, gw : 2 * gw],
            qkv_sum[:, 4 * gw : 5 * gw],
            qkv_sum[:, 5 * gw :],
        ]
    )
    grad_query_b = jnp.stack(
        [own_vec[:gw], own_vec[gw : 2 * gw], own_vec[4 * gw : 5 * gw], own_vec[5 * gw : 6 * gw]]
    )
    return (
        out_low[:words],
        out_low[words:],
        acc[:words],
        grad_ents,
        pos_sum,
        grad_query_w,
        grad_query_b,
        qkv_sum[:, 2 * gw : 3 * gw],
        qkv_sum[:, 3 * gw : 4 * gw],
        own_vec[3 * gw : 4 * gw],
        ffn_sum[:gw],
        vec[2],
        vec[0],
        vec[1],
        ffn_sum[gw : gw + width],
        own_vec[6 * gw :],
        ffn_sum[gw + width :],
        vec[5],
        vec[3],
        vec[4],
    )


def solution(mesh):
    rows = P(("dp", "tensor"), None)
    last = P(None, "tensor")
    placed = (
        P("dp", None),
        P("dp", None),
        P("dp", None, None),
        P("dp", None),
        P("dp", None),
        P(),
        P(None, None, "tensor"),
        last,
        last,
        last,
        P("tensor"),
        P("tensor", None),
        P(),
        P(),
        P(),
        last,
        P("tensor"),
        P("tensor", None),
        P(),
        P(),
        P(),
        rows,
        rows,
    )
    return jax.shard_map(
        shards,
        mesh=mesh,
        in_specs=placed,
        out_specs=(
            rows,
            rows,
            rows,
            rows,
            P(),
            P(None, None, "tensor"),
            last,
            last,
            last,
            P("tensor"),
            P("tensor", None),
            P(),
            P(),
            P(),
            last,
            P("tensor"),
            P("tensor", None),
            P(),
            P(),
            P(),
        ),
        check_vma=False,
    )
```

```python
from functools import partial

import jax
import jax.numpy as jnp
from jax import lax
from jax.experimental import pallas as pl
from jax.experimental.pallas import tpu as pltpu
from jax.sharding import PartitionSpec as P

HEAD_DIM = 64
SCALE = HEAD_DIM**-0.5
norm_epsilon = 1e-12
F32 = jnp.float32
BF16 = jnp.bfloat16
NT = (((1,), (1,)), ((), ()))
TN = (((0,), (0,)), ((), ()))
ERFC_STEP = 0.35
ERFC_POLY = (
    0.1396196249207051,
    0.13989555693599826,
    0.11957015144655456,
    0.10661400019997494,
    -0.025870835326937874,
    0.16337919550284652,
    -0.25954764983005574,
    0.14589250699009862,
    -0.029552569422939476,
)
ORDER = ((0, 0, 0), (0, 0, 1), (1, 0, 0), (0, 1, 1), (1, 0, 1), (1, 1, 1), (0, 1, 0), (1, 1, 0))
VMEM = pl.BlockSpec(memory_space=pltpu.VMEM)
SMEM = pl.BlockSpec(memory_space=pltpu.SMEM)
ANY = pl.BlockSpec(memory_space=pl.ANY)


def mm(a, b):
    return jnp.dot(a, b, preferred_element_type=F32)


def mm_nt(a, b):
    return lax.dot_general(a, b, NT, preferred_element_type=F32)


def mm_tn(a, b):
    return lax.dot_general(a, b, TN, preferred_element_type=F32)


def params(mib):
    return pltpu.CompilerParams(vmem_limit_bytes=mib << 20)


def cost(gflop, mbytes):
    return pl.CostEstimate(
        flops=int(gflop * 1e9), bytes_accessed=int(mbytes * 1e6), transcendentals=0
    )


def shape(dims, kind):
    return jax.ShapeDtypeStruct(dims, kind)


def start_kernel(info_ref, words_ref, ents_ref, spans_ref, table_ref, bias_ref, low_ref, turn_ref, resid_ref):
    words = words_ref.shape[0]
    low_words = words_ref[...]
    spans = spans_ref[0]
    begin = spans[:, 0:1]
    end = spans[:, 1:2]
    count = ents_ref.shape[0]
    position = lax.broadcasted_iota(jnp.int32, (count, words), 1)
    inside = jnp.where(jnp.logical_and(position >= begin, position < end), 1.0, 0.0).astype(BF16)
    share = 1.0 / (end - begin).astype(F32)
    rows = ents_ref[...].astype(F32) + mm(inside, table_ref[...]) * share
    low_ents = rows.astype(BF16)
    low_ref[:words] = low_words
    low_ref[words:] = low_ents
    turn_ref[:, :words] = low_words.T
    turn_ref[:, words:] = low_ents.T
    out_b = bias_ref[...].astype(F32)
    resid_ref[:words] = low_words.astype(F32) + out_b
    resid_ref[words:] = rows + out_b


def start_rows(info, word_in, entity_in, spans, table, out_b, words, ents):
    width = word_in.shape[1]
    total = words + ents
    whole = lambda i, info_ref: (0, 0)
    return pl.pallas_call(
        start_kernel,
        grid_spec=pltpu.PrefetchScalarGridSpec(
            num_scalar_prefetch=1,
            grid=(1,),
            in_specs=[
                pl.BlockSpec((words, width), lambda i, info_ref: (info_ref[0], 0)),
                pl.BlockSpec((ents, width), lambda i, info_ref: (info_ref[0], 0)),
                pl.BlockSpec((1, ents, 2), lambda i, info_ref: (info_ref[0], 0, 0)),
                pl.BlockSpec(table.shape, whole),
                pl.BlockSpec((1, width), whole),
            ],
            out_specs=[
                pl.BlockSpec((total, width), whole),
                pl.BlockSpec((width, total), whole),
                pl.BlockSpec((total, width), whole),
            ],
        ),
        out_shape=(shape((total, width), BF16), shape((width, total), BF16), shape((total, width), F32)),
        compiler_params=params(24),
        cost_estimate=cost(0.5, 8),
        name="start_rows",
    )(info, word_in, entity_in, spans, table, out_b)


def pack_kernel(info_ref, query_ref, key_ref, value_ref, out_ref, piece_ref):
    parts = (query_ref[0], query_ref[1], key_ref[...], value_ref[...], query_ref[2], query_ref[3], out_ref[...])
    piece_ref[...] = jnp.concatenate(parts, 1)


def pack_piece(info, query_w, key_w, value_w, out_turned):
    width, gw = key_w.shape
    unit = out_turned.shape[0]
    block = lambda i, info_ref: (info_ref[2], 0)
    return pl.pallas_call(
        pack_kernel,
        grid_spec=pltpu.PrefetchScalarGridSpec(
            num_scalar_prefetch=1,
            grid=(1,),
            in_specs=[
                pl.BlockSpec((4, unit, gw), lambda i, info_ref: (0, info_ref[2], 0)),
                pl.BlockSpec((unit, gw), block),
                pl.BlockSpec((unit, gw), block),
                pl.BlockSpec((unit, gw), lambda i, info_ref: (0, 0)),
            ],
            out_specs=pl.BlockSpec((unit, 7 * gw), lambda i, info_ref: (0, 0)),
        ),
        out_shape=shape((unit, 7 * gw), BF16),
        compiler_params=params(4),
        cost_estimate=cost(0.01, 1),
        name="pack_piece",
    )(info, query_w, key_w, value_w, out_turned)


def place_chunks(near_ref, far_ref, part, unit, targets, sem):
    stride = unit * len(targets)
    copies = []
    for core, source in enumerate((near_ref, far_ref)):
        for k, (first, second, half) in enumerate(ORDER):
            code = 4 * core + 2 * first + second
            place = (lax.bitwise_xor(part, jnp.int32(code)) * 2 + half) * unit
            for t, target in enumerate(targets):
                copies.append(
                    pltpu.make_async_copy(
                        source.at[pl.ds(k * stride + t * unit, unit)],
                        target.at[pl.ds(pl.multiple_of(place, 16), unit)],
                        sem,
                    )
                )
    for copy in copies:
        copy.start()
    return copies


def split_heads(words, gw, heads, pw_ref, pe_ref, qw_s, qe_s, k_s, v_s):
    half = 2 * gw
    for h in range(heads):
        o = h * HEAD_DIM
        e = o + HEAD_DIM
        qw_s[h, :words] = pw_ref[:, o:e]
        qw_s[h, words:] = pe_ref[:, half + o : half + e]
        qe_s[h, :words] = pw_ref[:, gw + o : gw + e]
        qe_s[h, words:] = pe_ref[:, half + gw + o : half + gw + e]
        k_s[h, :words] = pw_ref[:, half + o : half + e]
        k_s[h, words:] = pe_ref[:, o:e]
        v_s[h, :words] = pw_ref[:, half + gw + o : half + gw + e]
        v_s[h, words:] = pe_ref[:, gw + o : gw + e]


def attend_body(words, gw, heads, rows_ref, b_ref, acc_ref, w_ref, pw_ref, pe_ref, ctx_ref, lt_ref, out_ref, scratch):
    half = 2 * gw
    pw_ref[...] = (mm(rows_ref[:words], w_ref[:, : 4 * gw]) + b_ref[:, : 4 * gw].astype(F32)).astype(BF16)
    pe_ref[...] = (
        mm(rows_ref[words:], w_ref[:, half : 6 * gw]) + b_ref[:, half : 6 * gw].astype(F32)
    ).astype(BF16)
    split_heads(words, gw, heads, pw_ref, pe_ref, *scratch)
    qw_s, qe_s, k_s, v_s = scratch
    block = 128

    def step(qb, carry):
        rows = pl.ds(pl.multiple_of(qb * block, block), block)
        parts = []
        for h in range(heads):
            sw = mm_nt(qw_s[h, rows], k_s[h, :words])
            se = mm_nt(qe_s[h, rows], k_s[h, words:])
            top = jnp.maximum(jnp.max(sw, 1, keepdims=True), jnp.max(se, 1, keepdims=True))
            ew = jnp.exp((sw - top) * SCALE)
            ee = jnp.exp((se - top) * SCALE)
            total = jnp.sum(ew, 1, keepdims=True) + jnp.sum(ee, 1, keepdims=True)
            inv = 1.0 / total
            parts.append(
                mm((ew * inv).astype(BF16), v_s[h, :words]) + mm((ee * inv).astype(BF16), v_s[h, words:])
            )
            logt = top * SCALE + jnp.log(total)
            lt_ref[h : h + 1, rows] = jnp.broadcast_to(logt, (block, block)).T[0:1]
        ctx_ref[rows, :] = jnp.concatenate(parts, 1).astype(BF16)
        return carry

    lax.fori_loop(0, rows_ref.shape[0] // block, step, 0)
    out_ref[...] = acc_ref[...] + mm_nt(ctx_ref[...], w_ref[:, 6 * gw :])


def attend_own_kernel(
    words, gw, heads, rows_ref, b_ref, acc_ref, query_ref, key_ref, value_ref, ow_ref,
    w_ref, pw_ref, pe_ref, ctx_ref, lt_ref, out_ref, *scratch,
):
    parts = (query_ref[0], query_ref[1], key_ref[...], value_ref[...], query_ref[2], query_ref[3], ow_ref[...].T)
    for i, part in enumerate(parts):
        w_ref[:, i * gw : (i + 1) * gw] = part
    attend_body(words, gw, heads, rows_ref, b_ref, acc_ref, w_ref, pw_ref, pe_ref, ctx_ref, lt_ref, out_ref, scratch)


def attend_far_kernel(
    words, gw, heads, info_ref, rows_ref, b_ref, acc_ref, near_ref, far_ref,
    w_ref, pw_ref, pe_ref, ctx_ref, lt_ref, out_ref, *scratch,
):
    unit = w_ref.shape[0] // 16
    for copy in place_chunks(near_ref, far_ref, info_ref[2], unit, (w_ref,), scratch[-1]):
        copy.wait()
    attend_body(
        words, gw, heads, rows_ref, b_ref, acc_ref, w_ref, pw_ref, pe_ref, ctx_ref, lt_ref, out_ref, scratch[:-1]
    )


def attend_group(info, rows_low, bias, acc, weights, words, heads):
    total, width = rows_low.shape
    ents = total - words
    gw = heads * HEAD_DIM
    outs = (
        shape((width, 7 * gw), BF16),
        shape((words, 4 * gw), BF16),
        shape((ents, 4 * gw), BF16),
        shape((total, gw), BF16),
        shape((8, total), F32),
        shape((total, width), F32),
    )
    scratch = [pltpu.VMEM((heads, total, HEAD_DIM), BF16) for _ in range(4)]
    own = len(weights) == 4
    if own:
        body = partial(attend_own_kernel, words, gw, heads)
        args = (rows_low, bias, acc) + weights
        specs = [VMEM] * 7
        alias = {2: 5}
    else:
        body = partial(attend_far_kernel, words, gw, heads)
        args = (info, rows_low, bias, acc) + weights
        specs = [SMEM] + [VMEM] * 3 + [ANY] * 2
        alias = {3: 5}
        scratch.append(pltpu.SemaphoreType.DMA)
    return pl.pallas_call(
        body,
        in_specs=specs,
        out_specs=[VMEM] * 6,
        out_shape=outs,
        scratch_shapes=scratch,
        input_output_aliases=alias,
        compiler_params=params(28),
        cost_estimate=cost(8, 10),
        name="attend_own" if own else "attend_far",
    )(*args)


def gelu_pair(x):
    size = jnp.abs(x)
    t = 1.0 / (1.0 + ERFC_STEP * size)
    poly = jnp.full_like(x, ERFC_POLY[-1])
    for c in ERFC_POLY[-2::-1]:
        poly = poly * t + c
    bell = jnp.exp(x * x * -0.5)
    tail = poly * t * bell
    below = jnp.where(x >= 0, 1.0 - tail, tail)
    return x * below, below + x * (bell * 0.3989422804014327)


def norm_parts(values):
    centered = values - jnp.mean(values, 1, keepdims=True)
    inv = lax.rsqrt(jnp.mean(centered * centered, 1, keepdims=True) + norm_epsilon)
    return centered * inv, inv


def hidden_body(low, up_ref, down_ref, b_ref, at_ref, slope_ref):
    width = up_ref.shape[1]
    total = low.shape[0]
    block = 128
    upb = b_ref[...].astype(F32)
    act = []
    for i in range(total // block):
        lo = i * block
        pre = mm(low[lo : lo + block], up_ref[...]) + upb
        value, slope = gelu_pair(pre)
        slope_ref[lo : lo + block] = slope
        value = value.astype(BF16)
        at_ref[:, lo : lo + block] = value.T
        act.append(mm(value, down_ref[...]))
    return jnp.concatenate(act, 0)


def hidden_own_kernel(
    attended_ref, vec_ref, b_ref, up_ref, down_ref, low_ref, turn_ref, at_ref, slope_ref, out_ref
):
    scaled, _ = norm_parts(attended_ref[...])
    normed = scaled * vec_ref[0:1].astype(F32) + vec_ref[1:2].astype(F32)
    low = normed.astype(BF16)
    low_ref[...] = low
    turn_ref[...] = low.T
    out_ref[...] = normed + vec_ref[2:3].astype(F32)
    out_ref[...] += hidden_body(low_ref, up_ref, down_ref, b_ref, at_ref, slope_ref)


def hidden_own(attended, vec, bias, up, down):
    total, width = attended.shape
    ff = up.shape[1]
    return pl.pallas_call(
        hidden_own_kernel,
        in_specs=[VMEM] * 5,
        out_specs=[VMEM] * 5,
        out_shape=(
            shape((total, width), BF16),
            shape((width, total), BF16),
            shape((ff, total), BF16),
            shape((total, ff), F32),
            shape((total, width), F32),
        ),
        compiler_params=params(28),
        cost_estimate=cost(6, 12),
        name="hidden_own",
    )(attended, vec, bias, up, down)


def hidden_far_kernel(
    info_ref, low_ref, b_ref, acc_ref, near_ref, far_ref, up_ref, down_ref, at_ref, slope_ref, out_ref, sem
):
    unit = up_ref.shape[0] // 16
    for copy in place_chunks(near_ref, far_ref, info_ref[3], unit, (up_ref, down_ref), sem):
        copy.wait()
    out_ref[...] = acc_ref[...] + hidden_body(low_ref, up_ref, down_ref, b_ref, at_ref, slope_ref)


def hidden_far(info, low, bias, acc, near, far):
    total, width = low.shape
    return pl.pallas_call(
        hidden_far_kernel,
        in_specs=[SMEM] + [VMEM] * 3 + [ANY] * 2,
        out_specs=[VMEM] * 5,
        out_shape=(
            shape((width, width), BF16),
            shape((width, width), BF16),
            shape((width, total), BF16),
            shape((total, width), F32),
            shape((total, width), F32),
        ),
        scratch_shapes=[pltpu.SemaphoreType.DMA],
        input_output_aliases={3: 4},
        compiler_params=params(28),
        cost_estimate=cost(6, 12),
        name="hidden_far",
    )(info, low, bias, acc, near, far)


def norm_backward(grad_in, scaled, inv_std, gain_row):
    grad_gain = jnp.sum(grad_in * scaled, axis=0, keepdims=True)
    grad_shift = jnp.sum(grad_in, axis=0, keepdims=True)
    grad_scaled = grad_in * gain_row
    mean_first = jnp.mean(grad_scaled, axis=1, keepdims=True)
    mean_second = jnp.mean(grad_scaled * scaled, axis=1, keepdims=True)
    return inv_std * (grad_scaled - mean_first - scaled * mean_second), grad_gain, grad_shift


def loss_kernel(mixed_ref, vec_ref, mask_ref, cw_ref, ce_ref, ow_ref, oe_ref, low_ref, grad_ref, sums_ref):
    words = cw_ref.shape[0]
    scaled, inv = norm_parts(mixed_ref[...])
    gain = vec_ref[3:4].astype(F32)
    output = scaled * gain + vec_ref[4:5].astype(F32)
    ow_ref[...] = output[:words].astype(BF16)
    oe_ref[...] = output[words:].astype(BF16)
    cot = jnp.concatenate([cw_ref[...].astype(F32), ce_ref[...].astype(F32)], 0)
    grad, grad_gain, grad_shift = norm_backward(mask_ref[...] * cot, scaled, inv, gain)
    grad_ref[...] = grad
    low_ref[...] = grad.astype(BF16)
    sums_ref[0:1] = grad_gain
    sums_ref[1:2] = grad_shift
    sums_ref[2:3] = jnp.sum(grad, 0, keepdims=True)


def loss_back(mixed, vec, mask, cot_words, cot_ents):
    total, width = mixed.shape
    return pl.pallas_call(
        loss_kernel,
        in_specs=[VMEM] * 5,
        out_specs=[VMEM] * 5,
        out_shape=(
            shape(cot_words.shape, BF16),
            shape(cot_ents.shape, BF16),
            shape((total, width), BF16),
            shape((total, width), F32),
            shape((8, width), F32),
        ),
        compiler_params=params(28),
        cost_estimate=cost(3, 8),
        name="loss_back",
    )(mixed, vec, mask, cot_words, cot_ents)


def store_parts(value, ref, offset, stride, unit):
    for i in range(value.shape[0] // unit):
        ref[offset + i * stride : offset + i * stride + unit] = value[i * unit : (i + 1) * unit]


def hidden_back_kernel(
    info_ref, low_ref, at_ref, slope_ref, turn_ref, up_ref, down_ref, acc_ref, send_ref, keep_ref, out_ref, b_ref,
    full_s,
):
    unit = up_ref.shape[0] // 4
    half = full_s.shape[0] // 2
    low = low_ref[...]
    store_parts(mm(at_ref[...], low).astype(BF16), full_s, unit, 2 * unit, unit)
    pre = mm_nt(low, down_ref[...]) * slope_ref[...]
    pre_low = pre.astype(BF16)
    store_parts(mm(turn_ref[...], pre_low).astype(BF16), full_s, 0, 2 * unit, unit)
    core = info_ref[1]
    send_ref[...] = full_s[pl.ds(pl.multiple_of((1 - core) * half, 128), half)]
    keep_ref[...] = full_s[pl.ds(pl.multiple_of(core * half, 128), half)]
    out_ref[...] = acc_ref[...] + mm_nt(pre_low, up_ref[...])
    b_ref[...] = jnp.broadcast_to(jnp.sum(pre_low.astype(F32), 0, keepdims=True), b_ref.shape)


def hidden_back(info, mixed_low, act_t, slope, normed_t, up, down, acc):
    total, width = mixed_low.shape
    rows = up.shape[0]
    return pl.pallas_call(
        hidden_back_kernel,
        in_specs=[SMEM] + [VMEM] * 7,
        out_specs=[VMEM] * 4,
        out_shape=(
            shape((rows, width), BF16),
            shape((rows, width), BF16),
            shape((total, width), F32),
            shape((8, up.shape[1]), F32),
        ),
        scratch_shapes=[pltpu.VMEM((2 * rows, width), BF16)],
        input_output_aliases={7: 2},
        compiler_params=params(36),
        cost_estimate=cost(8, 14),
        name="hidden_back",
    )(info, mixed_low, act_t, slope, normed_t, up, down, acc)


def norm_back_kernel(attended_ref, grad_ref, vec_ref, out_ref, low_ref, turn_ref, sums_ref):
    scaled, inv = norm_parts(attended_ref[...])
    grad, grad_gain, grad_shift = norm_backward(grad_ref[...], scaled, inv, vec_ref[0:1].astype(F32))
    out_ref[...] = grad
    low = grad.astype(BF16)
    low_ref[...] = low
    turn_ref[...] = low.T
    sums_ref[0:1] = grad_gain
    sums_ref[1:2] = grad_shift
    sums_ref[2:3] = jnp.sum(grad, 0, keepdims=True)


def norm_back(attended, grad, vec):
    total, width = attended.shape
    return pl.pallas_call(
        norm_back_kernel,
        in_specs=[VMEM] * 3,
        out_specs=[VMEM] * 4,
        out_shape=(
            shape((total, width), F32),
            shape((total, width), BF16),
            shape((width, total), BF16),
            shape((8, width), F32),
        ),
        input_output_aliases={1: 0},
        compiler_params=params(24),
        cost_estimate=cost(3, 8),
        name="norm_back",
    )(attended, grad, vec)


def attend_back_kernel(
    words, gw, heads, info_ref, rt_ref, pw_ref, pe_ref, lt_ref, ctx_ref, low_ref, turn_ref, w_ref, acc_ref,
    send_ref, keep_ref, out_ref, db_ref,
    qw_s, qe_s, k_s, v_s, dc_s, p_s, ds_s, dpw_s, dpe_s, full_s,
):
    half = 2 * gw
    total = rt_ref.shape[1]
    split_heads(words, gw, heads, pw_ref, pe_ref, qw_s, qe_s, k_s, v_s)
    grad_ctx = mm(low_ref[...], w_ref[:, 6 * gw :]).astype(BF16)
    for h in range(heads):
        dc_s[h] = grad_ctx[:, h * HEAD_DIM : (h + 1) * HEAD_DIM]
    full_s[:, 6 * gw :] = mm(turn_ref[...], ctx_ref[...]).astype(BF16)
    block = 128
    for h in range(heads):
        o = h * HEAD_DIM
        e = o + HEAD_DIM

        def step(qb, carry):
            rows = pl.ds(pl.multiple_of(qb * block, block), block)
            logt = lt_ref[h : h + 1, rows]
            pw = jnp.exp(mm_nt(k_s[h, :words], qw_s[h, rows]) * SCALE - logt)
            pe = jnp.exp(mm_nt(k_s[h, words:], qe_s[h, rows]) * SCALE - logt)
            gw_ = mm_nt(v_s[h, :words], dc_s[h, rows])
            ge_ = mm_nt(v_s[h, words:], dc_s[h, rows])
            p_s[:words, rows] = pw.astype(BF16)
            p_s[words:, rows] = pe.astype(BF16)
            dot = jnp.sum(pw * gw_, 0, keepdims=True) + jnp.sum(pe * ge_, 0, keepdims=True)
            ds_s[:words, rows] = (pw * (gw_ - dot)).astype(BF16)
            ds_s[words:, rows] = (pe * (ge_ - dot)).astype(BF16)
            return carry

        lax.fori_loop(0, total // block, step, 0)
        dv = mm(p_s[...], dc_s[h]).astype(BF16)
        dkw = (mm(ds_s[:words], qw_s[h]) * SCALE).astype(BF16)
        dke = (mm(ds_s[words:], qe_s[h]) * SCALE).astype(BF16)
        dqw = (mm_tn(ds_s[:words], k_s[h, :words]) * SCALE).astype(BF16)
        dqe = (mm_tn(ds_s[words:], k_s[h, words:]) * SCALE).astype(BF16)
        dpw_s[:, o:e] = dqw[:words]
        dpw_s[:, gw + o : gw + e] = dqe[:words]
        dpw_s[:, half + o : half + e] = dkw
        dpw_s[:, half + gw + o : half + gw + e] = dv[:words]
        dpe_s[:, o:e] = dke
        dpe_s[:, gw + o : gw + e] = dv[words:]
        dpe_s[:, half + o : half + e] = dqw[words:]
        dpe_s[:, half + gw + o : half + gw + e] = dqe[words:]
    dpw = dpw_s[...]
    dpe = dpe_s[...]
    full_s[:, :half] = mm(rt_ref[:, :words], dpw[:, :half]).astype(BF16)
    full_s[:, half : 2 * half] = (
        mm(rt_ref[:, :words], dpw[:, half:]) + mm(rt_ref[:, words:], dpe[:, :half])
    ).astype(BF16)
    full_s[:, 2 * half : 3 * half] = mm(rt_ref[:, words:], dpe[:, half:]).astype(BF16)
    core = info_ref[1]
    rows = full_s.shape[0] // 2
    send_ref[...] = full_s[pl.ds(pl.multiple_of((1 - core) * rows, 128), rows)]
    keep_ref[...] = full_s[pl.ds(pl.multiple_of(core * rows, 128), rows)]
    out_ref[:words] = acc_ref[:words] + mm_nt(dpw, w_ref[:, : 2 * half])
    out_ref[words:] = acc_ref[words:] + mm_nt(dpe, w_ref[:, half : 3 * half])
    sw = jnp.sum(dpw.astype(F32), 0, keepdims=True)
    se = jnp.sum(dpe.astype(F32), 0, keepdims=True)
    db_ref[0:1, :half] = sw[:, :half]
    db_ref[0:1, half : 2 * half] = sw[:, half:] + se[:, :half]
    db_ref[0:1, 2 * half :] = se[:, half:]


def attend_back(info, rows_t, proj_w, proj_e, log_total, ctx, low, turned, weight, acc, heads):
    width, total = rows_t.shape
    words = proj_w.shape[0]
    ents = total - words
    gw = heads * HEAD_DIM
    return pl.pallas_call(
        partial(attend_back_kernel, words, gw, heads),
        in_specs=[SMEM] + [VMEM] * 9,
        out_specs=[VMEM] * 4,
        out_shape=(
            shape((width // 2, 7 * gw), BF16),
            shape((width // 2, 7 * gw), BF16),
            shape((total, width), F32),
            shape((8, 6 * gw), F32),
        ),
        scratch_shapes=[pltpu.VMEM((heads, total, HEAD_DIM), BF16) for _ in range(5)]
        + [
            pltpu.VMEM((total, total), BF16),
            pltpu.VMEM((total, total), BF16),
            pltpu.VMEM((words, 4 * gw), BF16),
            pltpu.VMEM((ents, 4 * gw), BF16),
            pltpu.VMEM((width, 7 * gw), BF16),
        ],
        input_output_aliases={9: 2},
        compiler_params=params(36),
        cost_estimate=cost(12, 14),
        name="attend_back",
    )(info, rows_t, proj_w, proj_e, log_total, ctx, low, turned, weight, acc)


def finish_kernel(info_ref, acc_ref, spans_ref, words_ref, ents_ref, pos_ref):
    words = words_ref.shape[0]
    count = ents_ref.shape[0]
    words_ref[...] = acc_ref[:words]
    grad = acc_ref[words:]
    ents_ref[...] = grad
    spans = spans_ref[0]
    begin = spans[:, 0:1]
    end = spans[:, 1:2]
    position = lax.broadcasted_iota(jnp.int32, (count, words), 1)
    inside = jnp.where(jnp.logical_and(position >= begin, position < end), 1.0, 0.0).astype(BF16)
    scaled = grad * (1.0 / (end - begin).astype(F32))
    high = scaled.astype(BF16)
    rest = (scaled - high.astype(F32)).astype(BF16)
    pos_ref[...] = (mm_tn(inside, high) + mm_tn(inside, rest)).astype(BF16)


def finish_rows(info, acc, spans, words):
    total, width = acc.shape
    ents = total - words
    whole = lambda i, info_ref: (0, 0)
    return pl.pallas_call(
        finish_kernel,
        grid_spec=pltpu.PrefetchScalarGridSpec(
            num_scalar_prefetch=1,
            grid=(1,),
            in_specs=[
                pl.BlockSpec((total, width), whole),
                pl.BlockSpec((1, ents, 2), lambda i, info_ref: (info_ref[0], 0, 0)),
            ],
            out_specs=[
                pl.BlockSpec((words, width), whole),
                pl.BlockSpec((ents, width), whole),
                pl.BlockSpec((words, width), whole),
            ],
        ),
        out_shape=(shape((words, width), F32), shape((ents, width), F32), shape((words, width), BF16)),
        compiler_params=params(16),
        cost_estimate=cost(0.5, 6),
        name="finish_rows",
    )(info, acc, spans)


def spread_query_kernel(info_ref, a_ref, b_ref, c_ref, d_ref, query_ref, key_ref, value_ref, out_ref):
    unit, width = a_ref.shape
    gw = width // 7
    part = info_ref[4]
    for i, ref in enumerate((a_ref, b_ref, c_ref, d_ref)):
        row = lax.bitwise_xor(part, jnp.int32(i))
        rows = pl.ds(pl.multiple_of(row * unit, 64), unit)
        value = ref[...].astype(F32)
        query_ref[0, rows] = value[:, :gw]
        query_ref[1, rows] = value[:, gw : 2 * gw]
        key_ref[rows] = value[:, 2 * gw : 3 * gw]
        value_ref[rows] = value[:, 3 * gw : 4 * gw]
        query_ref[2, rows] = value[:, 4 * gw : 5 * gw]
        query_ref[3, rows] = value[:, 5 * gw : 6 * gw]
        out_ref[rows] = value[:, 6 * gw :]


def spread_query(info, pieces):
    unit, width = pieces[0].shape
    gw = width // 7
    full = 4 * unit
    return pl.pallas_call(
        spread_query_kernel,
        in_specs=[SMEM] + [VMEM] * 4,
        out_specs=[VMEM] * 4,
        out_shape=(
            shape((4, full, gw), F32),
            shape((full, gw), F32),
            shape((full, gw), F32),
            shape((full, gw), F32),
        ),
        compiler_params=params(16),
        cost_estimate=cost(0.5, 7),
        name="spread_query",
    )(info, *pieces)


def spread_hidden_kernel(info_ref, a_ref, b_ref, c_ref, d_ref, up_ref, down_ref):
    unit = a_ref.shape[0] // 2
    part = info_ref[5]
    for i, ref in enumerate((a_ref, b_ref, c_ref, d_ref)):
        row = lax.bitwise_xor(part, jnp.int32(i))
        rows = pl.ds(pl.multiple_of(row * unit, 64), unit)
        up_ref[rows] = ref[:unit].astype(F32)
        down_ref[rows] = ref[unit:].astype(F32)


def spread_hidden(info, pieces):
    rows, width = pieces[0].shape
    out = shape((2 * rows, width), F32)
    return pl.pallas_call(
        spread_hidden_kernel,
        in_specs=[SMEM] + [VMEM] * 4,
        out_specs=[VMEM] * 2,
        out_shape=(out, out),
        compiler_params=params(16),
        cost_estimate=cost(0.5, 7),
        name="spread_hidden",
    )(info, *pieces)


class Links:
    def __init__(self):
        self.dp = lax.axis_size("dp")
        self.ring = lax.axis_size("tensor")
        dp_index = lax.axis_index("dp")
        self.z = lax.axis_index("tensor")
        self.core = dp_index % 2
        self.bits = (self.dp // 2).bit_length() - 1
        self.bit = [(dp_index // (2 << k)) % 2 for k in range(self.bits)]

    def shift_z(self, v, by):
        n = self.ring
        return lax.ppermute(v, "tensor", [(i, (i + by) % n) for i in range(n)])

    def swap_z(self, v, mask):
        return lax.ppermute(v, "tensor", [(i, i ^ mask) for i in range(self.ring)])

    def swap_core(self, v):
        return lax.ppermute(v, "dp", [(i, i ^ 1) for i in range(self.dp)])

    def swap_bit(self, v, k):
        return lax.ppermute(v, "dp", [(i, i ^ (2 << k)) for i in range(self.dp)])


def take_rows(v, start, size):
    return lax.dynamic_slice_in_dim(v, start, size, 0)


def after(value, *others):
    return lax.optimization_barrier((value,) + others)[0]


def gather_step(links, piece, first, second):
    unit = piece.shape[0] // 2
    low, high = piece[:unit], piece[unit:]
    low_first = links.swap_bit(low, first)
    high_second = links.swap_bit(high, second)
    high_both = links.swap_bit(jnp.concatenate([high, high_second], 0), first)
    low_both = links.swap_bit(jnp.concatenate([low, low_first], 0), second)
    near = jnp.concatenate([piece, low_first, high_second, high_both, low_both], 0)
    return near, links.swap_core(near)


def gather_stage(links, piece, first, second):
    groups = []
    for _ in range(links.ring - 1):
        piece = links.shift_z(piece, 1)
        groups.append(gather_step(links, piece, first, second))
    return groups, piece


def add_low(a, b):
    return (a.astype(F32) + b.astype(F32)).astype(BF16)


def join_rows(mine, other, flag):
    return jnp.where(flag == 0, jnp.concatenate([mine, other], 0), jnp.concatenate([other, mine], 0))


class Reduction:
    def __init__(self, links, k):
        self.links = links
        self.k = k
        self.acc = None

    def cores(self, send, keep):
        links, flag = self.links, self.links.bit[self.k]
        total = add_low(keep, links.swap_core(send))
        unit = total.shape[0] // 2
        return take_rows(total, flag * unit, unit), take_rows(total, (1 - flag) * unit, unit)

    def planes(self, mine, theirs):
        return add_low(mine, self.links.swap_bit(theirs, self.k))

    def ring(self, quarter):
        self.acc = quarter if self.acc is None else add_low(quarter, self.links.shift_z(self.acc, 1))
        return self.acc

    def rest(self):
        for j in range(self.links.bits):
            if j != self.k:
                self.acc = add_low(self.acc, self.links.swap_bit(self.acc, j))
        return self.acc

    def spread(self):
        links = self.links
        other = links.swap_bit(self.acc, self.k)
        return self.acc, other, links.swap_core(self.acc), links.swap_core(other)


def reduce_everywhere(links, v):
    v = v + links.swap_core(v)
    for j in range(links.bits):
        v = v + links.swap_bit(v, j)
    mask = 1
    while mask < links.ring:
        v = v + links.swap_z(v, mask)
        mask *= 2
    return v


def reduce_pos(links, v):
    flags = [(links.core, links.swap_core)] + [
        (links.bit[j], partial(links.swap_bit, k=j)) for j in range(min(2, links.bits))
    ]
    for flag, swap in flags:
        half = v.shape[0] // 2
        v = add_low(take_rows(v, flag * half, half), swap(take_rows(v, (1 - flag) * half, half)))
    for j in range(2, links.bits):
        v = add_low(v, links.swap_bit(v, j))
    mask = 1
    while mask < links.ring:
        v = add_low(v, links.swap_z(v, mask))
        mask *= 2
    for flag, swap in reversed(flags):
        v = join_rows(v, swap(v), flag)
    return v


def shards(
    word_in,
    entity_in,
    entity_spans,
    word_mask,
    entity_mask,
    pos_table,
    query_w,
    query_b,
    key_w,
    value_w,
    value_b,
    out_w,
    out_b,
    norm1_gain,
    norm1_bias,
    up_w,
    up_b,
    down_w,
    down_b,
    norm2_gain,
    norm2_bias,
    cot_words,
    cot_entities,
):
    links = Links()
    n = links.ring
    z = links.z
    words = cot_words.shape[0]
    ents = cot_entities.shape[0]
    width = word_in.shape[1]
    gw = key_w.shape[1]
    heads = gw // HEAD_DIM
    ff = up_w.shape[1]
    c, b0, b1 = links.core, links.bit[0], links.bit[1]
    part_q = 4 * c + 2 * b0 + b1
    part_f = 4 * c + 2 * b1 + b0
    info = jnp.stack([z, c, part_q, part_f, 2 * c + b0, 2 * c + b1, z, z]).astype(jnp.int32)
    unit = width // 8

    out_piece = lax.dynamic_slice_in_dim(out_w, part_q * unit, unit, 1).T
    piece_q = pack_piece(info, query_w, key_w, value_w, out_piece)
    query_groups, last_q = gather_stage(links, piece_q, 0, 1)
    small = unit // 2
    up_piece = take_rows(up_w, part_f * unit, unit)
    down_piece = take_rows(down_w, part_f * unit, unit)
    piece_f = jnp.concatenate([up_piece[:small], down_piece[:small], up_piece[small:], down_piece[small:]], 0)
    piece_f = after(piece_f, last_q)
    ffn_groups, _ = gather_stage(links, piece_f, 1, 0)
    bias_own = jnp.concatenate(
        [query_b[0], query_b[1], jnp.zeros((gw,), BF16), value_b, query_b[2], query_b[3], up_b]
    )[None]
    biases = [bias_own] + [links.shift_z(bias_own, r) for r in range(1, n)]

    rows_low, rows_t, acc = start_rows(
        info, word_in, entity_in, entity_spans, pos_table, out_b[None], words, ents
    )
    weights = []
    saved = []
    for r in range(n):
        source = (query_w, key_w, value_w, out_w) if r == 0 else query_groups[r - 1]
        w, pw, pe, ctx, lt, acc = attend_group(
            info, rows_low, biases[r][:, : 6 * gw], acc, source, words, heads
        )
        weights.append(w)
        saved.append((pw, pe, lt, ctx))
    attended = acc

    vec = jnp.stack([norm1_gain, norm1_bias, down_b, norm2_gain, norm2_bias] + [down_b] * 3)
    normed_low, normed_t, act, slope, acc = hidden_own(attended, vec, biases[0][:, 6 * gw :], up_w, down_w)
    ffn = [(up_w, down_w, act, slope)]
    for r in range(1, n):
        up, down, act, slope, acc = hidden_far(
            info, normed_low, biases[r][:, 6 * gw :], acc, *ffn_groups[r - 1]
        )
        ffn.append((up, down, act, slope))
    mask_row = jnp.concatenate(
        [
            lax.dynamic_index_in_dim(word_mask, z, 0, keepdims=False),
            lax.dynamic_index_in_dim(entity_mask, z, 0, keepdims=False),
        ]
    ).astype(F32)[:, None]
    out_words, out_ents, mixed_low, acc, sums_two = loss_back(acc, vec, mask_row, cot_words, cot_entities)

    order = list(range(1, n)) + [0]
    red_f = Reduction(links, 1)
    halves_f = []
    up_sums = [None] * n
    for i, r in enumerate(order):
        up, down, act, slope = ffn[r]
        if i >= 2:
            acc = after(acc, halves_f[i - 2][1])
        send, keep, acc, sums = hidden_back(info, mixed_low, act, slope, normed_t, up, down, acc)
        up_sums[r] = sums[0]
        halves_f.append(red_f.cores(send, keep))
    acc, attended_low, attended_t, sums_one = norm_back(attended, acc, vec)

    red_q = Reduction(links, 0)
    quarters_f = [red_f.planes(*halves_f[0])]
    red_f.ring(quarters_f[0])
    acc = after(acc, quarters_f[0], halves_f[-1][1])
    halves_q = []
    quarters_q = []
    query_sums = [None] * n
    for i, r in enumerate(order):
        if i == 1:
            quarters_f.append(red_f.planes(*halves_f[1]))
            acc = after(acc, red_f.ring(quarters_f[1]))
        elif i == 2:
            quarters_f.append(red_f.planes(*halves_f[2]))
            acc = after(acc, quarters_f[2], halves_q[0][1])
        elif i == 3:
            quarters_f.append(red_f.planes(*halves_f[3]))
            acc = after(acc, red_f.ring(quarters_f[2]), quarters_f[3], halves_q[1][1])
        pw, pe, lt, ctx = saved[r]
        send, keep, acc, sums = attend_back(
            info, rows_t, pw, pe, lt, ctx, attended_low, attended_t, weights[r], acc, heads
        )
        query_sums[r] = sums[0]
        halves_q.append(red_q.cores(send, keep))
    for i in range(n):
        quarters_q.append(red_q.planes(*halves_q[i]))
    grad_words, grad_ents, grad_pos = finish_rows(info, acc, entity_spans, words)
    red_f.ring(quarters_f[3])
    for i in range(n):
        red_q.ring(quarters_q[i])
    red_f.rest()
    red_q.rest()
    grad_up, grad_down = spread_hidden(info, red_f.spread())
    grad_query_w, grad_key_w, grad_value_w, grad_out_t = spread_query(info, red_q.spread())
    pos_sum = reduce_pos(links, grad_pos).astype(F32)

    group_vec = jnp.stack([jnp.concatenate([query_sums[r], up_sums[r]]) for r in range(n)])
    group_abs = jnp.take(group_vec, (z - jnp.arange(n)) % n, axis=0)
    flat = jnp.concatenate([sums_one[:3], sums_two[:3], group_abs.reshape(-1, width)], 0)
    vec_sum = reduce_everywhere(links, flat)
    own_vec = lax.dynamic_index_in_dim(vec_sum[6:].reshape(n, 6 * gw + ff), z, 0, keepdims=False)
    grad_query_b = jnp.stack(
        [own_vec[:gw], own_vec[gw : 2 * gw], own_vec[4 * gw : 5 * gw], own_vec[5 * gw : 6 * gw]]
    )
    return (
        out_words,
        out_ents,
        grad_words,
        grad_ents,
        pos_sum,
        grad_query_w,
        grad_query_b,
        grad_key_w,
        grad_value_w,
        own_vec[3 * gw : 4 * gw],
        grad_out_t.T,
        vec_sum[2],
        vec_sum[0],
        vec_sum[1],
        grad_up,
        own_vec[6 * gw :],
        grad_down,
        vec_sum[5],
        vec_sum[3],
        vec_sum[4],
    )


def solution(mesh):
    rows = P(("dp", "tensor"), None)
    last = P(None, "tensor")
    placed = (
        P("dp", None),
        P("dp", None),
        P("dp", None, None),
        P("dp", None),
        P("dp", None),
        P(),
        P(None, None, "tensor"),
        last,
        last,
        last,
        P("tensor"),
        P("tensor", None),
        P(),
        P(),
        P(),
        last,
        P("tensor"),
        P("tensor", None),
        P(),
        P(),
        P(),
        rows,
        rows,
    )
    return jax.shard_map(
        shards,
        mesh=mesh,
        in_specs=placed,
        out_specs=(
            rows,
            rows,
            rows,
            rows,
            P(),
            P(None, None, "tensor"),
            last,
            last,
            last,
            P("tensor"),
            P("tensor", None),
            P(),
            P(),
            P(),
            last,
            P("tensor"),
            P("tensor", None),
            P(),
            P(),
            P(),
        ),
        check_vma=False,
    )
```

```python
from functools import partial

import jax
import jax.numpy as jnp
from jax import lax
from jax.experimental import pallas as pl
from jax.experimental.pallas import tpu as pltpu
from jax.sharding import PartitionSpec as P

HEAD_DIM = 64
SCALE = HEAD_DIM**-0.5
norm_epsilon = 1e-12
F32 = jnp.float32
BF16 = jnp.bfloat16
NT = (((1,), (1,)), ((), ()))
TN = (((0,), (0,)), ((), ()))
ERFC_STEP = 0.35
ERFC_POLY = (
    0.1396196249207051,
    0.13989555693599826,
    0.11957015144655456,
    0.10661400019997494,
    -0.025870835326937874,
    0.16337919550284652,
    -0.25954764983005574,
    0.14589250699009862,
    -0.029552569422939476,
)
CODES = (0, 2, 1, 3, 4, 6, 5, 7)
TILE = 16
VMEM = pl.BlockSpec(memory_space=pltpu.VMEM)
SMEM = pl.BlockSpec(memory_space=pltpu.SMEM)
HBM = pl.BlockSpec(memory_space=pltpu.HBM)
DMA = pltpu.SemaphoreType.DMA


def mm(a, b):
    return jnp.dot(a, b, preferred_element_type=F32)


def mm_nt(a, b):
    return lax.dot_general(a, b, NT, preferred_element_type=F32)


def mm_tn(a, b):
    return lax.dot_general(a, b, TN, preferred_element_type=F32)


def params(mib):
    return pltpu.CompilerParams(vmem_limit_bytes=mib << 20)


def cost(gflop, mbytes):
    return pl.CostEstimate(
        flops=int(gflop * 1e9), bytes_accessed=int(mbytes * 1e6), transcendentals=0
    )


def shape(dims, kind):
    return jax.ShapeDtypeStruct(dims, kind)


def start(pairs, sem):
    copies = [pltpu.make_async_copy(source, target, sem) for source, target in pairs]
    for copy in copies:
        copy.start()
    return copies


def wait(copies):
    for copy in copies:
        copy.wait()


def rows_at(first, size):
    return pl.ds(pl.multiple_of(first, TILE), size)


def place(pieces, part, unit, targets):
    pairs = []
    for piece, code in zip(pieces, CODES):
        row = lax.bitwise_xor(part, jnp.int32(code)) * unit
        for t, target in enumerate(targets):
            pairs.append((piece.at[pl.ds(t * unit, unit)], target.at[rows_at(row, unit)]))
    return pairs


def blocks_out(full_s, part, unit, first, send_ref, near_ref, pass_ref):
    second = 3 - first
    order = (0, second, first, 3)
    pairs = []
    for i, code in enumerate(order):
        mine = lax.bitwise_xor(part, jnp.int32(code)) * unit
        other = lax.bitwise_xor(part, jnp.int32(code + 4)) * unit
        keep = near_ref if i < 2 else pass_ref
        pairs.append((full_s.at[rows_at(other, unit)], send_ref.at[pl.ds(i * unit, unit)]))
        pairs.append((full_s.at[rows_at(mine, unit)], keep.at[pl.ds((i % 2) * unit, unit)]))
    return pairs


def pack_kernel(
    gw, info_ref, qb_ref, vb_ref, ub_ref, query_ref, key_ref, value_ref, ow_ref, up_ref, down_ref,
    w_ref, piece_ref, ffn_ref, w_s, sem,
):
    parts = (query_ref.at[0], query_ref.at[1], key_ref, value_ref, query_ref.at[2], query_ref.at[3], ow_ref)
    reads = start([(v, w_s.at[pl.ds(i * gw, gw)]) for i, v in enumerate(parts)], sem.at[0])
    part = info_ref[2]
    unit = ffn_ref.shape[0] // 2
    ffn = start(
        [(v.at[rows_at(part * unit, unit)], ffn_ref.at[pl.ds(i * unit, unit)]) for i, v in enumerate((up_ref, down_ref))],
        sem.at[1],
    )
    qb = qb_ref[...].astype(F32)
    none = jnp.zeros((1, gw), F32)
    first = jnp.concatenate([qb[0:1], qb[1:2], none, vb_ref[...].astype(F32)], 1)
    second = jnp.concatenate([qb[2:3], qb[3:4], none, none], 1)
    spare = w_s.shape[0] - 7 * gw
    row = lax.broadcasted_iota(jnp.int32, (spare, 4 * gw), 0)
    rows = jnp.where(row == 0, first, jnp.where(row == 1, second, jnp.where(row == 2, ub_ref[...].astype(F32), 0.0)))
    w_s[7 * gw :] = rows.astype(BF16)
    wait(reads)
    size = piece_ref.shape[0]
    piece = start([(w_s.at[rows_at(part * size, size)], piece_ref)], sem.at[2])
    whole = start([(w_s, w_ref)], sem.at[3])
    wait(piece)
    wait(ffn)
    wait(whole)


def pack(info, query_b, value_b, up_b, query_t, key_t, value_t, out_w, up_w, down_w, rows):
    gw, width = key_t.shape
    unit = up_w.shape[0] // 8
    return pl.pallas_call(
        partial(pack_kernel, gw),
        in_specs=[SMEM] + [VMEM] * 3 + [HBM] * 6,
        out_specs=[HBM] * 3,
        out_shape=(shape((rows, width), BF16), shape((rows // 8, width), BF16), shape((2 * unit, width), BF16)),
        scratch_shapes=[pltpu.VMEM((rows, width), BF16), DMA((4,))],
        compiler_params=params(12),
        cost_estimate=cost(0.01, 8),
        name="pack",
    )(info, query_b, value_b, up_b, query_t, key_t, value_t, out_w, up_w, down_w)


def start_kernel(info_ref, words_ref, ents_ref, spans_ref, table_ref, bias_ref, low_ref, resid_ref, w_s, e_s, t_s, sem):
    words, count = w_s.shape[0], e_s.shape[0]
    z = info_ref[0]
    ents = start(
        [(ents_ref.at[rows_at(z * count, count)], e_s), (table_ref, t_s)],
        sem.at[0],
    )
    reads = start([(words_ref.at[rows_at(z * words, words)], w_s)], sem.at[1])
    spans = spans_ref[z]
    begin = spans[:, 0:1]
    end = spans[:, 1:2]
    position = lax.broadcasted_iota(jnp.int32, (count, words), 1)
    inside = jnp.where(jnp.logical_and(position >= begin, position < end), 1.0, 0.0).astype(BF16)
    share = 1.0 / (end - begin).astype(F32)
    out_b = bias_ref[...].astype(F32)
    wait(ents)
    rows = e_s[...].astype(F32) + mm(inside, t_s[...]) * share
    low_ref[words:] = rows.astype(BF16)
    resid_ref[words:] = rows + out_b
    wait(reads)
    low_ref[:words] = w_s[...]
    resid_ref[:words] = w_s[...].astype(F32) + out_b


def start_rows(info, word_in, entity_in, spans, table, out_b, words, ents):
    width = word_in.shape[1]
    total = words + ents
    return pl.pallas_call(
        start_kernel,
        in_specs=[SMEM, HBM, HBM, VMEM, HBM, VMEM],
        out_specs=[VMEM] * 2,
        out_shape=(shape((total, width), BF16), shape((total, width), F32)),
        scratch_shapes=[
            pltpu.VMEM((words, width), BF16),
            pltpu.VMEM((ents, width), BF16),
            pltpu.VMEM(table.shape, BF16),
            DMA((2,)),
        ],
        compiler_params=params(16),
        cost_estimate=cost(0.5, 6),
        name="start_rows",
    )(info, word_in, entity_in, spans, table, out_b)


def split_heads(words, gw, heads, pw_ref, pe_ref, qw_s, qe_s, k_s, v_s):
    half = 2 * gw
    for h in range(heads):
        o = h * HEAD_DIM
        e = o + HEAD_DIM
        qw_s[h, :words] = pw_ref[:, o:e]
        qw_s[h, words:] = pe_ref[:, half + o : half + e]
        qe_s[h, :words] = pw_ref[:, gw + o : gw + e]
        qe_s[h, words:] = pe_ref[:, half + gw + o : half + gw + e]
        k_s[h, :words] = pw_ref[:, half + o : half + e]
        k_s[h, words:] = pe_ref[:, o:e]
        v_s[h, :words] = pw_ref[:, half + gw + o : half + gw + e]
        v_s[h, words:] = pe_ref[:, gw + o : gw + e]


def attend_kernel(words, gw, heads, count, info_ref, rows_ref, acc_ref, *refs):
    pieces = refs[:count]
    pw_ref, pe_ref, ctx_ref, lt_ref, bias_ref, out_ref, w_s, pw_s, pe_s, ctx_s, qw_s, qe_s, k_s, v_s, sem = refs[count:]
    half = 2 * gw
    if count == 1:
        wait(start([(pieces[0], w_s)], sem.at[0]))
    else:
        wait(start(place(pieces, info_ref[2], w_s.shape[0] // 8, (w_s,)), sem.at[0]))
    rows_b = w_s[7 * gw : 7 * gw + TILE]
    bias_ref[...] = rows_b
    rows_b = rows_b.astype(F32)
    bias_e = jnp.concatenate([rows_b[0:1, half:], rows_b[1:2, :half]], 1)
    pw_s[...] = (mm_nt(rows_ref[:words], w_s[: 4 * gw]) + rows_b[0:1]).astype(BF16)
    pe_s[...] = (mm_nt(rows_ref[words:], w_s[half : 6 * gw]) + bias_e).astype(BF16)
    saves = start([(pw_s, pw_ref), (pe_s, pe_ref)], sem.at[1])
    split_heads(words, gw, heads, pw_s, pe_s, qw_s, qe_s, k_s, v_s)
    block = 128

    def step(qb, carry):
        rows = pl.ds(pl.multiple_of(qb * block, block), block)
        parts = []
        for h in range(heads):
            sw = mm_nt(qw_s[h, rows], k_s[h, :words])
            se = mm_nt(qe_s[h, rows], k_s[h, words:])
            top = jnp.maximum(jnp.max(sw, 1, keepdims=True), jnp.max(se, 1, keepdims=True))
            ew = jnp.exp((sw - top) * SCALE)
            ee = jnp.exp((se - top) * SCALE)
            total = jnp.sum(ew, 1, keepdims=True) + jnp.sum(ee, 1, keepdims=True)
            inv = 1.0 / total
            parts.append(
                mm((ew * inv).astype(BF16), v_s[h, :words]) + mm((ee * inv).astype(BF16), v_s[h, words:])
            )
            logt = top * SCALE + jnp.log(total)
            lt_ref[h : h + 1, rows] = jnp.broadcast_to(logt, (block, block)).T[0:1]
        ctx_s[rows, :] = jnp.concatenate(parts, 1).astype(BF16)
        return carry

    lax.fori_loop(0, rows_ref.shape[0] // block, step, 0)
    last = start([(ctx_s, ctx_ref)], sem.at[2])
    out_ref[...] = acc_ref[...] + mm(ctx_s[...], w_s[6 * gw : 7 * gw])
    wait(saves)
    wait(last)


def attend(info, rows_low, acc, pieces, words, heads, rows):
    total, width = rows_low.shape
    ents = total - words
    gw = heads * HEAD_DIM
    count = len(pieces)
    return pl.pallas_call(
        partial(attend_kernel, words, gw, heads, count),
        in_specs=[SMEM] + [VMEM] * 2 + [HBM] * count,
        out_specs=[HBM] * 3 + [VMEM] * 3,
        out_shape=(
            shape((words, 4 * gw), BF16),
            shape((ents, 4 * gw), BF16),
            shape((total, gw), BF16),
            shape((8, total), F32),
            shape((TILE, width), BF16),
            shape((total, width), F32),
        ),
        scratch_shapes=[
            pltpu.VMEM((rows, width), BF16),
            pltpu.VMEM((words, 4 * gw), BF16),
            pltpu.VMEM((ents, 4 * gw), BF16),
            pltpu.VMEM((total, gw), BF16),
        ]
        + [pltpu.VMEM((heads, total, HEAD_DIM), BF16) for _ in range(4)]
        + [DMA((3,))],
        input_output_aliases={2: 5},
        compiler_params=params(24),
        cost_estimate=cost(8, 6),
        name="attend_own" if count == 1 else "attend_far",
    )(info, rows_low, acc, *pieces)


def gelu_pair(x):
    size = jnp.abs(x)
    t = 1.0 / (1.0 + ERFC_STEP * size)
    poly = jnp.full_like(x, ERFC_POLY[-1])
    for c in ERFC_POLY[-2::-1]:
        poly = poly * t + c
    bell = jnp.exp(x * x * -0.5)
    tail = poly * t * bell
    below = jnp.where(x >= 0, 1.0 - tail, tail)
    return x * below, below + x * (bell * 0.3989422804014327)


def norm_parts(values):
    centered = values - jnp.mean(values, 1, keepdims=True)
    inv = lax.rsqrt(jnp.mean(centered * centered, 1, keepdims=True) + norm_epsilon)
    return centered * inv, inv


def hidden_kernel(n, info_ref, attended_ref, vec_ref, wm_ref, em_ref, cw_ref, ce_ref, *refs):
    bias_refs, refs = refs[:n], refs[n:]
    up_own, down_own = refs[:2]
    pieces, refs = refs[2 : 2 + 8 * (n - 1)], refs[2 + 8 * (n - 1) :]
    low_ref, turn_ref, at_ref, slope_ref, ow_ref, oe_ref, mixed_ref, grad_ref, sums_ref, up_s, down_s, acc_s, b_s, sem = refs
    total, width = attended_ref.shape
    unit = width // 8
    part = info_ref[2]
    reads = [start([(up_own, up_s.at[0]), (down_own, down_s.at[0])], sem.at[0])]
    for r in range(1, n):
        reads.append(start(place(pieces[8 * (r - 1) : 8 * r], part, unit, (up_s.at[r], down_s.at[r])), sem.at[r]))
    for r in range(n):
        b_s[r] = bias_refs[r][2:3].astype(F32)
    scaled, _ = norm_parts(attended_ref[...])
    normed = scaled * vec_ref[0:1].astype(F32) + vec_ref[1:2].astype(F32)
    low = normed.astype(BF16)
    low_ref[...] = low
    turn_ref[...] = low.T
    acc_s[...] = normed + vec_ref[2:3].astype(F32)
    block = 128

    def group(r):
        for lo in range(0, total, block):
            pre = mm(low_ref[lo : lo + block], up_s[r]) + b_s[r]
            value, slope = gelu_pair(pre)
            slope_ref[r, lo : lo + block] = slope
            value = value.astype(BF16)
            at_ref[r, :, lo : lo + block] = value.T
            acc_s[lo : lo + block] += mm(value, down_s[r])

    for r in range(n):
        wait(reads[r])
        group(r)

    words = cw_ref.shape[0]
    z = info_ref[0]
    scaled, inv = norm_parts(acc_s[...])
    gain = vec_ref[3:4].astype(F32)
    output = scaled * gain + vec_ref[4:5].astype(F32)
    ow_ref[...] = output[:words].astype(BF16)
    oe_ref[...] = output[words:].astype(BF16)

    def column(ref, size):
        return jnp.broadcast_to(ref[pl.ds(z, 1), :].astype(F32), (128, size)).T[:, 0:1]

    cot = jnp.concatenate(
        [
            column(wm_ref, words) * cw_ref[...].astype(F32),
            column(em_ref, total - words) * ce_ref[...].astype(F32),
        ],
        0,
    )
    grad, grad_gain, grad_shift = norm_backward(cot, scaled, inv, gain)
    grad_ref[...] = grad
    mixed_ref[...] = grad.astype(BF16)
    sums_ref[0:1] = grad_gain
    sums_ref[1:2] = grad_shift
    sums_ref[2:3] = jnp.sum(grad, 0, keepdims=True)
    sums_ref[3:] = jnp.zeros((5, width), F32)


def hidden(info, attended, vec, word_mask, entity_mask, cot_words, cot_ents, biases, own, groups):
    total, width = attended.shape
    n = len(biases)
    pieces = [v for g in groups for v in g]
    return pl.pallas_call(
        partial(hidden_kernel, n),
        in_specs=[SMEM] + [VMEM] * (6 + n) + [HBM] * (2 + len(pieces)),
        out_specs=[VMEM] * 9,
        out_shape=(
            shape((total, width), BF16),
            shape((width, total), BF16),
            shape((n, width, total), BF16),
            shape((n, total, width), F32),
            shape(cot_words.shape, BF16),
            shape(cot_ents.shape, BF16),
            shape((total, width), BF16),
            shape((total, width), F32),
            shape((8, width), F32),
        ),
        scratch_shapes=[
            pltpu.VMEM((n, width, width), BF16),
            pltpu.VMEM((n, width, width), BF16),
            pltpu.VMEM((total, width), F32),
            pltpu.VMEM((n, 1, width), F32),
            DMA((n,)),
        ],
        compiler_params=params(48),
        cost_estimate=cost(22, 20),
        name="hidden",
    )(info, attended, vec, word_mask, entity_mask, cot_words, cot_ents, *biases, *own, *pieces)


def norm_backward(grad_in, scaled, inv_std, gain_row):
    grad_gain = jnp.sum(grad_in * scaled, axis=0, keepdims=True)
    grad_shift = jnp.sum(grad_in, axis=0, keepdims=True)
    grad_scaled = grad_in * gain_row
    mean_first = jnp.mean(grad_scaled, axis=1, keepdims=True)
    mean_second = jnp.mean(grad_scaled * scaled, axis=1, keepdims=True)
    return inv_std * (grad_scaled - mean_first - scaled * mean_second), grad_gain, grad_shift


def hidden_back_kernel(r, first, count, info_ref, low_ref, at_ref, slope_ref, turn_ref, acc_ref, *refs):
    pieces = refs[:count]
    send_ref, near_ref, pass_ref, out_ref, b_ref, up_s, down_s, full_s, sem = refs[count:]
    unit = up_s.shape[0] // 8
    part = info_ref[2]
    if count == 2:
        reads = start([(pieces[0], up_s), (pieces[1], down_s)], sem.at[0])
    else:
        reads = start(place(pieces, part, unit, (up_s, down_s)), sem.at[0])
    low = low_ref[...]
    grad_down = mm(at_ref[r], low).astype(BF16)
    for i in range(8):
        full_s[(2 * i + 1) * unit : (2 * i + 2) * unit] = grad_down[i * unit : (i + 1) * unit]
    wait(reads)
    pre_low = (mm_nt(low, down_s[...]) * slope_ref[r]).astype(BF16)
    grad_up = mm(turn_ref[...], pre_low).astype(BF16)
    for i in range(8):
        full_s[2 * i * unit : (2 * i + 1) * unit] = grad_up[i * unit : (i + 1) * unit]
    writes = start(blocks_out(full_s, part, 2 * unit, first, send_ref, near_ref, pass_ref), sem.at[1])
    out_ref[...] = acc_ref[...] + mm_nt(pre_low, up_s[...])
    b_ref[...] = jnp.broadcast_to(jnp.sum(pre_low.astype(F32), 0, keepdims=True), b_ref.shape)
    wait(writes)


def hidden_back(info, r, first, mixed_low, act_t, slope, normed_t, acc, pieces):
    total, width = mixed_low.shape
    count = len(pieces)
    return pl.pallas_call(
        partial(hidden_back_kernel, r, first, count),
        in_specs=[SMEM] + [VMEM] * 5 + [HBM] * count,
        out_specs=[HBM] * 3 + [VMEM] * 2,
        out_shape=(
            shape((width, width), BF16),
            shape((width // 2, width), BF16),
            shape((width // 2, width), BF16),
            shape((total, width), F32),
            shape((8, width), F32),
        ),
        scratch_shapes=[
            pltpu.VMEM((width, width), BF16),
            pltpu.VMEM((width, width), BF16),
            pltpu.VMEM((2 * width, width), BF16),
            DMA((2,)),
        ],
        input_output_aliases={5: 3},
        compiler_params=params(32),
        cost_estimate=cost(7, 8),
        name="hidden_back",
    )(info, mixed_low, act_t, slope, normed_t, acc, *pieces)


def norm_back_kernel(attended_ref, grad_ref, vec_ref, sums_ref, out_ref, low_ref, all_ref):
    scaled, inv = norm_parts(attended_ref[...])
    grad, grad_gain, grad_shift = norm_backward(grad_ref[...], scaled, inv, vec_ref[0:1].astype(F32))
    out_ref[...] = grad
    low_ref[...] = grad.astype(BF16)
    all_ref[...] = sums_ref[...]
    all_ref[3:4] = grad_gain
    all_ref[4:5] = grad_shift
    all_ref[5:6] = jnp.sum(grad, 0, keepdims=True)


def norm_back(attended, grad, vec, sums):
    total, width = attended.shape
    return pl.pallas_call(
        norm_back_kernel,
        in_specs=[VMEM] * 4,
        out_specs=[VMEM] * 3,
        out_shape=(shape((total, width), F32), shape((total, width), BF16), shape((8, width), F32)),
        input_output_aliases={1: 0},
        compiler_params=params(24),
        cost_estimate=cost(2, 6),
        name="norm_back",
    )(attended, grad, vec, sums)


def attend_back_kernel(words, gw, heads, first, count, info_ref, rows_ref, lt_ref, low_ref, up_ref, acc_ref, *refs):
    pw_ref, pe_ref, ctx_ref = refs[:3]
    pieces = refs[3 : 3 + count]
    (
        send_ref, near_ref, pass_ref, out_ref,
        w_s, pw_s, pe_s, ctx_s, qw_s, qe_s, k_s, v_s, dc_s, p_s, ds_s, dpw_s, dpe_s, full_s, sem,
    ) = refs[3 + count :]
    half = 2 * gw
    total = rows_ref.shape[0]
    part = info_ref[2]
    size = w_s.shape[0] // 8
    saved = start([(pw_ref, pw_s), (pe_ref, pe_s)], sem.at[0])
    if count == 1:
        reads = start([(pieces[0], w_s)], sem.at[1])
    else:
        reads = start(place(pieces, part, size, (w_s,)), sem.at[1])
    last = start([(ctx_ref, ctx_s)], sem.at[2])
    wait(saved)
    split_heads(words, gw, heads, pw_s, pe_s, qw_s, qe_s, k_s, v_s)
    wait(reads)
    grad_ctx = mm_nt(low_ref[...], w_s[6 * gw : 7 * gw]).astype(BF16)
    for h in range(heads):
        dc_s[h] = grad_ctx[:, h * HEAD_DIM : (h + 1) * HEAD_DIM]
    wait(last)
    full_s[6 * gw : 7 * gw] = mm_tn(ctx_s[...], low_ref[...]).astype(BF16)
    block = 128
    for h in range(heads):
        o = h * HEAD_DIM
        e = o + HEAD_DIM

        def step(qb, carry):
            rows = pl.ds(pl.multiple_of(qb * block, block), block)
            logt = lt_ref[h : h + 1, rows]
            pw = jnp.exp(mm_nt(k_s[h, :words], qw_s[h, rows]) * SCALE - logt)
            pe = jnp.exp(mm_nt(k_s[h, words:], qe_s[h, rows]) * SCALE - logt)
            gw_ = mm_nt(v_s[h, :words], dc_s[h, rows])
            ge_ = mm_nt(v_s[h, words:], dc_s[h, rows])
            p_s[:words, rows] = pw.astype(BF16)
            p_s[words:, rows] = pe.astype(BF16)
            dot = jnp.sum(pw * gw_, 0, keepdims=True) + jnp.sum(pe * ge_, 0, keepdims=True)
            ds_s[:words, rows] = (pw * (gw_ - dot)).astype(BF16)
            ds_s[words:, rows] = (pe * (ge_ - dot)).astype(BF16)
            return carry

        lax.fori_loop(0, total // block, step, 0)
        dv = mm(p_s[...], dc_s[h]).astype(BF16)
        dkw = (mm(ds_s[:words], qw_s[h]) * SCALE).astype(BF16)
        dke = (mm(ds_s[words:], qe_s[h]) * SCALE).astype(BF16)
        dqw = (mm_tn(ds_s[:words], k_s[h, :words]) * SCALE).astype(BF16)
        dqe = (mm_tn(ds_s[words:], k_s[h, words:]) * SCALE).astype(BF16)
        dpw_s[:, o:e] = dqw[:words]
        dpw_s[:, gw + o : gw + e] = dqe[:words]
        dpw_s[:, half + o : half + e] = dkw
        dpw_s[:, half + gw + o : half + gw + e] = dv[:words]
        dpe_s[:, o:e] = dke
        dpe_s[:, gw + o : gw + e] = dv[words:]
        dpe_s[:, half + o : half + e] = dqw[words:]
        dpe_s[:, half + gw + o : half + gw + e] = dqe[words:]
    dpw = dpw_s[...]
    dpe = dpe_s[...]
    rows_w = rows_ref[:words]
    rows_e = rows_ref[words:]
    full_s[:half] = mm_tn(dpw[:, :half], rows_w).astype(BF16)
    full_s[half : 2 * half] = (mm_tn(dpw[:, half:], rows_w) + mm_tn(dpe[:, :half], rows_e)).astype(BF16)
    full_s[2 * half : 3 * half] = mm_tn(dpe[:, half:], rows_e).astype(BF16)
    sw = jnp.sum(dpw.astype(F32), 0, keepdims=True)
    se = jnp.sum(dpe.astype(F32), 0, keepdims=True)
    sum_a = jnp.concatenate([sw[:, :half], sw[:, half:] + se[:, :half]], 1)
    sum_b = jnp.concatenate([se[:, half:], jnp.zeros((1, half), F32)], 1)
    spare = w_s.shape[0] - 7 * gw
    row = lax.broadcasted_iota(jnp.int32, (spare, 2 * half), 0)
    sums = jnp.where(row == 0, sum_a, jnp.where(row == 1, sum_b, jnp.where(row == 2, up_ref[0:1], 0.0)))
    full_s[7 * gw :] = sums.astype(BF16)
    writes = start(blocks_out(full_s, part, size, first, send_ref, near_ref, pass_ref), sem.at[3])
    out_ref[:words] = acc_ref[:words] + mm(dpw, w_s[: 2 * half])
    out_ref[words:] = acc_ref[words:] + mm(dpe, w_s[half : 3 * half])
    wait(writes)


def attend_back(info, first, rows_low, saved, low, up_sums, acc, pieces, words, heads, rows):
    total, width = rows_low.shape
    pw, pe, ctx, lt = saved
    ents = total - words
    gw = heads * HEAD_DIM
    count = len(pieces)
    return pl.pallas_call(
        partial(attend_back_kernel, words, gw, heads, first, count),
        in_specs=[SMEM] + [VMEM] * 5 + [HBM] * (3 + count),
        out_specs=[HBM] * 3 + [VMEM],
        out_shape=(
            shape((rows // 2, width), BF16),
            shape((rows // 4, width), BF16),
            shape((rows // 4, width), BF16),
            shape((total, width), F32),
        ),
        scratch_shapes=[
            pltpu.VMEM((rows, width), BF16),
            pltpu.VMEM((words, 4 * gw), BF16),
            pltpu.VMEM((ents, 4 * gw), BF16),
            pltpu.VMEM((total, gw), BF16),
        ]
        + [pltpu.VMEM((heads, total, HEAD_DIM), BF16) for _ in range(5)]
        + [
            pltpu.VMEM((total, total), BF16),
            pltpu.VMEM((total, total), BF16),
            pltpu.VMEM((words, 4 * gw), BF16),
            pltpu.VMEM((ents, 4 * gw), BF16),
            pltpu.VMEM((rows, width), BF16),
            DMA((4,)),
        ],
        input_output_aliases={5: 3},
        compiler_params=params(32),
        cost_estimate=cost(11, 8),
        name="attend_back",
    )(info, rows_low, lt, low, up_sums, acc, pw, pe, ctx, *pieces)


def finish_kernel(info_ref, acc_ref, spans_ref, words_ref, ents_ref, send_ref, near_ref, pass_ref, pos_s, sem):
    words = words_ref.shape[0]
    count = ents_ref.shape[0]
    grad = acc_ref[words:]
    ents_ref[...] = grad
    spans = spans_ref[info_ref[0]]
    begin = spans[:, 0:1]
    end = spans[:, 1:2]
    position = lax.broadcasted_iota(jnp.int32, (count, words), 1)
    inside = jnp.where(jnp.logical_and(position >= begin, position < end), 1.0, 0.0).astype(BF16)
    scaled = grad * (1.0 / (end - begin).astype(F32))
    high = scaled.astype(BF16)
    rest = (scaled - high.astype(F32)).astype(BF16)
    pos_s[...] = (mm_tn(inside, high) + mm_tn(inside, rest)).astype(BF16)
    writes = start(blocks_out(pos_s, info_ref[2], words // 8, 2, send_ref, near_ref, pass_ref), sem)
    words_ref[...] = acc_ref[:words]
    wait(writes)


def finish_rows(info, acc, spans, words):
    total, width = acc.shape
    ents = total - words
    return pl.pallas_call(
        finish_kernel,
        in_specs=[SMEM] + [VMEM] * 2,
        out_specs=[VMEM] * 2 + [HBM] * 3,
        out_shape=(
            shape((words, width), F32),
            shape((ents, width), F32),
            shape((words // 2, width), BF16),
            shape((words // 4, width), BF16),
            shape((words // 4, width), BF16),
        ),
        scratch_shapes=[pltpu.VMEM((words, width), BF16), DMA],
        compiler_params=params(16),
        cost_estimate=cost(0.5, 6),
        name="finish_rows",
    )(info, acc, spans)


def spread_query_kernel(info_ref, *refs):
    pieces = refs[:8]
    query_ref, key_ref, value_ref, out_ref, qb_ref, vb_ref, ub_ref, s, sem = refs[8:]
    wait(start(place(pieces, info_ref[2], s.shape[0] // 8, (s,)), sem))
    gw = key_ref.shape[0]
    for i, k in ((0, 0), (1, 1), (2, 4), (3, 5)):
        query_ref[i] = s[k * gw : (k + 1) * gw].astype(F32)
    key_ref[...] = s[2 * gw : 3 * gw].astype(F32)
    value_ref[...] = s[3 * gw : 4 * gw].astype(F32)
    out_ref[...] = s[6 * gw : 7 * gw].astype(F32)
    rows = s[7 * gw : 7 * gw + TILE].astype(F32)
    qb_ref[0:1] = rows[0:1, :gw]
    qb_ref[1:2] = rows[0:1, gw : 2 * gw]
    qb_ref[2:3] = rows[1:2, :gw]
    qb_ref[3:4] = rows[1:2, gw : 2 * gw]
    vb_ref[...] = rows[0:1, 3 * gw :]
    ub_ref[...] = rows[2:3]


def spread_query(info, pieces, gw):
    unit, width = pieces[0].shape
    flat = shape((gw, width), F32)
    return pl.pallas_call(
        spread_query_kernel,
        in_specs=[SMEM] + [HBM] * 8,
        out_specs=[VMEM] * 7,
        out_shape=(
            shape((4, gw, width), F32), flat, flat, flat,
            shape((4, gw), F32), shape((1, gw), F32), shape((1, width), F32),
        ),
        scratch_shapes=[pltpu.VMEM((8 * unit, width), BF16), DMA],
        compiler_params=params(16),
        cost_estimate=cost(0.5, 7),
        name="spread_query",
    )(info, *pieces)


def spread_hidden_kernel(info_ref, *refs):
    pieces = refs[:8]
    up_ref, down_ref, up_s, down_s, sem = refs[8:]
    wait(start(place(pieces, info_ref[2], up_ref.shape[0] // 8, (up_s, down_s)), sem))
    up_ref[...] = up_s[...].astype(F32)
    down_ref[...] = down_s[...].astype(F32)


def spread_hidden(info, pieces):
    rows, width = pieces[0].shape
    out = shape((4 * rows, width), F32)
    return pl.pallas_call(
        spread_hidden_kernel,
        in_specs=[SMEM] + [HBM] * 8,
        out_specs=[VMEM] * 2,
        out_shape=(out, out),
        scratch_shapes=[pltpu.VMEM((4 * rows, width), BF16)] * 2 + [DMA],
        compiler_params=params(16),
        cost_estimate=cost(0.5, 7),
        name="spread_hidden",
    )(info, *pieces)


def spread_pos_kernel(info_ref, *refs):
    pieces = refs[:8]
    pos_ref, s, sem = refs[8:]
    wait(start(place(pieces, info_ref[2], s.shape[0] // 8, (s,)), sem))
    pos_ref[...] = s[...].astype(F32)


def spread_pos(info, pieces):
    rows, width = pieces[0].shape
    return pl.pallas_call(
        spread_pos_kernel,
        in_specs=[SMEM] + [HBM] * 8,
        out_specs=VMEM,
        out_shape=shape((8 * rows, width), F32),
        scratch_shapes=[pltpu.VMEM((8 * rows, width), BF16), DMA],
        compiler_params=params(8),
        cost_estimate=cost(0.5, 3),
        name="spread_pos",
    )(info, *pieces)


class Links:
    def __init__(self):
        self.dp = lax.axis_size("dp")
        self.ring = lax.axis_size("tensor")
        dp_index = lax.axis_index("dp")
        self.z = lax.axis_index("tensor")
        self.core = dp_index % 2
        self.bits = (self.dp // 2).bit_length() - 1
        self.bit = [(dp_index // (2 << k)) % 2 for k in range(self.bits)]

    def shift_z(self, v, by):
        n = self.ring
        return lax.ppermute(v, "tensor", [(i, (i + by) % n) for i in range(n)])

    def swap_z(self, v, mask):
        return lax.ppermute(v, "tensor", [(i, i ^ mask) for i in range(self.ring)])

    def swap(self, v, code):
        return lax.ppermute(v, "dp", [(i, i ^ code) for i in range(self.dp)])

    def swap_core(self, v):
        return self.swap(v, 1)

    def swap_code(self, v, code):
        return self.swap(v, ((code >> 1) & 1) * 2 + (code & 1) * 4)


def after(value, *others):
    return lax.optimization_barrier((value,) + others)[0]


def gather_group(links, piece, first):
    second = 3 - first
    over = {first: links.swap_code(piece, first), second: links.swap_code(piece, second)}
    near = (piece, over[2], over[1], links.swap_code(over[first], second))
    return near + tuple(links.swap_core(v) for v in near)


def add_low(*parts):
    total = parts[0].astype(F32)
    for part in parts[1:]:
        total = total + part.astype(F32)
    return total.astype(BF16)


class Blocks:
    def __init__(self, links, first, send, near, far):
        self.links, self.first, self.near, self.far = links, first, near, far
        self.unit = near.shape[0] // 2
        self.got = links.swap_core(send)

    def one(self):
        u = self.unit
        value = add_low(self.far, self.got[2 * u :])
        self.a = self.links.swap_code(value, self.first)
        return value

    def two(self):
        u = self.unit
        value = add_low(self.near[u:], self.got[u : 2 * u], self.a[u:])
        self.parts = (self.a[:u], self.links.swap_code(value, 3 - self.first))
        return value

    def direct(self):
        u = self.unit
        first, second = self.first, 3 - self.first
        a = add_low(self.far[:u], self.got[2 * u : 3 * u])
        b = add_low(self.far[u:], self.got[3 * u :])
        c = add_low(self.near[u:], self.got[u : 2 * u])
        links = self.links
        self.parts = (links.swap_code(b, 3), links.swap_code(a, first), links.swap_code(c, second))

    def rest(self, *more):
        u = self.unit
        value = add_low(self.near[:u], self.got[:u], *self.parts, *more)
        for j in range(2, self.links.bits):
            value = add_low(value, self.links.swap(value, 2 << j))
        return value


def spread_all(links, value):
    near = (value, links.swap_code(value, 2), links.swap_code(value, 1), links.swap_code(value, 3))
    return near + tuple(links.swap_core(v) for v in near)


def reduce_everywhere(links, v):
    v = v + links.swap_core(v)
    for j in range(links.bits):
        v = v + links.swap(v, 2 << j)
    mask = 1
    while mask < links.ring:
        v = v + links.swap_z(v, mask)
        mask *= 2
    return v


def shards(
    word_in,
    entity_in,
    entity_spans,
    word_mask,
    entity_mask,
    pos_table,
    query_w,
    query_b,
    key_w,
    value_w,
    value_b,
    out_w,
    out_b,
    norm1_gain,
    norm1_bias,
    up_w,
    up_b,
    down_w,
    down_b,
    norm2_gain,
    norm2_bias,
    cot_words,
    cot_entities,
):
    links = Links()
    n = links.ring
    z = links.z
    words = cot_words.shape[0]
    ents = cot_entities.shape[0]
    width = word_in.shape[1]
    gw = key_w.shape[1]
    heads = gw // HEAD_DIM
    rows = -(-(7 * gw + 3) // (8 * TILE)) * 8 * TILE
    part = 4 * links.core + 2 * links.bit[0] + links.bit[1]
    info = jnp.stack([z, links.core, part, part]).astype(jnp.int32)

    own_w, piece_q, piece_f = pack(
        info, query_b, value_b[None], up_b[None], jnp.swapaxes(query_w, 1, 2), key_w.T, value_w.T, out_w, up_w, down_w, rows
    )
    shifted = []
    for _ in range(n - 1):
        piece_q = links.shift_z(piece_q, 1)
        shifted.append(piece_q)
    piece_f = after(piece_f, shifted[0])
    query_groups = [(own_w,)] + [gather_group(links, v, 1 + i % 2) for i, v in enumerate(shifted)]
    ffn_groups = []
    for i in range(n - 1):
        piece_f = links.shift_z(piece_f, 1)
        ffn_groups.append(gather_group(links, piece_f, 2 - i % 2))

    rows_low, acc = start_rows(info, word_in, entity_in, entity_spans, pos_table, out_b[None], words, ents)
    saved = []
    biases = []
    for r in range(n):
        pw, pe, ctx, lt, bias, acc = attend(info, rows_low, acc, query_groups[r], words, heads, rows)
        saved.append((pw, pe, ctx, lt))
        biases.append(bias)
    attended = acc

    vec = jnp.stack([norm1_gain, norm1_bias, down_b, norm2_gain, norm2_bias] + [down_b] * 3)
    _, normed_t, act_t, slope, out_words, out_ents, mixed_low, acc, sums = hidden(
        info, attended, vec, word_mask, entity_mask, cot_words, cot_entities, biases, (up_w, down_w), ffn_groups
    )

    order = list(range(1, n)) + [0]
    ffn_pieces = [(up_w, down_w)] + ffn_groups
    blocks_f = []
    up_sums = [None] * n
    for i, r in enumerate(order):
        first = 2 - i % 2
        send, near, far, acc, up_sums[r] = hidden_back(
            info, r, first, mixed_low, act_t, slope, normed_t, acc, ffn_pieces[r]
        )
        blocks_f.append(Blocks(links, first, send, near, far))
        if i:
            acc = after(acc, blocks_f[i - 1].one())
    acc, attended_low, sums = norm_back(attended, acc, vec, sums)

    last = n - 1
    blocks_q = []
    sent_f = []
    sent_q = []
    acc = after(acc, blocks_f[last].one(), *[b.two() for b in blocks_f[: n // 2]])
    pieces_f = None
    for i, r in enumerate(order):
        first = 1 + i % 2
        send, near, far, acc = attend_back(
            info, first, rows_low, saved[r], attended_low, up_sums[r], acc, query_groups[r], words, heads, rows
        )
        blocks_q.append(Blocks(links, first, send, near, far))
        if i == 0:
            ready = [b.two() for b in blocks_f[n // 2 :]]
            done = [b.rest() for b in blocks_f[: n // 2]]
            sent_f += [links.shift_z(v, -order[j]) for j, v in enumerate(done)]
            acc = after(acc, *ready, *done)
        elif i == 1:
            done = [b.rest() for b in blocks_f[n // 2 : last]]
            sent_f += [links.shift_z(v, -order[n // 2 + j]) for j, v in enumerate(done)]
            total_sums = reduce_everywhere(links, sums)
            acc = after(acc, *done, blocks_q[0].one())
        elif i == 2:
            value = blocks_f[last].rest(*sent_f)
            pieces_f = spread_all(links, value)
            acc = after(acc, value, blocks_q[0].two(), blocks_q[1].one(), total_sums)
    grad_words, grad_ents, *pos_blocks = finish_rows(info, acc, entity_spans, words)
    blocks_p = Blocks(links, 2, *pos_blocks)

    done = blocks_q[0].rest()
    sent_q.append(links.shift_z(done, -order[0]))
    blocks_q[1].two()
    blocks_q[2].direct()
    blocks_q[3].direct()
    blocks_p.direct()
    for j in range(1, last):
        sent_q.append(links.shift_z(blocks_q[j].rest(), -order[j]))
    grad_up, grad_down = spread_hidden(info, pieces_f)
    value = blocks_q[last].rest(*sent_q)
    pieces_q = spread_all(links, value)
    pos = blocks_p.rest()
    mask = 1
    while mask < n:
        pos = add_low(pos, links.swap_z(pos, mask))
        mask *= 2
    pieces_p = spread_all(links, pos)
    grad_query_t, grad_key_t, grad_value_t, grad_out, grad_query_b, grad_value_b, grad_up_b = spread_query(
        info, pieces_q, gw
    )
    pos_sum = spread_pos(info, pieces_p)
    return (
        out_words,
        out_ents,
        grad_words,
        grad_ents,
        pos_sum,
        jnp.swapaxes(grad_query_t, 1, 2),
        grad_query_b,
        grad_key_t.T,
        grad_value_t.T,
        grad_value_b[0],
        grad_out,
        total_sums[5],
        total_sums[3],
        total_sums[4],
        grad_up,
        grad_up_b[0],
        grad_down,
        total_sums[2],
        total_sums[0],
        total_sums[1],
    )


def solution(mesh):
    rows = P(("dp", "tensor"), None)
    last = P(None, "tensor")
    placed = (
        P("dp", None),
        P("dp", None),
        P("dp", None, None),
        P("dp", None),
        P("dp", None),
        P(),
        P(None, None, "tensor"),
        last,
        last,
        last,
        P("tensor"),
        P("tensor", None),
        P(),
        P(),
        P(),
        last,
        P("tensor"),
        P("tensor", None),
        P(),
        P(),
        P(),
        rows,
        rows,
    )
    return jax.shard_map(
        shards,
        mesh=mesh,
        in_specs=placed,
        out_specs=(
            rows,
            rows,
            rows,
            rows,
            P(),
            P(None, None, "tensor"),
            last,
            last,
            last,
            P("tensor"),
            P("tensor", None),
            P(),
            P(),
            P(),
            last,
            P("tensor"),
            P("tensor", None),
            P(),
            P(),
            P(),
        ),
        check_vma=False,
    )
```

```python
from functools import partial

import jax
import jax.numpy as jnp
from jax import lax
from jax.experimental import pallas as pl
from jax.experimental.pallas import tpu as pltpu
from jax.sharding import PartitionSpec as P

HEAD_DIM = 64
SCALE = HEAD_DIM**-0.5
norm_epsilon = 1e-12
F32 = jnp.float32
BF16 = jnp.bfloat16
NT = (((1,), (1,)), ((), ()))
TN = (((0,), (0,)), ((), ()))
ERFC_STEP = 0.35
ERFC_POLY = (
    0.1396196249207051,
    0.13989555693599826,
    0.11957015144655456,
    0.10661400019997494,
    -0.025870835326937874,
    0.16337919550284652,
    -0.25954764983005574,
    0.14589250699009862,
    -0.029552569422939476,
)
TILE = 16
VMEM = pl.BlockSpec(memory_space=pltpu.VMEM)
SMEM = pl.BlockSpec(memory_space=pltpu.SMEM)
HBM = pl.BlockSpec(memory_space=pltpu.HBM)
DMA = pltpu.SemaphoreType.DMA


def mm(a, b):
    return jnp.dot(a, b, preferred_element_type=F32)


def mm_nt(a, b):
    return lax.dot_general(a, b, NT, preferred_element_type=F32)


def mm_tn(a, b):
    return lax.dot_general(a, b, TN, preferred_element_type=F32)


def params(mib):
    return pltpu.CompilerParams(vmem_limit_bytes=mib << 20)


def cost(gflop, mbytes):
    return pl.CostEstimate(
        flops=int(gflop * 1e9), bytes_accessed=int(mbytes * 1e6), transcendentals=0
    )


def shape(dims, kind):
    return jax.ShapeDtypeStruct(dims, kind)


def start(pairs, sem):
    copies = [pltpu.make_async_copy(source, target, sem) for source, target in pairs]
    for copy in copies:
        copy.start()
    return copies


def wait(copies):
    for copy in copies:
        copy.wait()


def rows_at(first, size):
    return pl.ds(pl.multiple_of(first, TILE), size)


def place(pieces, info_ref, unit, targets, skip=0):
    part, first = info_ref[2], info_ref[3]
    second = 3 - first
    pairs = []
    for piece, code in zip(pieces, (0, first, second, 3, 4, 4 + second, 4 + first, 7)):
        row = lax.bitwise_xor(part, jnp.int32(code)) * unit
        for t, target in enumerate(targets):
            pairs.append((piece.at[pl.ds(skip + t * unit, unit)], target.at[rows_at(row, unit)]))
    return pairs


def blocks_out(sources, info_ref, send_ref, near_ref, pass_ref):
    part, first = info_ref[2], info_ref[3]
    second = 3 - first
    keep = (0, second, first, 3)
    send = (4, 4 + first, 4 + second, 7)
    total = sum(unit for _, unit in sources)
    pairs = []
    for i in range(4):
        done = 0
        for source, unit in sources:
            other = lax.bitwise_xor(part, jnp.int32(send[i])) * unit
            mine = lax.bitwise_xor(part, jnp.int32(keep[i])) * unit
            to = near_ref if i < 2 else pass_ref
            pairs.append((source.at[rows_at(other, unit)], send_ref.at[pl.ds(i * total + done, unit)]))
            pairs.append((source.at[rows_at(mine, unit)], to.at[pl.ds((i % 2) * total + done, unit)]))
            done += unit
    return pairs


def pack_kernel(
    gw, info_ref, qb_ref, vb_ref, ub_ref, query_ref, key_ref, value_ref, ow_ref, up_ref, down_ref,
    w_ref, piece_ref, ffn_ref, w_s, sem,
):
    parts = (query_ref.at[0], query_ref.at[1], key_ref, value_ref, query_ref.at[2], query_ref.at[3], ow_ref)
    reads = start([(v, w_s.at[pl.ds(i * gw, gw)]) for i, v in enumerate(parts)], sem.at[0])
    part = info_ref[2]
    unit = ffn_ref.shape[0] // 2
    ffn = start(
        [(v.at[rows_at(part * unit, unit)], ffn_ref.at[pl.ds(i * unit, unit)]) for i, v in enumerate((up_ref, down_ref))],
        sem.at[1],
    )
    qb = qb_ref[...].astype(F32)
    none = jnp.zeros((1, gw), F32)
    first = jnp.concatenate([qb[0:1], qb[1:2], none, vb_ref[...].astype(F32)], 1)
    second = jnp.concatenate([qb[2:3], qb[3:4], none, none], 1)
    spare = w_s.shape[0] - 7 * gw
    row = lax.broadcasted_iota(jnp.int32, (spare, 4 * gw), 0)
    rows = jnp.where(row == 0, first, jnp.where(row == 1, second, jnp.where(row == 2, ub_ref[...].astype(F32), 0.0)))
    w_s[7 * gw :] = rows.astype(BF16)
    wait(reads)
    size = piece_ref.shape[0]
    piece = start([(w_s.at[rows_at(part * size, size)], piece_ref)], sem.at[2])
    whole = start([(w_s, w_ref)], sem.at[3])
    wait(piece)
    wait(ffn)
    wait(whole)


def pack(info, query_b, value_b, up_b, query_t, key_t, value_t, out_w, up_w, down_w, rows):
    gw, width = key_t.shape
    unit = up_w.shape[0] // 8
    return pl.pallas_call(
        partial(pack_kernel, gw),
        in_specs=[SMEM] + [VMEM] * 3 + [HBM] * 6,
        out_specs=[HBM] * 3,
        out_shape=(shape((rows, width), BF16), shape((rows // 8, width), BF16), shape((2 * unit, width), BF16)),
        scratch_shapes=[pltpu.VMEM((rows, width), BF16), DMA((4,))],
        compiler_params=params(12),
        cost_estimate=cost(0.01, 8),
        name="pack",
    )(info, query_b, value_b, up_b, query_t, key_t, value_t, out_w, up_w, down_w)


def start_kernel(info_ref, words_ref, ents_ref, spans_ref, table_ref, bias_ref, low_ref, resid_ref, w_s, e_s, t_s, sem):
    words, count = w_s.shape[0], e_s.shape[0]
    z = info_ref[0]
    ents = start(
        [(ents_ref.at[rows_at(z * count, count)], e_s), (table_ref, t_s)],
        sem.at[0],
    )
    reads = start([(words_ref.at[rows_at(z * words, words)], w_s)], sem.at[1])
    spans = spans_ref[z]
    begin = spans[:, 0:1]
    end = spans[:, 1:2]
    position = lax.broadcasted_iota(jnp.int32, (count, words), 1)
    inside = jnp.where(jnp.logical_and(position >= begin, position < end), 1.0, 0.0).astype(BF16)
    share = 1.0 / (end - begin).astype(F32)
    out_b = bias_ref[...].astype(F32)
    wait(ents)
    rows = e_s[...].astype(F32) + mm(inside, t_s[...]) * share
    low_ref[words:] = rows.astype(BF16)
    resid_ref[words:] = rows + out_b
    wait(reads)
    low_ref[:words] = w_s[...]
    resid_ref[:words] = w_s[...].astype(F32) + out_b


def start_rows(info, word_in, entity_in, spans, table, out_b, words, ents):
    width = word_in.shape[1]
    total = words + ents
    return pl.pallas_call(
        start_kernel,
        in_specs=[SMEM, HBM, HBM, VMEM, HBM, VMEM],
        out_specs=[VMEM] * 2,
        out_shape=(shape((total, width), BF16), shape((total, width), F32)),
        scratch_shapes=[
            pltpu.VMEM((words, width), BF16),
            pltpu.VMEM((ents, width), BF16),
            pltpu.VMEM(table.shape, BF16),
            DMA((2,)),
        ],
        compiler_params=params(16),
        cost_estimate=cost(0.5, 6),
        name="start_rows",
    )(info, word_in, entity_in, spans, table, out_b)


def split_heads(words, gw, heads, pw_ref, pe_ref, qw_s, qe_s, k_s, v_s):
    half = 2 * gw
    for h in range(heads):
        o = h * HEAD_DIM
        e = o + HEAD_DIM
        qw_s[h, :words] = pw_ref[:, o:e]
        qw_s[h, words:] = pe_ref[:, half + o : half + e]
        qe_s[h, :words] = pw_ref[:, gw + o : gw + e]
        qe_s[h, words:] = pe_ref[:, half + gw + o : half + gw + e]
        k_s[h, :words] = pw_ref[:, half + o : half + e]
        k_s[h, words:] = pe_ref[:, o:e]
        v_s[h, :words] = pw_ref[:, half + gw + o : half + gw + e]
        v_s[h, words:] = pe_ref[:, gw + o : gw + e]


def attend_kernel(words, gw, heads, count, info_ref, rows_ref, acc_ref, *refs):
    pieces = refs[:count]
    pw_ref, pe_ref, ctx_ref, lt_ref, bias_ref, out_ref, w_s, pw_s, pe_s, ctx_s, qw_s, qe_s, k_s, v_s, sem = refs[count:]
    half = 2 * gw
    if count == 1:
        wait(start([(pieces[0], w_s)], sem.at[0]))
    else:
        wait(start(place(pieces, info_ref, w_s.shape[0] // 8, (w_s,)), sem.at[0]))
    rows_b = w_s[7 * gw : 7 * gw + TILE]
    bias_ref[...] = rows_b
    rows_b = rows_b.astype(F32)
    bias_e = jnp.concatenate([rows_b[0:1, half:], rows_b[1:2, :half]], 1)
    pw_s[...] = (mm_nt(rows_ref[:words], w_s[: 4 * gw]) + rows_b[0:1]).astype(BF16)
    pe_s[...] = (mm_nt(rows_ref[words:], w_s[half : 6 * gw]) + bias_e).astype(BF16)
    saves = start([(pw_s, pw_ref), (pe_s, pe_ref)], sem.at[1])
    split_heads(words, gw, heads, pw_s, pe_s, qw_s, qe_s, k_s, v_s)
    block = 128

    def step(qb, carry):
        rows = pl.ds(pl.multiple_of(qb * block, block), block)
        parts = []
        for h in range(heads):
            sw = mm_nt(qw_s[h, rows], k_s[h, :words])
            se = mm_nt(qe_s[h, rows], k_s[h, words:])
            top = jnp.maximum(jnp.max(sw, 1, keepdims=True), jnp.max(se, 1, keepdims=True))
            ew = jnp.exp((sw - top) * SCALE)
            ee = jnp.exp((se - top) * SCALE)
            total = jnp.sum(ew, 1, keepdims=True) + jnp.sum(ee, 1, keepdims=True)
            inv = 1.0 / total
            parts.append(
                mm((ew * inv).astype(BF16), v_s[h, :words]) + mm((ee * inv).astype(BF16), v_s[h, words:])
            )
            logt = top * SCALE + jnp.log(total)
            lt_ref[h : h + 1, rows] = jnp.broadcast_to(logt, (block, block)).T[0:1]
        ctx_s[rows, :] = jnp.concatenate(parts, 1).astype(BF16)
        return carry

    lax.fori_loop(0, rows_ref.shape[0] // block, step, 0)
    last = start([(ctx_s, ctx_ref)], sem.at[2])
    out_ref[...] = acc_ref[...] + mm(ctx_s[...], w_s[6 * gw : 7 * gw])
    wait(saves)
    wait(last)


def attend(info, rows_low, acc, pieces, words, heads, rows):
    total, width = rows_low.shape
    ents = total - words
    gw = heads * HEAD_DIM
    count = len(pieces)
    return pl.pallas_call(
        partial(attend_kernel, words, gw, heads, count),
        in_specs=[SMEM] + [VMEM] * 2 + [HBM] * count,
        out_specs=[HBM] * 3 + [VMEM] * 3,
        out_shape=(
            shape((words, 4 * gw), BF16),
            shape((ents, 4 * gw), BF16),
            shape((total, gw), BF16),
            shape((8, total), F32),
            shape((TILE, width), BF16),
            shape((total, width), F32),
        ),
        scratch_shapes=[
            pltpu.VMEM((rows, width), BF16),
            pltpu.VMEM((words, 4 * gw), BF16),
            pltpu.VMEM((ents, 4 * gw), BF16),
            pltpu.VMEM((total, gw), BF16),
        ]
        + [pltpu.VMEM((heads, total, HEAD_DIM), BF16) for _ in range(4)]
        + [DMA((3,))],
        input_output_aliases={2: 5},
        compiler_params=params(24),
        cost_estimate=cost(8, 6),
        name="attend_own" if count == 1 else "attend_far",
    )(info, rows_low, acc, *pieces)


def gelu_pair(x):
    size = jnp.abs(x)
    t = 1.0 / (1.0 + ERFC_STEP * size)
    poly = jnp.full_like(x, ERFC_POLY[-1])
    for c in ERFC_POLY[-2::-1]:
        poly = poly * t + c
    bell = jnp.exp(x * x * -0.5)
    tail = poly * t * bell
    below = jnp.where(x >= 0, 1.0 - tail, tail)
    return x * below, below + x * (bell * 0.3989422804014327)


def norm_parts(values):
    centered = values - jnp.mean(values, 1, keepdims=True)
    inv = lax.rsqrt(jnp.mean(centered * centered, 1, keepdims=True) + norm_epsilon)
    return centered * inv, inv


def hidden_kernel(n, info_ref, attended_ref, vec_ref, wm_ref, em_ref, cw_ref, ce_ref, *refs):
    bias_refs, refs = refs[:n], refs[n:]
    up_own, down_own = refs[:2]
    pieces, refs = refs[2:10], refs[10:]
    turn_ref, at_ref, slope_ref, up_s, down_s, ow_ref, oe_ref, mixed_ref, grad_ref, sums_ref, low_ref, acc_s, b_s, sem = refs
    total, width = attended_ref.shape
    unit = width // 8
    reads = [start([(up_own, up_s.at[0]), (down_own, down_s.at[0])], sem.at[0])]
    for r in range(1, n):
        reads.append(start(place(pieces, info_ref, unit, (up_s.at[r], down_s.at[r]), 2 * unit * (r - 1)), sem.at[r]))
    for r in range(n):
        b_s[r] = bias_refs[r][2:3].astype(F32)
    scaled, _ = norm_parts(attended_ref[...])
    normed = scaled * vec_ref[0:1].astype(F32) + vec_ref[1:2].astype(F32)
    low = normed.astype(BF16)
    low_ref[...] = low
    turn_ref[...] = low.T
    acc_s[...] = normed + vec_ref[2:3].astype(F32)
    block = 128

    def group(r):
        for lo in range(0, total, block):
            pre = mm(low_ref[lo : lo + block], up_s[r]) + b_s[r]
            value, slope = gelu_pair(pre)
            slope_ref[r, lo : lo + block] = slope
            value = value.astype(BF16)
            at_ref[r, :, lo : lo + block] = value.T
            acc_s[lo : lo + block] += mm(value, down_s[r])

    for r in range(n):
        wait(reads[r])
        group(r)

    words = cw_ref.shape[0]
    z = info_ref[0]
    scaled, inv = norm_parts(acc_s[...])
    gain = vec_ref[3:4].astype(F32)
    output = scaled * gain + vec_ref[4:5].astype(F32)
    ow_ref[...] = output[:words].astype(BF16)
    oe_ref[...] = output[words:].astype(BF16)

    def column(ref, size):
        return jnp.broadcast_to(ref[pl.ds(z, 1), :].astype(F32), (128, size)).T[:, 0:1]

    cot = jnp.concatenate(
        [
            column(wm_ref, words) * cw_ref[...].astype(F32),
            column(em_ref, total - words) * ce_ref[...].astype(F32),
        ],
        0,
    )
    grad, grad_gain, grad_shift = norm_backward(cot, scaled, inv, gain)
    grad_ref[...] = grad
    mixed_ref[...] = grad.astype(BF16)
    sums_ref[0:1] = grad_gain
    sums_ref[1:2] = grad_shift
    sums_ref[2:3] = jnp.sum(grad, 0, keepdims=True)
    sums_ref[3:] = jnp.zeros((5, width), F32)


def hidden(info, attended, vec, word_mask, entity_mask, cot_words, cot_ents, biases, own, pieces):
    total, width = attended.shape
    n = len(biases)
    return pl.pallas_call(
        partial(hidden_kernel, n),
        in_specs=[SMEM] + [VMEM] * (6 + n) + [HBM] * (2 + len(pieces)),
        out_specs=[VMEM] * 10,
        out_shape=(
            shape((width, total), BF16),
            shape((n, width, total), BF16),
            shape((n, total, width), F32),
            shape((n, width, width), BF16),
            shape((n, width, width), BF16),
            shape(cot_words.shape, BF16),
            shape(cot_ents.shape, BF16),
            shape((total, width), BF16),
            shape((total, width), F32),
            shape((8, width), F32),
        ),
        scratch_shapes=[
            pltpu.VMEM((total, width), BF16),
            pltpu.VMEM((total, width), F32),
            pltpu.VMEM((n, 1, width), F32),
            DMA((n,)),
        ],
        compiler_params=params(48),
        cost_estimate=cost(22, 20),
        name="hidden",
    )(info, attended, vec, word_mask, entity_mask, cot_words, cot_ents, *biases, *own, *pieces)


def norm_backward(grad_in, scaled, inv_std, gain_row):
    grad_gain = jnp.sum(grad_in * scaled, axis=0, keepdims=True)
    grad_shift = jnp.sum(grad_in, axis=0, keepdims=True)
    grad_scaled = grad_in * gain_row
    mean_first = jnp.mean(grad_scaled, axis=1, keepdims=True)
    mean_second = jnp.mean(grad_scaled * scaled, axis=1, keepdims=True)
    return inv_std * (grad_scaled - mean_first - scaled * mean_second), grad_gain, grad_shift


def hidden_back_kernel(
    pair, info_ref, low_ref, at_ref, slope_ref, turn_ref, up_ref, down_ref, acc_ref,
    send_ref, near_ref, pass_ref, out_ref, b_ref, *refs,
):
    full, sem = refs[:-1], refs[-1]
    unit = turn_ref.shape[0] // 8
    low = low_ref[...]
    out_ref[...] = acc_ref[...]
    for k, r in enumerate(pair):
        grad_down = mm(at_ref[r], low).astype(BF16)
        for i in range(8):
            full[k][(2 * i + 1) * unit : (2 * i + 2) * unit] = grad_down[i * unit : (i + 1) * unit]
        pre_low = (mm_nt(low, down_ref[r]) * slope_ref[r]).astype(BF16)
        grad_up = mm(turn_ref[...], pre_low).astype(BF16)
        for i in range(8):
            full[k][2 * i * unit : (2 * i + 1) * unit] = grad_up[i * unit : (i + 1) * unit]
        b_ref[8 * k : 8 * k + 8] = jnp.broadcast_to(jnp.sum(pre_low.astype(F32), 0, keepdims=True), (8, b_ref.shape[1]))
        out_ref[...] += mm_nt(pre_low, up_ref[r])
    wait(start(blocks_out([(f, 2 * unit) for f in full], info_ref, send_ref, near_ref, pass_ref), sem))


def hidden_back(info, pair, mixed_low, act_t, slope, normed_t, up, down, acc):
    total, width = mixed_low.shape
    k = len(pair)
    return pl.pallas_call(
        partial(hidden_back_kernel, pair),
        in_specs=[SMEM] + [VMEM] * 7,
        out_specs=[HBM] * 3 + [VMEM] * 2,
        out_shape=(
            shape((k * width, width), BF16),
            shape((k * width // 2, width), BF16),
            shape((k * width // 2, width), BF16),
            shape((total, width), F32),
            shape((8 * k, width), F32),
        ),
        scratch_shapes=[pltpu.VMEM((2 * width, width), BF16) for _ in pair] + [DMA],
        input_output_aliases={7: 3},
        compiler_params=params(24),
        cost_estimate=cost(7 * k, 8 * k),
        name="hidden_back",
    )(info, mixed_low, act_t, slope, normed_t, up, down, acc)


def norm_back_kernel(attended_ref, grad_ref, vec_ref, sums_ref, out_ref, low_ref, all_ref):
    scaled, inv = norm_parts(attended_ref[...])
    grad, grad_gain, grad_shift = norm_backward(grad_ref[...], scaled, inv, vec_ref[0:1].astype(F32))
    out_ref[...] = grad
    low_ref[...] = grad.astype(BF16)
    all_ref[...] = sums_ref[...]
    all_ref[3:4] = grad_gain
    all_ref[4:5] = grad_shift
    all_ref[5:6] = jnp.sum(grad, 0, keepdims=True)


def norm_back(attended, grad, vec, sums):
    total, width = attended.shape
    return pl.pallas_call(
        norm_back_kernel,
        in_specs=[VMEM] * 4,
        out_specs=[VMEM] * 3,
        out_shape=(shape((total, width), F32), shape((total, width), BF16), shape((8, width), F32)),
        input_output_aliases={1: 0},
        compiler_params=params(24),
        cost_estimate=cost(2, 6),
        name="norm_back",
    )(attended, grad, vec, sums)


def attend_back_kernel(words, gw, heads, final, count, info_ref, rows_ref, lt_ref, low_ref, up_ref, acc_ref, *refs):
    pw_ref, pe_ref, ctx_ref = refs[:3]
    pieces, refs = refs[3 : 3 + count], refs[3 + count :]
    if final:
        spans_ref, send_ref, near_ref, pass_ref, words_ref, ents_ref, pos_s, *refs = refs
    else:
        send_ref, near_ref, pass_ref, out_ref, *refs = refs
    (
        w_s, pw_s, pe_s, ctx_s, qw_s, qe_s, k_s, v_s, dc_s, p_s, ds_s, dpw_s, dpe_s, full_s, sem,
    ) = refs
    half = 2 * gw
    total = rows_ref.shape[0]
    size = w_s.shape[0] // 8
    saved = start([(pw_ref, pw_s), (pe_ref, pe_s)], sem.at[0])
    if count == 1:
        reads = start([(pieces[0], w_s)], sem.at[1])
    else:
        reads = start(place(pieces, info_ref, size, (w_s,)), sem.at[1])
    last = start([(ctx_ref, ctx_s)], sem.at[2])
    wait(saved)
    split_heads(words, gw, heads, pw_s, pe_s, qw_s, qe_s, k_s, v_s)
    wait(reads)
    grad_ctx = mm_nt(low_ref[...], w_s[6 * gw : 7 * gw]).astype(BF16)
    for h in range(heads):
        dc_s[h] = grad_ctx[:, h * HEAD_DIM : (h + 1) * HEAD_DIM]
    wait(last)
    full_s[6 * gw : 7 * gw] = mm_tn(ctx_s[...], low_ref[...]).astype(BF16)
    block = 128
    for h in range(heads):
        o = h * HEAD_DIM
        e = o + HEAD_DIM

        def step(qb, carry):
            rows = pl.ds(pl.multiple_of(qb * block, block), block)
            logt = lt_ref[h : h + 1, rows]
            pw = jnp.exp(mm_nt(k_s[h, :words], qw_s[h, rows]) * SCALE - logt)
            pe = jnp.exp(mm_nt(k_s[h, words:], qe_s[h, rows]) * SCALE - logt)
            gw_ = mm_nt(v_s[h, :words], dc_s[h, rows])
            ge_ = mm_nt(v_s[h, words:], dc_s[h, rows])
            p_s[:words, rows] = pw.astype(BF16)
            p_s[words:, rows] = pe.astype(BF16)
            dot = jnp.sum(pw * gw_, 0, keepdims=True) + jnp.sum(pe * ge_, 0, keepdims=True)
            ds_s[:words, rows] = (pw * (gw_ - dot)).astype(BF16)
            ds_s[words:, rows] = (pe * (ge_ - dot)).astype(BF16)
            return carry

        lax.fori_loop(0, total // block, step, 0)
        dv = mm(p_s[...], dc_s[h]).astype(BF16)
        dkw = (mm(ds_s[:words], qw_s[h]) * SCALE).astype(BF16)
        dke = (mm(ds_s[words:], qe_s[h]) * SCALE).astype(BF16)
        dqw = (mm_tn(ds_s[:words], k_s[h, :words]) * SCALE).astype(BF16)
        dqe = (mm_tn(ds_s[words:], k_s[h, words:]) * SCALE).astype(BF16)
        dpw_s[:, o:e] = dqw[:words]
        dpw_s[:, gw + o : gw + e] = dqe[:words]
        dpw_s[:, half + o : half + e] = dkw
        dpw_s[:, half + gw + o : half + gw + e] = dv[:words]
        dpe_s[:, o:e] = dke
        dpe_s[:, gw + o : gw + e] = dv[words:]
        dpe_s[:, half + o : half + e] = dqw[words:]
        dpe_s[:, half + gw + o : half + gw + e] = dqe[words:]
    dpw = dpw_s[...]
    dpe = dpe_s[...]
    rows_w = rows_ref[:words]
    rows_e = rows_ref[words:]
    full_s[:half] = mm_tn(dpw[:, :half], rows_w).astype(BF16)
    full_s[half : 2 * half] = (mm_tn(dpw[:, half:], rows_w) + mm_tn(dpe[:, :half], rows_e)).astype(BF16)
    full_s[2 * half : 3 * half] = mm_tn(dpe[:, half:], rows_e).astype(BF16)
    sw = jnp.sum(dpw.astype(F32), 0, keepdims=True)
    se = jnp.sum(dpe.astype(F32), 0, keepdims=True)
    sum_a = jnp.concatenate([sw[:, :half], sw[:, half:] + se[:, :half]], 1)
    sum_b = jnp.concatenate([se[:, half:], jnp.zeros((1, half), F32)], 1)
    spare = w_s.shape[0] - 7 * gw
    row = lax.broadcasted_iota(jnp.int32, (spare, 2 * half), 0)
    sums = jnp.where(row == 0, sum_a, jnp.where(row == 1, sum_b, jnp.where(row == 2, up_ref[0:1], 0.0)))
    full_s[7 * gw :] = sums.astype(BF16)
    if final:
        grad = acc_ref[words:] + mm(dpe, w_s[half : 3 * half])
        ents_ref[...] = grad
        spans = spans_ref[info_ref[0]]
        begin = spans[:, 0:1]
        end = spans[:, 1:2]
        position = lax.broadcasted_iota(jnp.int32, (total - words, words), 1)
        inside = jnp.where(jnp.logical_and(position >= begin, position < end), 1.0, 0.0).astype(BF16)
        scaled = grad * (1.0 / (end - begin).astype(F32))
        high = scaled.astype(BF16)
        rest = (scaled - high.astype(F32)).astype(BF16)
        pos_s[...] = (mm_tn(inside, high) + mm_tn(inside, rest)).astype(BF16)
        sources = [(full_s, size), (pos_s, words // 8)]
        writes = start(blocks_out(sources, info_ref, send_ref, near_ref, pass_ref), sem.at[3])
        words_ref[...] = acc_ref[:words] + mm(dpw, w_s[: 2 * half])
    else:
        writes = start(blocks_out([(full_s, size)], info_ref, send_ref, near_ref, pass_ref), sem.at[3])
        out_ref[:words] = acc_ref[:words] + mm(dpw, w_s[: 2 * half])
        out_ref[words:] = acc_ref[words:] + mm(dpe, w_s[half : 3 * half])
    wait(writes)


def attend_back(info, rows_low, saved, low, up_sums, acc, pieces, words, heads, rows, spans=None):
    total, width = rows_low.shape
    pw, pe, ctx, lt = saved
    ents = total - words
    gw = heads * HEAD_DIM
    count = len(pieces)
    final = spans is not None
    moved = rows + words if final else rows
    grads = (shape((words, width), F32), shape((ents, width), F32)) if final else (shape((total, width), F32),)
    return pl.pallas_call(
        partial(attend_back_kernel, words, gw, heads, final, count),
        in_specs=[SMEM] + [VMEM] * 5 + [HBM] * (3 + count) + [VMEM] * final,
        out_specs=[HBM] * 3 + [VMEM] * len(grads),
        out_shape=(
            shape((moved // 2, width), BF16),
            shape((moved // 4, width), BF16),
            shape((moved // 4, width), BF16),
        )
        + grads,
        scratch_shapes=[pltpu.VMEM((words, width), BF16)] * final
        + [
            pltpu.VMEM((rows, width), BF16),
            pltpu.VMEM((words, 4 * gw), BF16),
            pltpu.VMEM((ents, 4 * gw), BF16),
            pltpu.VMEM((total, gw), BF16),
        ]
        + [pltpu.VMEM((heads, total, HEAD_DIM), BF16) for _ in range(5)]
        + [
            pltpu.VMEM((total, total), BF16),
            pltpu.VMEM((total, total), BF16),
            pltpu.VMEM((words, 4 * gw), BF16),
            pltpu.VMEM((ents, 4 * gw), BF16),
            pltpu.VMEM((rows, width), BF16),
            DMA((4,)),
        ],
        input_output_aliases={} if final else {5: 3},
        compiler_params=params(32),
        cost_estimate=cost(11, 8),
        name="attend_back",
    )(info, rows_low, lt, low, up_sums, acc, pw, pe, ctx, *pieces, *((spans,) if final else ()))


def spread_query_kernel(info_ref, *refs):
    pieces = refs[:8]
    query_ref, key_ref, value_ref, out_ref, qb_ref, vb_ref, ub_ref, s, sem = refs[8:]
    wait(start(place(pieces, info_ref, s.shape[0] // 8, (s,)), sem))
    gw = key_ref.shape[0]
    for i, k in ((0, 0), (1, 1), (2, 4), (3, 5)):
        query_ref[i] = s[k * gw : (k + 1) * gw].astype(F32)
    key_ref[...] = s[2 * gw : 3 * gw].astype(F32)
    value_ref[...] = s[3 * gw : 4 * gw].astype(F32)
    out_ref[...] = s[6 * gw : 7 * gw].astype(F32)
    rows = s[7 * gw : 7 * gw + TILE].astype(F32)
    qb_ref[0:1] = rows[0:1, :gw]
    qb_ref[1:2] = rows[0:1, gw : 2 * gw]
    qb_ref[2:3] = rows[1:2, :gw]
    qb_ref[3:4] = rows[1:2, gw : 2 * gw]
    vb_ref[...] = rows[0:1, 3 * gw :]
    ub_ref[...] = rows[2:3]


def spread_query(info, pieces, gw):
    unit, width = pieces[0].shape
    flat = shape((gw, width), F32)
    return pl.pallas_call(
        spread_query_kernel,
        in_specs=[SMEM] + [HBM] * 8,
        out_specs=[VMEM] * 7,
        out_shape=(
            shape((4, gw, width), F32), flat, flat, flat,
            shape((4, gw), F32), shape((1, gw), F32), shape((1, width), F32),
        ),
        scratch_shapes=[pltpu.VMEM((8 * unit, width), BF16), DMA],
        compiler_params=params(16),
        cost_estimate=cost(0.5, 7),
        name="spread_query",
    )(info, *pieces)


def spread_hidden_kernel(info_ref, *refs):
    pieces = refs[:8]
    up_ref, down_ref, up_s, down_s, sem = refs[8:]
    wait(start(place(pieces, info_ref, up_ref.shape[0] // 8, (up_s, down_s)), sem))
    up_ref[...] = up_s[...].astype(F32)
    down_ref[...] = down_s[...].astype(F32)


def spread_hidden(info, pieces):
    rows, width = pieces[0].shape
    out = shape((4 * rows, width), F32)
    return pl.pallas_call(
        spread_hidden_kernel,
        in_specs=[SMEM] + [HBM] * 8,
        out_specs=[VMEM] * 2,
        out_shape=(out, out),
        scratch_shapes=[pltpu.VMEM((4 * rows, width), BF16)] * 2 + [DMA],
        compiler_params=params(16),
        cost_estimate=cost(0.5, 7),
        name="spread_hidden",
    )(info, *pieces)


def spread_pos_kernel(info_ref, *refs):
    pieces = refs[:8]
    pos_ref, s, sem = refs[8:]
    wait(start(place(pieces, info_ref, s.shape[0] // 8, (s,)), sem))
    pos_ref[...] = s[...].astype(F32)


def spread_pos(info, pieces):
    rows, width = pieces[0].shape
    return pl.pallas_call(
        spread_pos_kernel,
        in_specs=[SMEM] + [HBM] * 8,
        out_specs=VMEM,
        out_shape=shape((8 * rows, width), F32),
        scratch_shapes=[pltpu.VMEM((8 * rows, width), BF16), DMA],
        compiler_params=params(8),
        cost_estimate=cost(0.5, 3),
        name="spread_pos",
    )(info, *pieces)


class Links:
    def __init__(self):
        self.dp = lax.axis_size("dp")
        self.ring = lax.axis_size("tensor")
        dp_index = lax.axis_index("dp")
        self.z = lax.axis_index("tensor")
        self.core = dp_index % 2
        self.bits = (self.dp // 2).bit_length() - 1
        self.bit = [(dp_index // (2 << k)) % 2 for k in range(self.bits)]

    def shift_z(self, v, by):
        n = self.ring
        return lax.ppermute(v, "tensor", [(i, (i + by) % n) for i in range(n)])

    def swap_z(self, v, mask):
        return lax.ppermute(v, "tensor", [(i, i ^ mask) for i in range(self.ring)])

    def swap(self, v, code):
        return lax.ppermute(v, "dp", [(i, i ^ code) for i in range(self.dp)])

    def swap_core(self, v):
        return self.swap(v, 1)

    def first(self, v):
        return lax.ppermute(v, "dp", [(i, i ^ (4 if i % 2 else 2)) for i in range(self.dp)])

    def second(self, v):
        return lax.ppermute(v, "dp", [(i, i ^ (2 if i % 2 else 4)) for i in range(self.dp)])


def after(value, *others):
    return lax.optimization_barrier((value,) + others)[0]


def sync(*values):
    return lax.optimization_barrier(values)


def add_low(*parts):
    total = parts[0].astype(F32)
    for part in parts[1:]:
        total = total + part.astype(F32)
    return total.astype(BF16)


class Blocks:
    def __init__(self, links, send, near, far):
        self.links, self.send, self.near, self.far = links, send, near, far
        self.unit = near.shape[0] // 2

    def one(self):
        return add_low(self.far, self.got[2 * self.unit :])

    def two(self):
        u = self.unit
        return add_low(self.near[u:], self.got[u : 2 * u], self.a[u:])

    def rest(self, low, high, *more):
        value = add_low(self.near[low:high], self.got[low:high], self.a[low:high], self.b[low:high], *more)
        for j in range(2, self.links.bits):
            value = add_low(value, self.links.swap(value, 2 << j))
        return value


def shards(
    word_in,
    entity_in,
    entity_spans,
    word_mask,
    entity_mask,
    pos_table,
    query_w,
    query_b,
    key_w,
    value_w,
    value_b,
    out_w,
    out_b,
    norm1_gain,
    norm1_bias,
    up_w,
    up_b,
    down_w,
    down_b,
    norm2_gain,
    norm2_bias,
    cot_words,
    cot_entities,
):
    links = Links()
    n = links.ring
    z = links.z
    words = cot_words.shape[0]
    ents = cot_entities.shape[0]
    width = word_in.shape[1]
    gw = key_w.shape[1]
    heads = gw // HEAD_DIM
    rows = -(-(7 * gw + 3) // (8 * TILE)) * 8 * TILE
    part = 4 * links.core + 2 * links.bit[0] + links.bit[1]
    info = jnp.stack([z, links.core, part, 2 - links.core]).astype(jnp.int32)

    own_w, piece_q, piece_f = pack(
        info, query_b, value_b[None], up_b[None], jnp.swapaxes(query_w, 1, 2), key_w.T, value_w.T, out_w, up_w, down_w, rows
    )
    first, second, core, shift = links.first, links.second, links.swap_core, links.shift_z
    v1, v2, v3 = (shift(piece_q, r) for r in range(1, n))
    rows_low, acc = start_rows(info, word_in, entity_in, entity_spans, pos_table, out_b[None], words, ents)
    saved = []
    biases = []

    def attend_one(acc, pieces):
        pw, pe, ctx, lt, bias, acc = attend(info, rows_low, acc, pieces, words, heads, rows)
        saved.append((pw, pe, ctx, lt))
        biases.append(bias)
        return acc

    acc = attend_one(acc, (own_w,))
    acc, v1, piece_f = sync(acc, v1, piece_f)
    a1, b1, f1 = first(v1), second(v1), shift(piece_f, 1)
    acc, v1, a1, b1, v2, v3, piece_f = sync(acc, v1, a1, b1, v2, v3, piece_f)
    c1, kv, ka, kb, a2, b2 = second(a1), core(v1), core(a1), core(b1), first(v2), second(v2)
    acc, c1, kv, ka, kb, a2, b2, piece_f, v3 = sync(acc, c1, kv, ka, kb, a2, b2, piece_f, v3)
    kc, f2, f3 = core(c1), shift(piece_f, 2), shift(piece_f, 3)
    acc, kc, a2, v3 = sync(acc, kc, a2, v3)
    group_1 = (v1, a1, b1, c1, kv, ka, kb, kc)

    c2, a3, b3 = second(a2), first(v3), second(v3)
    acc = attend_one(acc, group_1)
    acc, c2, a3, b3, f1, f2, f3 = sync(acc, c2, a3, b3, f1, f2, f3)
    kv, ka, kb, kc = core(v2), core(a2), core(b2), core(c2)
    acc, kv, ka, kb, kc, far_f, a3, v3 = sync(acc, kv, ka, kb, kc, jnp.concatenate([f1, f2, f3], 0), a3, v3)
    group_2 = (v2, a2, b2, c2, kv, ka, kb, kc)

    c3, af, bf, kv, ka = second(a3), first(far_f), second(far_f), core(v3), core(a3)
    acc = attend_one(acc, group_2)
    acc, c3, af, bf, kv, ka = sync(acc, c3, af, bf, kv, ka)
    kb, kc = core(b3), core(c3)
    acc, kb, kc, af, bf, far_f = sync(acc, kb, kc, af, bf, far_f)
    group_3 = (v3, a3, b3, c3, kv, ka, kb, kc)

    cf, kv, ka, kb = second(af), core(far_f), core(af), core(bf)
    acc = attend_one(acc, group_3)
    attended, cf, kv, ka, kb = sync(acc, cf, kv, ka, kb)
    ffn_pieces = (far_f, af, bf, cf, kv, ka, kb, core(cf))
    query_groups = ((own_w,), group_1, group_2, group_3)

    vec = jnp.stack([norm1_gain, norm1_bias, down_b, norm2_gain, norm2_bias] + [down_b] * 3)
    normed_t, act_t, slope, up, down, out_words, out_ents, mixed_low, acc, sums = hidden(
        info, attended, vec, word_mask, entity_mask, cot_words, cot_entities, biases, (up_w, down_w), ffn_pieces
    )

    size = width // 4
    unit = rows // 8
    up_sums = [None] * n

    def ffn_pair(pair, acc):
        send, near, far, acc, up_sum = hidden_back(info, pair, mixed_low, act_t, slope, normed_t, up, down, acc)
        for k, r in enumerate(pair):
            up_sums[r] = up_sum[8 * k : 8 * k + 8]
        return Blocks(links, send, near, far), acc

    fa, acc = ffn_pair((1, 2), acc)
    fa.got = core(fa.send)
    fb, acc = ffn_pair((3, 0), acc)
    acc, fa.got = sync(acc, fa.got)
    one_a = fa.one()
    acc, attended_low, sums = norm_back(attended, acc, vec, sums)
    acc, one_a, sums = sync(acc, one_a, sums)

    def back(r, acc, spans=None):
        send, near, far, *acc = attend_back(
            info, rows_low, saved[r], attended_low, up_sums[r], acc, query_groups[r], words, heads, rows, spans
        )
        return Blocks(links, send, near, far), *acc

    fa.a, fb.got, more = first(one_a), core(fb.send), core(sums)
    q1, acc = back(1, acc)
    acc, fa.a, fb.got, more = sync(acc, fa.a, fb.got, more)
    acc, two_a, one_b, sums = sync(acc, fa.two(), fb.one(), sums + more)

    fa.b, fb.a, q1.got, more = second(two_a), first(one_b), core(q1.send), links.swap(sums, 2)
    q2, acc = back(2, acc)
    acc, fa.b, fb.a, q1.got, more = sync(acc, fa.b, fb.a, q1.got, more)
    acc, r1, r2, two_b, one_1, sums = sync(
        acc, fa.rest(0, size), fa.rest(size, 2 * size), fb.two(), q1.one(), sums + more
    )

    z1, z2, fb.b, q1.a, q2.got = shift(r1, -1), shift(r2, -2), second(two_b), first(one_1), core(q2.send)
    q3, acc = back(3, acc)
    acc, z1, z2, fb.b, q1.a, q2.got = sync(acc, z1, z2, fb.b, q1.a, q2.got)
    acc, r3, two_1, one_2 = sync(acc, fb.rest(0, size), q1.two(), q2.one())

    z3, q1.b, q2.a, q3.got, more = shift(r3, -3), second(two_1), first(one_2), core(q3.send), links.swap(sums, 4)
    q4, grad_words, grad_ents = back(0, acc, entity_spans)
    q4.send, z3, q1.b, q2.a, q3.got, more = sync(q4.send, z3, q1.b, q2.a, q3.got, more)

    q4.got = core(q4.send)
    value_1, two_2, one_3 = q1.rest(0, unit), q2.two(), q3.one()
    y1, q2.b, q3.a = shift(value_1, -1), second(two_2), first(one_3)
    sums = sums + more
    for j in range(2, links.bits):
        sums = sums + links.swap(sums, 2 << j)
    own_f = fb.rest(size, 2 * size, z1, z2, z3)
    q4.got, q2.b, q3.a, sums, own_f = sync(q4.got, q2.b, q3.a, sums, own_f)

    q4.a, y2, q3.b, ga = first(q4.one()), shift(q2.rest(0, unit), -2), second(q3.two()), first(own_f)
    q4.a, q3.b, y1, ga, own_f, sums = sync(q4.a, q3.b, y1, ga, own_f, sums)

    q4.b, y3, gb, more = second(q4.two()), shift(q3.rest(0, unit), -3), second(own_f), links.swap_z(sums, 1)
    q4.b, y2, gb, more, ga, sums = sync(q4.b, y2, gb, more, ga, sums)

    pos = q4.rest(unit, unit + words // 8)
    p1, p2, p3 = (links.swap_z(pos, mask) for mask in (1, 2, 3))
    gc = second(ga)
    sums = sums + more
    p1, p2, p3, y3, gc, pos, sums = sync(p1, p2, p3, y3, gc, pos, sums)

    pos = ((pos.astype(F32) + p1.astype(F32)) + (p2.astype(F32) + p3.astype(F32))).astype(BF16)
    own_q = q4.rest(0, unit, y1, y2, y3)
    qa, qb, pa, pb, more = first(own_q), second(own_q), first(pos), second(pos), links.swap_z(sums, 2)
    total_sums = sums + more
    qa, qb, pa, pb, own_q, pos, own_f, ga, gb, gc = sync(qa, qb, pa, pb, own_q, pos, own_f, ga, gb, gc)
    near_q = (own_q, qa, qb, second(qa))
    near_p = (pos, pa, pb, second(pa))
    near_f = (own_f, ga, gb, gc)
    grad_up, grad_down = spread_hidden(info, near_f + tuple(core(v) for v in near_f))
    pos_sum = spread_pos(info, near_p + tuple(core(v) for v in near_p))
    grad_query_t, grad_key_t, grad_value_t, grad_out, grad_query_b, grad_value_b, grad_up_b = spread_query(
        info, near_q + tuple(core(v) for v in near_q), gw
    )
    return (
        out_words,
        out_ents,
        grad_words,
        grad_ents,
        pos_sum,
        jnp.swapaxes(grad_query_t, 1, 2),
        grad_query_b,
        grad_key_t.T,
        grad_value_t.T,
        grad_value_b[0],
        grad_out,
        total_sums[5],
        total_sums[3],
        total_sums[4],
        grad_up,
        grad_up_b[0],
        grad_down,
        total_sums[2],
        total_sums[0],
        total_sums[1],
    )


def solution(mesh):
    rows = P(("dp", "tensor"), None)
    last = P(None, "tensor")
    placed = (
        P("dp", None),
        P("dp", None),
        P("dp", None, None),
        P("dp", None),
        P("dp", None),
        P(),
        P(None, None, "tensor"),
        last,
        last,
        last,
        P("tensor"),
        P("tensor", None),
        P(),
        P(),
        P(),
        last,
        P("tensor"),
        P("tensor", None),
        P(),
        P(),
        P(),
        rows,
        rows,
    )
    return jax.shard_map(
        shards,
        mesh=mesh,
        in_specs=placed,
        out_specs=(
            rows,
            rows,
            rows,
            rows,
            P(),
            P(None, None, "tensor"),
            last,
            last,
            last,
            P("tensor"),
            P("tensor", None),
            P(),
            P(),
            P(),
            last,
            P("tensor"),
            P("tensor", None),
            P(),
            P(),
            P(),
        ),
        check_vma=False,
    )
```

```python
from functools import partial

import jax
import jax.numpy as jnp
from jax import lax
from jax.experimental import pallas as pl
from jax.experimental.pallas import tpu as pltpu
from jax.sharding import PartitionSpec as P

HEAD_DIM = 64
SCALE = HEAD_DIM**-0.5
norm_epsilon = 1e-12
F32 = jnp.float32
BF16 = jnp.bfloat16
NT = (((1,), (1,)), ((), ()))
TN = (((0,), (0,)), ((), ()))
ERFC_STEP = 0.35
ERFC_POLY = (
    0.1396196249207051,
    0.13989555693599826,
    0.11957015144655456,
    0.10661400019997494,
    -0.025870835326937874,
    0.16337919550284652,
    -0.25954764983005574,
    0.14589250699009862,
    -0.029552569422939476,
)
TILE = 16
VMEM = pl.BlockSpec(memory_space=pltpu.VMEM)
SMEM = pl.BlockSpec(memory_space=pltpu.SMEM)
HBM = pl.BlockSpec(memory_space=pltpu.HBM)
DMA = pltpu.SemaphoreType.DMA


def mm(a, b):
    return jnp.dot(a, b, preferred_element_type=F32)


def mm_nt(a, b):
    return lax.dot_general(a, b, NT, preferred_element_type=F32)


def mm_tn(a, b):
    return lax.dot_general(a, b, TN, preferred_element_type=F32)


def params(mib):
    return pltpu.CompilerParams(vmem_limit_bytes=mib << 20)


def cost(gflop, mbytes):
    return pl.CostEstimate(
        flops=int(gflop * 1e9), bytes_accessed=int(mbytes * 1e6), transcendentals=0
    )


def shape(dims, kind):
    return jax.ShapeDtypeStruct(dims, kind)


def far(values):
    return tuple(pltpu.with_memory_space_constraint(v, pltpu.HBM) for v in values)


def far_shape(dims, kind):
    return pltpu.HBM(dims, kind)


def start(pairs, sem):
    copies = [pltpu.make_async_copy(source, target, sem) for source, target in pairs]
    for copy in copies:
        copy.start()
    return copies


def wait(copies):
    for copy in copies:
        copy.wait()


def rows_at(first, size):
    return pl.ds(pl.multiple_of(first, TILE), size)


def place(pieces, info_ref, unit, targets, skip=0):
    part, first = info_ref[2], info_ref[3]
    second = 3 - first
    pairs = []
    for piece, code in zip(pieces, (0, first, second, 3, 4, 4 + second, 4 + first, 7)):
        row = lax.bitwise_xor(part, jnp.int32(code)) * unit
        for t, target in enumerate(targets):
            pairs.append((piece.at[pl.ds(skip + t * unit, unit)], target.at[rows_at(row, unit)]))
    return pairs


def blocks_out(sources, info_ref, send_ref, near_ref, pass_ref):
    part, first = info_ref[2], info_ref[3]
    second = 3 - first
    keep = (0, second, first, 3)
    send = (4, 4 + first, 4 + second, 7)
    total = sum(unit for _, unit in sources)
    pairs = []
    for i in range(4):
        done = 0
        for source, unit in sources:
            other = lax.bitwise_xor(part, jnp.int32(send[i])) * unit
            mine = lax.bitwise_xor(part, jnp.int32(keep[i])) * unit
            to = near_ref if i < 2 else pass_ref
            pairs.append((source.at[rows_at(other, unit)], send_ref.at[pl.ds(i * total + done, unit)]))
            pairs.append((source.at[rows_at(mine, unit)], to.at[pl.ds((i % 2) * total + done, unit)]))
            done += unit
    return pairs


def own_parts(query_ref, key_ref, value_ref, out_ref):
    return (query_ref.at[0], query_ref.at[1], key_ref, value_ref, query_ref.at[2], query_ref.at[3], out_ref)


def spare_rows(qb_ref, vb_ref, ub_ref, spare):
    qb = qb_ref[...].astype(F32)
    none = jnp.zeros((1, qb.shape[1]), F32)
    first = jnp.concatenate([qb[0:1], qb[1:2], none, vb_ref[...].astype(F32)], 1)
    second = jnp.concatenate([qb[2:3], qb[3:4], none, none], 1)
    row = lax.broadcasted_iota(jnp.int32, (spare, first.shape[1]), 0)
    rows = jnp.where(row == 0, first, jnp.where(row == 1, second, jnp.where(row == 2, ub_ref[...].astype(F32), 0.0)))
    return rows.astype(BF16)


def pack_kernel(
    gw, info_ref, qb_ref, vb_ref, ub_ref, query_ref, key_ref, value_ref, ow_ref, up_ref, down_ref,
    piece_ref, ffn_ref, w_s, f_s, sem,
):
    part = info_ref[2]
    size = piece_ref.shape[0]
    low = lax.div(part * size, jnp.int32(gw))
    copies = []
    for i, ref in enumerate(own_parts(query_ref, key_ref, value_ref, ow_ref)):
        needed = jnp.logical_or(low == i, low + 1 == i)
        copies.append((needed, pltpu.make_async_copy(ref, w_s.at[pl.ds(i * gw, gw)], sem.at[0])))
    for needed, copy in copies:
        pl.when(needed)(copy.start)
    unit = f_s.shape[0] // 2
    ffn = start(
        [(v.at[rows_at(part * unit, unit)], f_s.at[pl.ds(i * unit, unit)]) for i, v in enumerate((up_ref, down_ref))],
        sem.at[1],
    )
    w_s[7 * gw :] = spare_rows(qb_ref, vb_ref, ub_ref, w_s.shape[0] - 7 * gw)
    for needed, copy in copies:
        pl.when(needed)(copy.wait)
    piece = start([(w_s.at[rows_at(part * size, size)], piece_ref)], sem.at[2])
    wait(ffn)
    last = start([(f_s, ffn_ref)], sem.at[3])
    wait(piece)
    wait(last)


def pack(info, biases, own, up_w, down_w, rows):
    gw, width = own[1].shape
    unit = up_w.shape[0] // 8
    return pl.pallas_call(
        partial(pack_kernel, gw),
        in_specs=[SMEM] + [VMEM] * 3 + [HBM] * 6,
        out_specs=[HBM] * 2,
        out_shape=(far_shape((rows // 8, width), BF16), far_shape((2 * unit, width), BF16)),
        scratch_shapes=[pltpu.VMEM((rows, width), BF16), pltpu.VMEM((2 * unit, width), BF16), DMA((4,))],
        compiler_params=params(4),
        cost_estimate=cost(0.01, 3),
        name="pack",
    )(info, *biases, *far(own + (up_w, down_w)))


def start_kernel(info_ref, words_ref, ents_ref, spans_ref, table_ref, bias_ref, low_ref, resid_ref, w_s, e_s, t_s, sem):
    words, count = w_s.shape[0], e_s.shape[0]
    z = info_ref[0]
    ents = start(
        [(ents_ref.at[rows_at(z * count, count)], e_s), (table_ref, t_s)],
        sem.at[0],
    )
    reads = start([(words_ref.at[rows_at(z * words, words)], w_s)], sem.at[1])
    spans = spans_ref[z]
    begin = spans[:, 0:1]
    end = spans[:, 1:2]
    position = lax.broadcasted_iota(jnp.int32, (count, words), 1)
    inside = jnp.where(jnp.logical_and(position >= begin, position < end), 1.0, 0.0).astype(BF16)
    share = 1.0 / (end - begin).astype(F32)
    out_b = bias_ref[...].astype(F32)
    wait(ents)
    rows = e_s[...].astype(F32) + mm(inside, t_s[...]) * share
    low_ref[words:] = rows.astype(BF16)
    resid_ref[words:] = rows + out_b
    wait(reads)
    low_ref[:words] = w_s[...]
    resid_ref[:words] = w_s[...].astype(F32) + out_b


def start_rows(info, word_in, entity_in, spans, table, out_b, words, ents):
    width = word_in.shape[1]
    total = words + ents
    return pl.pallas_call(
        start_kernel,
        in_specs=[SMEM, HBM, HBM, VMEM, HBM, VMEM],
        out_specs=[VMEM] * 2,
        out_shape=(shape((total, width), BF16), shape((total, width), F32)),
        scratch_shapes=[
            pltpu.VMEM((words, width), BF16),
            pltpu.VMEM((ents, width), BF16),
            pltpu.VMEM(table.shape, BF16),
            DMA((2,)),
        ],
        compiler_params=params(6),
        cost_estimate=cost(0.5, 6),
        name="start_rows",
    )(info, *far((word_in, entity_in)), spans, *far((table,)), out_b)


def split_heads(words, gw, heads, pw_ref, pe_ref, qw_s, qe_s, k_s, v_s):
    half = 2 * gw
    for h in range(heads):
        o = h * HEAD_DIM
        e = o + HEAD_DIM
        qw_s[h, :words] = pw_ref[:, o:e] * SCALE
        qw_s[h, words:] = pe_ref[:, half + o : half + e] * SCALE
        qe_s[h, :words] = pw_ref[:, gw + o : gw + e] * SCALE
        qe_s[h, words:] = pe_ref[:, half + gw + o : half + gw + e] * SCALE
        k_s[h, :words] = pw_ref[:, half + o : half + e]
        k_s[h, words:] = pe_ref[:, o:e]
        v_s[h, :words] = pw_ref[:, half + gw + o : half + gw + e]
        v_s[h, words:] = pe_ref[:, gw + o : gw + e]


def attend_kernel(words, gw, heads, count, info_ref, rows_ref, acc_ref, *refs):
    own = count == 4
    small, refs = (refs[:3], refs[3:]) if own else ((), refs)
    pieces = refs[:count]
    pw_ref, pe_ref, ctx_ref, lt_ref, bias_ref, out_ref, w_s, pw_s, pe_s, ctx_s, qw_s, qe_s, k_s, v_s, sem = refs[count:]
    half = 2 * gw
    if own:
        reads = start([(v, w_s.at[pl.ds(i * gw, gw)]) for i, v in enumerate(own_parts(*pieces))], sem.at[0])
        w_s[7 * gw :] = spare_rows(*small, w_s.shape[0] - 7 * gw)
        wait(reads)
    else:
        wait(start(place(pieces, info_ref, w_s.shape[0] // 8, (w_s,)), sem.at[0]))
    rows_b = w_s[7 * gw : 7 * gw + TILE]
    bias_ref[...] = rows_b
    rows_b = rows_b.astype(F32)
    bias_e = jnp.concatenate([rows_b[0:1, half:], rows_b[1:2, :half]], 1)
    pw_s[...] = (mm_nt(rows_ref[:words], w_s[: 4 * gw]) + rows_b[0:1]).astype(BF16)
    pe_s[...] = (mm_nt(rows_ref[words:], w_s[half : 6 * gw]) + bias_e).astype(BF16)
    saves = start([(pw_s, pw_ref), (pe_s, pe_ref)], sem.at[1])
    split_heads(words, gw, heads, pw_s, pe_s, qw_s, qe_s, k_s, v_s)
    block = 128

    def step(qb, carry):
        rows = pl.ds(pl.multiple_of(qb * block, block), block)
        parts = []
        for h in range(heads):
            sw = mm_nt(qw_s[h, rows], k_s[h, :words])
            se = mm_nt(qe_s[h, rows], k_s[h, words:])
            top = jnp.maximum(jnp.max(sw, 1, keepdims=True), jnp.max(se, 1, keepdims=True))
            ew = jnp.exp(sw - top)
            ee = jnp.exp(se - top)
            total = jnp.sum(ew, 1, keepdims=True) + jnp.sum(ee, 1, keepdims=True)
            inv = 1.0 / total
            parts.append(
                mm((ew * inv).astype(BF16), v_s[h, :words]) + mm((ee * inv).astype(BF16), v_s[h, words:])
            )
            logt = top + jnp.log(total)
            lt_ref[h : h + 1, rows] = jnp.broadcast_to(logt, (block, block)).T[0:1]
        ctx_s[rows, :] = jnp.concatenate(parts, 1).astype(BF16)
        return carry

    lax.fori_loop(0, rows_ref.shape[0] // block, step, 0)
    last = start([(ctx_s, ctx_ref)], sem.at[2])
    out_ref[...] = acc_ref[...] + mm(ctx_s[...], w_s[6 * gw : 7 * gw])
    wait(saves)
    wait(last)


def attend(info, rows_low, acc, pieces, words, heads, rows, small=()):
    total, width = rows_low.shape
    ents = total - words
    gw = heads * HEAD_DIM
    count = len(pieces)
    return pl.pallas_call(
        partial(attend_kernel, words, gw, heads, count),
        in_specs=[SMEM] + [VMEM] * (2 + len(small)) + [HBM] * count,
        out_specs=[HBM] * 3 + [VMEM] * 3,
        out_shape=(
            far_shape((words, 4 * gw), BF16),
            far_shape((ents, 4 * gw), BF16),
            far_shape((total, gw), BF16),
            shape((8, total), F32),
            shape((TILE, width), BF16),
            shape((total, width), F32),
        ),
        scratch_shapes=[
            pltpu.VMEM((rows, width), BF16),
            pltpu.VMEM((words, 4 * gw), BF16),
            pltpu.VMEM((ents, 4 * gw), BF16),
            pltpu.VMEM((total, gw), BF16),
        ]
        + [pltpu.VMEM((heads, total, HEAD_DIM), BF16) for _ in range(4)]
        + [DMA((3,))],
        input_output_aliases={2: 5},
        compiler_params=params(11),
        cost_estimate=cost(8, 6),
        name="attend_own" if small else "attend_far",
    )(info, rows_low, acc, *small, *far(pieces))


def gelu_pair(x):
    size = jnp.abs(x)
    t = 1.0 / (1.0 + ERFC_STEP * size)
    poly = jnp.full_like(x, ERFC_POLY[-1])
    for c in ERFC_POLY[-2::-1]:
        poly = poly * t + c
    bell = jnp.exp(x * x * -0.5)
    tail = poly * t * bell
    below = jnp.where(x >= 0, 1.0 - tail, tail)
    return x * below, below + x * (bell * 0.3989422804014327)


def norm_parts(values):
    centered = values - jnp.mean(values, 1, keepdims=True)
    inv = lax.rsqrt(jnp.mean(centered * centered, 1, keepdims=True) + norm_epsilon)
    return centered * inv, inv


def hidden_kernel(n, info_ref, attended_ref, vec_ref, wm_ref, em_ref, cw_ref, ce_ref, *refs):
    bias_refs, refs = refs[:n], refs[n:]
    up_own, down_own = refs[:2]
    pieces, refs = (refs[2:10], refs[10:18]), refs[18:]
    turn_ref, at_ref, slope_ref, up_s, down_s, ow_ref, oe_ref, mixed_ref, grad_ref, sums_ref, low_ref, acc_s, b_s, sem = refs
    total, width = attended_ref.shape
    unit = width // 8
    reads = [start([(up_own, up_s.at[0]), (down_own, down_s.at[0])], sem.at[0])]
    for r in range(1, n):
        held, skip = pieces[r // 3], 2 * unit * ((r - 1) % 2)
        reads.append(start(place(held, info_ref, unit, (up_s.at[r], down_s.at[r]), skip), sem.at[r]))
    for r in range(n):
        b_s[r] = bias_refs[r][2:3].astype(F32)
    scaled, _ = norm_parts(attended_ref[...])
    normed = scaled * vec_ref[0:1].astype(F32) + vec_ref[1:2].astype(F32)
    low = normed.astype(BF16)
    low_ref[...] = low
    turn_ref[...] = low.T
    acc_s[...] = normed + vec_ref[2:3].astype(F32)
    block = 128

    def group(r):
        for lo in range(0, total, block):
            pre = mm(low_ref[lo : lo + block], up_s[r]) + b_s[r]
            value, slope = gelu_pair(pre)
            slope_ref[r, lo : lo + block] = slope
            value = value.astype(BF16)
            at_ref[r, :, lo : lo + block] = value.T
            acc_s[lo : lo + block] += mm(value, down_s[r])

    for r in range(n):
        wait(reads[r])
        group(r)

    words = cw_ref.shape[0]
    z = info_ref[0]
    scaled, inv = norm_parts(acc_s[...])
    gain = vec_ref[3:4].astype(F32)
    output = scaled * gain + vec_ref[4:5].astype(F32)
    ow_ref[...] = output[:words].astype(BF16)
    oe_ref[...] = output[words:].astype(BF16)

    def column(ref, size):
        return jnp.broadcast_to(ref[pl.ds(z, 1), :].astype(F32), (128, size)).T[:, 0:1]

    cot = jnp.concatenate(
        [
            column(wm_ref, words) * cw_ref[...].astype(F32),
            column(em_ref, total - words) * ce_ref[...].astype(F32),
        ],
        0,
    )
    grad, grad_gain, grad_shift = norm_backward(cot, scaled, inv, gain)
    grad_ref[...] = grad
    mixed_ref[...] = grad.astype(BF16)
    sums_ref[0:1] = grad_gain
    sums_ref[1:2] = grad_shift
    sums_ref[2:3] = jnp.sum(grad, 0, keepdims=True)
    sums_ref[3:] = jnp.zeros((5, width), F32)


def hidden(info, attended, vec, word_mask, entity_mask, cot_words, cot_ents, biases, own, pieces):
    total, width = attended.shape
    n = len(biases)
    return pl.pallas_call(
        partial(hidden_kernel, n),
        in_specs=[SMEM] + [VMEM] * (6 + n) + [HBM] * (2 + len(pieces)),
        out_specs=[VMEM] * 10,
        out_shape=(
            shape((width, total), BF16),
            shape((n, width, total), BF16),
            shape((n, total, width), F32),
            shape((n, width, width), BF16),
            shape((n, width, width), BF16),
            shape(cot_words.shape, BF16),
            shape(cot_ents.shape, BF16),
            shape((total, width), BF16),
            shape((total, width), F32),
            shape((8, width), F32),
        ),
        scratch_shapes=[
            pltpu.VMEM((total, width), BF16),
            pltpu.VMEM((total, width), F32),
            pltpu.VMEM((n, 1, width), F32),
            DMA((n,)),
        ],
        compiler_params=params(18),
        cost_estimate=cost(22, 20),
        name="hidden",
    )(info, attended, vec, word_mask, entity_mask, cot_words, cot_ents, *biases, *far(own), *far(pieces))


def norm_backward(grad_in, scaled, inv_std, gain_row):
    grad_gain = jnp.sum(grad_in * scaled, axis=0, keepdims=True)
    grad_shift = jnp.sum(grad_in, axis=0, keepdims=True)
    grad_scaled = grad_in * gain_row
    mean_first = jnp.mean(grad_scaled, axis=1, keepdims=True)
    mean_second = jnp.mean(grad_scaled * scaled, axis=1, keepdims=True)
    return inv_std * (grad_scaled - mean_first - scaled * mean_second), grad_gain, grad_shift


def hidden_back_kernel(
    pair, info_ref, low_ref, at_ref, slope_ref, turn_ref, up_ref, down_ref, acc_ref,
    send_ref, near_ref, pass_ref, out_ref, b_ref, *refs,
):
    full, sem = refs[:-1], refs[-1]
    unit = turn_ref.shape[0] // 8
    low = low_ref[...]
    out_ref[...] = acc_ref[...]
    for k, r in enumerate(pair):
        grad_down = mm(at_ref[r], low).astype(BF16)
        for i in range(8):
            full[k][(2 * i + 1) * unit : (2 * i + 2) * unit] = grad_down[i * unit : (i + 1) * unit]
        pre_low = (mm_nt(low, down_ref[r]) * slope_ref[r]).astype(BF16)
        grad_up = mm(turn_ref[...], pre_low).astype(BF16)
        for i in range(8):
            full[k][2 * i * unit : (2 * i + 1) * unit] = grad_up[i * unit : (i + 1) * unit]
        b_ref[8 * k : 8 * k + 8] = jnp.broadcast_to(jnp.sum(pre_low.astype(F32), 0, keepdims=True), (8, b_ref.shape[1]))
        out_ref[...] += mm_nt(pre_low, up_ref[r])
    wait(start(blocks_out([(f, 2 * unit) for f in full], info_ref, send_ref, near_ref, pass_ref), sem))


def hidden_back(info, pair, mixed_low, act_t, slope, normed_t, up, down, acc):
    total, width = mixed_low.shape
    k = len(pair)
    return pl.pallas_call(
        partial(hidden_back_kernel, pair),
        in_specs=[SMEM] + [VMEM] * 7,
        out_specs=[HBM] * 3 + [VMEM] * 2,
        out_shape=(
            far_shape((k * width, width), BF16),
            far_shape((k * width // 2, width), BF16),
            far_shape((k * width // 2, width), BF16),
            shape((total, width), F32),
            shape((8 * k, width), F32),
        ),
        scratch_shapes=[pltpu.VMEM((2 * width, width), BF16) for _ in pair] + [DMA],
        input_output_aliases={7: 3},
        compiler_params=params(12),
        cost_estimate=cost(7 * k, 8 * k),
        name="hidden_back",
    )(info, mixed_low, act_t, slope, normed_t, up, down, acc)


def norm_back_kernel(attended_ref, grad_ref, vec_ref, sums_ref, out_ref, low_ref, all_ref):
    scaled, inv = norm_parts(attended_ref[...])
    grad, grad_gain, grad_shift = norm_backward(grad_ref[...], scaled, inv, vec_ref[0:1].astype(F32))
    out_ref[...] = grad
    low_ref[...] = grad.astype(BF16)
    all_ref[...] = sums_ref[...]
    all_ref[3:4] = grad_gain
    all_ref[4:5] = grad_shift
    all_ref[5:6] = jnp.sum(grad, 0, keepdims=True)


def norm_back(attended, grad, vec, sums):
    total, width = attended.shape
    return pl.pallas_call(
        norm_back_kernel,
        in_specs=[VMEM] * 4,
        out_specs=[VMEM] * 3,
        out_shape=(shape((total, width), F32), shape((total, width), BF16), shape((8, width), F32)),
        input_output_aliases={1: 0},
        compiler_params=params(8),
        cost_estimate=cost(2, 6),
        name="norm_back",
    )(attended, grad, vec, sums)


def attend_back_kernel(words, gw, heads, final, count, info_ref, rows_ref, lt_ref, low_ref, up_ref, acc_ref, *refs):
    pw_ref, pe_ref, ctx_ref = refs[:3]
    pieces, refs = refs[3 : 3 + count], refs[3 + count :]
    if final:
        spans_ref, send_ref, near_ref, pass_ref, words_ref, ents_ref, pos_s, *refs = refs
    else:
        send_ref, near_ref, pass_ref, out_ref, *refs = refs
    (
        w_s, pw_s, pe_s, ctx_s, qw_s, qe_s, k_s, v_s, dc_s, p_s, ds_s, dpw_s, dpe_s, full_s, sem,
    ) = refs
    half = 2 * gw
    total = rows_ref.shape[0]
    size = w_s.shape[0] // 8
    saved = start([(pw_ref, pw_s), (pe_ref, pe_s)], sem.at[0])
    if count == 4:
        reads = start([(v, w_s.at[pl.ds(i * gw, gw)]) for i, v in enumerate(own_parts(*pieces))], sem.at[1])
    else:
        reads = start(place(pieces, info_ref, size, (w_s,)), sem.at[1])
    last = start([(ctx_ref, ctx_s)], sem.at[2])
    wait(saved)
    split_heads(words, gw, heads, pw_s, pe_s, qw_s, qe_s, k_s, v_s)
    wait(reads)
    grad_ctx = mm_nt(low_ref[...], w_s[6 * gw : 7 * gw]).astype(BF16)
    for h in range(heads):
        dc_s[h] = grad_ctx[:, h * HEAD_DIM : (h + 1) * HEAD_DIM]
    wait(last)
    full_s[6 * gw : 7 * gw] = mm_tn(ctx_s[...], low_ref[...]).astype(BF16)
    block = 128
    for h in range(heads):
        o = h * HEAD_DIM
        e = o + HEAD_DIM

        def step(qb, carry):
            rows = pl.ds(pl.multiple_of(qb * block, block), block)
            logt = lt_ref[h : h + 1, rows]
            pw = jnp.exp(mm_nt(k_s[h, :words], qw_s[h, rows]) - logt)
            pe = jnp.exp(mm_nt(k_s[h, words:], qe_s[h, rows]) - logt)
            gw_ = mm_nt(v_s[h, :words], dc_s[h, rows])
            ge_ = mm_nt(v_s[h, words:], dc_s[h, rows])
            p_s[:words, rows] = pw.astype(BF16)
            p_s[words:, rows] = pe.astype(BF16)
            dot = jnp.sum(pw * gw_, 0, keepdims=True) + jnp.sum(pe * ge_, 0, keepdims=True)
            ds_s[:words, rows] = (pw * (gw_ - dot)).astype(BF16)
            ds_s[words:, rows] = (pe * (ge_ - dot)).astype(BF16)
            return carry

        lax.fori_loop(0, total // block, step, 0)
        dv = mm(p_s[...], dc_s[h]).astype(BF16)
        dkw = mm(ds_s[:words], qw_s[h]).astype(BF16)
        dke = mm(ds_s[words:], qe_s[h]).astype(BF16)
        dqw = (mm_tn(ds_s[:words], k_s[h, :words]) * SCALE).astype(BF16)
        dqe = (mm_tn(ds_s[words:], k_s[h, words:]) * SCALE).astype(BF16)
        dpw_s[:, o:e] = dqw[:words]
        dpw_s[:, gw + o : gw + e] = dqe[:words]
        dpw_s[:, half + o : half + e] = dkw
        dpw_s[:, half + gw + o : half + gw + e] = dv[:words]
        dpe_s[:, o:e] = dke
        dpe_s[:, gw + o : gw + e] = dv[words:]
        dpe_s[:, half + o : half + e] = dqw[words:]
        dpe_s[:, half + gw + o : half + gw + e] = dqe[words:]
    dpw = dpw_s[...]
    dpe = dpe_s[...]
    rows_w = rows_ref[:words]
    rows_e = rows_ref[words:]
    full_s[:half] = mm_tn(dpw[:, :half], rows_w).astype(BF16)
    full_s[half : 2 * half] = (mm_tn(dpw[:, half:], rows_w) + mm_tn(dpe[:, :half], rows_e)).astype(BF16)
    full_s[2 * half : 3 * half] = mm_tn(dpe[:, half:], rows_e).astype(BF16)
    sw = jnp.sum(dpw.astype(F32), 0, keepdims=True)
    se = jnp.sum(dpe.astype(F32), 0, keepdims=True)
    sum_a = jnp.concatenate([sw[:, :half], sw[:, half:] + se[:, :half]], 1)
    sum_b = jnp.concatenate([se[:, half:], jnp.zeros((1, half), F32)], 1)
    spare = w_s.shape[0] - 7 * gw
    row = lax.broadcasted_iota(jnp.int32, (spare, 2 * half), 0)
    sums = jnp.where(row == 0, sum_a, jnp.where(row == 1, sum_b, jnp.where(row == 2, up_ref[0:1], 0.0)))
    full_s[7 * gw :] = sums.astype(BF16)
    if final:
        grad = acc_ref[words:] + mm(dpe, w_s[half : 3 * half])
        ents_ref[...] = grad
        spans = spans_ref[info_ref[0]]
        begin = spans[:, 0:1]
        end = spans[:, 1:2]
        position = lax.broadcasted_iota(jnp.int32, (total - words, words), 1)
        inside = jnp.where(jnp.logical_and(position >= begin, position < end), 1.0, 0.0).astype(BF16)
        scaled = grad * (1.0 / (end - begin).astype(F32))
        high = scaled.astype(BF16)
        rest = (scaled - high.astype(F32)).astype(BF16)
        pos_s[...] = (mm_tn(inside, high) + mm_tn(inside, rest)).astype(BF16)
        sources = [(full_s, size), (pos_s, words // 8)]
        writes = start(blocks_out(sources, info_ref, send_ref, near_ref, pass_ref), sem.at[3])
        words_ref[...] = acc_ref[:words] + mm(dpw, w_s[: 2 * half])
    else:
        writes = start(blocks_out([(full_s, size)], info_ref, send_ref, near_ref, pass_ref), sem.at[3])
        out_ref[:words] = acc_ref[:words] + mm(dpw, w_s[: 2 * half])
        out_ref[words:] = acc_ref[words:] + mm(dpe, w_s[half : 3 * half])
    wait(writes)


def attend_back(info, rows_low, saved, low, up_sums, acc, pieces, words, heads, rows, spans=None):
    total, width = rows_low.shape
    pw, pe, ctx, lt = saved
    ents = total - words
    gw = heads * HEAD_DIM
    count = len(pieces)
    final = spans is not None
    moved = rows + words if final else rows
    grads = (shape((words, width), F32), shape((ents, width), F32)) if final else (shape((total, width), F32),)
    return pl.pallas_call(
        partial(attend_back_kernel, words, gw, heads, final, count),
        in_specs=[SMEM] + [VMEM] * 5 + [HBM] * (3 + count) + [VMEM] * final,
        out_specs=[HBM] * 3 + [VMEM] * len(grads),
        out_shape=(
            far_shape((moved // 2, width), BF16),
            far_shape((moved // 4, width), BF16),
            far_shape((moved // 4, width), BF16),
        )
        + grads,
        scratch_shapes=[pltpu.VMEM((words, width), BF16)] * final
        + [
            pltpu.VMEM((rows, width), BF16),
            pltpu.VMEM((words, 4 * gw), BF16),
            pltpu.VMEM((ents, 4 * gw), BF16),
            pltpu.VMEM((total, gw), BF16),
        ]
        + [pltpu.VMEM((heads, total, HEAD_DIM), BF16) for _ in range(5)]
        + [
            pltpu.VMEM((total, total), BF16),
            pltpu.VMEM((total, total), BF16),
            pltpu.VMEM((words, 4 * gw), BF16),
            pltpu.VMEM((ents, 4 * gw), BF16),
            pltpu.VMEM((rows, width), BF16),
            DMA((4,)),
        ],
        input_output_aliases={} if final else {5: 3},
        compiler_params=params(20),
        cost_estimate=cost(11, 8),
        name="attend_back",
    )(info, rows_low, lt, low, up_sums, acc, *far((pw, pe, ctx)), *far(pieces), *((spans,) if final else ()))


def spread_query_kernel(info_ref, *refs):
    pieces = refs[:8]
    query_ref, key_ref, value_ref, out_ref, qb_ref, vb_ref, ub_ref, s, sem = refs[8:]
    wait(start(place(pieces, info_ref, s.shape[0] // 8, (s,)), sem))
    gw = key_ref.shape[0]
    for i, k in ((0, 0), (1, 1), (2, 4), (3, 5)):
        query_ref[i] = s[k * gw : (k + 1) * gw].astype(F32)
    key_ref[...] = s[2 * gw : 3 * gw].astype(F32)
    value_ref[...] = s[3 * gw : 4 * gw].astype(F32)
    out_ref[...] = s[6 * gw : 7 * gw].astype(F32)
    rows = s[7 * gw : 7 * gw + TILE].astype(F32)
    qb_ref[0:1] = rows[0:1, :gw]
    qb_ref[1:2] = rows[0:1, gw : 2 * gw]
    qb_ref[2:3] = rows[1:2, :gw]
    qb_ref[3:4] = rows[1:2, gw : 2 * gw]
    vb_ref[...] = rows[0:1, 3 * gw :]
    ub_ref[...] = rows[2:3]


def spread_query(info, pieces, gw):
    unit, width = pieces[0].shape
    flat = shape((gw, width), F32)
    return pl.pallas_call(
        spread_query_kernel,
        in_specs=[SMEM] + [HBM] * 8,
        out_specs=[VMEM] * 7,
        out_shape=(
            shape((4, gw, width), F32), flat, flat, flat,
            shape((4, gw), F32), shape((1, gw), F32), shape((1, width), F32),
        ),
        scratch_shapes=[pltpu.VMEM((8 * unit, width), BF16), DMA],
        compiler_params=params(8),
        cost_estimate=cost(0.5, 7),
        name="spread_query",
    )(info, *far(pieces))


def spread_hidden_kernel(info_ref, *refs):
    pieces = refs[:8]
    up_ref, down_ref, up_s, down_s, sem = refs[8:]
    wait(start(place(pieces, info_ref, up_ref.shape[0] // 8, (up_s, down_s)), sem))
    up_ref[...] = up_s[...].astype(F32)
    down_ref[...] = down_s[...].astype(F32)


def spread_hidden(info, pieces):
    rows, width = pieces[0].shape
    out = shape((4 * rows, width), F32)
    return pl.pallas_call(
        spread_hidden_kernel,
        in_specs=[SMEM] + [HBM] * 8,
        out_specs=[VMEM] * 2,
        out_shape=(out, out),
        scratch_shapes=[pltpu.VMEM((4 * rows, width), BF16)] * 2 + [DMA],
        compiler_params=params(9),
        cost_estimate=cost(0.5, 7),
        name="spread_hidden",
    )(info, *far(pieces))


def spread_pos_kernel(info_ref, *refs):
    pieces = refs[:8]
    pos_ref, s, sem = refs[8:]
    wait(start(place(pieces, info_ref, s.shape[0] // 8, (s,)), sem))
    pos_ref[...] = s[...].astype(F32)


def spread_pos(info, pieces):
    rows, width = pieces[0].shape
    return pl.pallas_call(
        spread_pos_kernel,
        in_specs=[SMEM] + [HBM] * 8,
        out_specs=VMEM,
        out_shape=shape((8 * rows, width), F32),
        scratch_shapes=[pltpu.VMEM((8 * rows, width), BF16), DMA],
        compiler_params=params(4),
        cost_estimate=cost(0.5, 3),
        name="spread_pos",
    )(info, *far(pieces))


class Links:
    def __init__(self):
        self.dp = lax.axis_size("dp")
        self.ring = lax.axis_size("tensor")
        dp_index = lax.axis_index("dp")
        self.z = lax.axis_index("tensor")
        self.core = dp_index % 2
        self.bits = (self.dp // 2).bit_length() - 1
        self.bit = [(dp_index // (2 << k)) % 2 for k in range(self.bits)]

    def shift_z(self, v, by):
        n = self.ring
        return lax.ppermute(v, "tensor", [(i, (i + by) % n) for i in range(n)])

    def swap_z(self, v, mask):
        return lax.ppermute(v, "tensor", [(i, i ^ mask) for i in range(self.ring)])

    def swap(self, v, code):
        return lax.ppermute(v, "dp", [(i, i ^ code) for i in range(self.dp)])

    def swap_core(self, v):
        return self.swap(v, 1)

    def first(self, v):
        return lax.ppermute(v, "dp", [(i, i ^ (4 if i % 2 else 2)) for i in range(self.dp)])

    def second(self, v):
        return lax.ppermute(v, "dp", [(i, i ^ (2 if i % 2 else 4)) for i in range(self.dp)])


def after(value, *others):
    return lax.optimization_barrier((value,) + others)[0]


def sync(*values):
    return lax.optimization_barrier(values)


def add_low(*parts):
    total = parts[0].astype(F32)
    for part in parts[1:]:
        total = total + part.astype(F32)
    return total.astype(BF16)


class Blocks:
    def __init__(self, links, send, near, far):
        self.links, self.send, self.near, self.far = links, send, near, far
        self.unit = near.shape[0] // 2

    def one(self):
        return add_low(self.far, self.got[2 * self.unit :])

    def two(self):
        u = self.unit
        return add_low(self.near[u:], self.got[u : 2 * u], self.a[u:])

    def rest(self, low, high, *more):
        value = add_low(self.near[low:high], self.got[low:high], self.a[low:high], self.b[low:high], *more)
        for j in range(2, self.links.bits):
            value = add_low(value, self.links.swap(value, 2 << j))
        return value


def shards(
    word_in,
    entity_in,
    entity_spans,
    word_mask,
    entity_mask,
    pos_table,
    query_w,
    query_b,
    key_w,
    value_w,
    value_b,
    out_w,
    out_b,
    norm1_gain,
    norm1_bias,
    up_w,
    up_b,
    down_w,
    down_b,
    norm2_gain,
    norm2_bias,
    cot_words,
    cot_entities,
):
    links = Links()
    n = links.ring
    z = links.z
    words = cot_words.shape[0]
    ents = cot_entities.shape[0]
    width = word_in.shape[1]
    gw = key_w.shape[1]
    heads = gw // HEAD_DIM
    rows = -(-(7 * gw + 3) // (8 * TILE)) * 8 * TILE
    part = 4 * links.core + 2 * links.bit[0] + links.bit[1]
    info = jnp.stack([z, links.core, part, 2 - links.core]).astype(jnp.int32)

    small = (query_b, value_b[None], up_b[None])
    own = (jnp.swapaxes(query_w, 1, 2), key_w.T, value_w.T, out_w)
    piece_q, piece_f = pack(info, small, own, up_w, down_w, rows)
    first, second, core, shift = links.first, links.second, links.swap_core, links.shift_z
    rows_low, acc = start_rows(info, word_in, entity_in, entity_spans, pos_table, out_b[None], words, ents)
    saved = [None] * n
    biases = [None] * n

    def attend_one(r, acc, pieces, small=()):
        pw, pe, ctx, lt, biases[r], acc = attend(info, rows_low, acc, pieces, words, heads, rows, small)
        saved[r] = (pw, pe, ctx, lt)
        return acc

    v1, v3 = shift(piece_q, 1), shift(piece_q, 3)
    acc = attend_one(0, acc, own, small)
    acc, v1, v3, piece_f = sync(acc, v1, v3, piece_f)
    a1, b1, v2, f1, f3 = first(v1), second(v1), shift(v1, 1), shift(piece_f, 1), shift(piece_f, 3)
    acc, v1, a1, b1, v3 = sync(acc, v1, a1, b1, v3)
    c1, kv, ka, kb, a3, b3 = second(a1), core(v1), core(a1), core(b1), first(v3), second(v3)
    acc, c1, kv, ka, kb, v2, f1, f3, v3 = sync(acc, c1, kv, ka, kb, v2, f1, f3, v3)
    kc, f2 = core(c1), shift(f1, 1)
    acc, kc, a3, b3, v2, f3 = sync(acc, kc, a3, b3, v2, f3)
    group_1 = (v1, a1, b1, c1, kv, ka, kb, kc)

    c3, a2, b2, ag, bg = second(a3), first(v2), second(v2), first(f3), second(f3)
    acc = attend_one(1, acc, group_1)
    acc, c3, a2, b2, ag, bg, f1, f2 = sync(acc, c3, a2, b2, ag, bg, f1, f2)
    kv, ka, kb, kc = core(v3), core(a3), core(b3), core(c3)
    far_f = jnp.concatenate([f1, f2], 0)
    acc, kv, ka, kb, kc, far_f, a2, ag, v2 = sync(acc, kv, ka, kb, kc, far_f, a2, ag, v2)
    group_3 = (v3, a3, b3, c3, kv, ka, kb, kc)

    c2, cg, af, kv, ka = second(a2), second(ag), first(far_f), core(v2), core(a2)
    acc = attend_one(3, acc, group_3)
    acc, c2, cg, af, kv, ka, b2, far_f = sync(acc, c2, cg, af, kv, ka, b2, far_f)
    kb, kc = core(b2), core(c2)
    acc, kb, kc, far_f, af, f3, ag, bg = sync(acc, kb, kc, far_f, af, f3, ag, bg)
    group_2 = (v2, a2, b2, c2, kv, ka, kb, kc)

    bf, cf, kv_g, ka_g, kb_g = second(far_f), second(af), core(f3), core(ag), core(bg)
    acc = attend_one(2, acc, group_2)
    acc, bf, cf, kv_g, ka_g, kb_g, cg, af, far_f = sync(acc, bf, cf, kv_g, ka_g, kb_g, cg, af, far_f)
    attended = acc
    ffn_pieces = (
        far_f, af, bf, cf, core(far_f), core(af), core(bf), core(cf), f3, ag, bg, cg, kv_g, ka_g, kb_g, core(cg)
    )
    query_groups = (own, group_1, group_2, group_3)

    vec = jnp.stack([norm1_gain, norm1_bias, down_b, norm2_gain, norm2_bias] + [down_b] * 3)
    normed_t, act_t, slope, up, down, out_words, out_ents, mixed_low, acc, sums = hidden(
        info, attended, vec, word_mask, entity_mask, cot_words, cot_entities, biases, (up_w, down_w), ffn_pieces
    )

    size = width // 4
    unit = rows // 8
    up_sums = [None] * n

    def ffn_blocks(group, acc):
        send, near, rest, acc, up_sum = hidden_back(info, group, mixed_low, act_t, slope, normed_t, up, down, acc)
        for k, r in enumerate(group):
            up_sums[r] = up_sum[8 * k : 8 * k + 8]
        return Blocks(links, send, near, rest), acc

    def back(r, acc, spans=None):
        send, near, rest, *acc = attend_back(
            info, rows_low, saved[r], attended_low, up_sums[r], acc, query_groups[r], words, heads, rows, spans
        )
        return Blocks(links, send, near, rest), *acc

    fa, acc = ffn_blocks((2, 1), acc)
    fa.got = core(fa.send)
    fb, acc = ffn_blocks((3,), acc)
    acc, fa.got = sync(acc, fa.got)
    acc, one_a = sync(acc, fa.one())

    fa.a, fb.got = first(one_a), core(fb.send)
    fc, acc = ffn_blocks((0,), acc)
    acc, fb.got = sync(acc, fb.got)
    one_b = fb.one()
    acc, attended_low, sums = norm_back(attended, acc, vec, sums)
    more = core(sums)
    acc, one_b, sums, more = sync(acc, one_b, sums, more)
    sums = sums + more

    fb.a, fc.got, more = first(one_b), core(fc.send), links.swap(sums, 2)
    q1, acc = back(2, acc)
    acc, fa.a, fb.a, fc.got, more = sync(acc, fa.a, fb.a, fc.got, more)
    acc, two_a, two_b, one_c, sums = sync(acc, fa.two(), fb.two(), fc.one(), sums + more)

    fa.b, fb.b, fc.a, q1.got = second(two_a), second(two_b), first(one_c), core(q1.send)
    q2, acc = back(1, acc)
    acc, fa.b, fb.b, fc.a, q1.got = sync(acc, fa.b, fb.b, fc.a, q1.got)
    q2.got = core(q2.send)
    acc, r2, r1, r3, two_c, one_1, q2.got = sync(
        acc, fa.rest(0, size), fa.rest(size, 2 * size), fb.rest(0, size), fc.two(), q1.one(), q2.got
    )

    z2, z1, z3, q1.a, fc.b = shift(r2, -2), shift(r1, -1), shift(r3, -3), first(one_1), second(two_c)
    q3, acc = back(3, acc)
    acc, z2, z1, z3, q1.a, fc.b = sync(acc, z2, z1, z3, q1.a, fc.b)
    acc, own_f, two_1, one_2 = sync(acc, fc.rest(0, size, z1, z2, z3), q1.two(), q2.one())

    ga, gb, q1.b, q2.a, q3.got = first(own_f), second(own_f), second(two_1), first(one_2), core(q3.send)
    q4, grad_words, grad_ents = back(0, acc, entity_spans)
    q4.send, ga, gb, q1.b, q2.a, q3.got, sums = sync(q4.send, ga, gb, q1.b, q2.a, q3.got, sums)

    y1, q2.b, q3.a = shift(q1.rest(0, unit), -2), second(q2.two()), first(q3.one())
    q4.got = core(q4.send)
    q4.a = first(q4.one())
    q4.a, q2.b, q3.a, y1, ga, sums = sync(q4.a, q2.b, q3.a, y1, ga, sums)

    q4.b, q3.b, y2, gc, more = (
        second(q4.two()), second(q3.two()), shift(q2.rest(0, unit), -1), second(ga), links.swap(sums, 4)
    )
    q4.b, q3.b, y2, gc, more, own_f, ga, gb = sync(q4.b, q3.b, y2, gc, more, own_f, ga, gb)
    sums = sums + more
    for j in range(2, links.bits):
        sums = sums + links.swap(sums, 2 << j)

    pos = q4.rest(unit, unit + words // 8)
    p1, p2, p3 = (links.swap_z(pos, mask) for mask in (1, 2, 3))
    y3 = shift(q3.rest(0, unit), -3)
    near_f = (own_f, ga, gb, gc)
    far_f = tuple(core(v) for v in near_f)
    p1, p2, p3, y3, pos, sums, *far_f = sync(p1, p2, p3, y3, pos, sums, *far_f)

    pos = ((pos.astype(F32) + p1.astype(F32)) + (p2.astype(F32) + p3.astype(F32))).astype(BF16)
    own_q = q4.rest(0, unit, y1, y2, y3)
    pa, pb, qa, qb, more = first(pos), second(pos), first(own_q), second(own_q), links.swap_z(sums, 1)
    grad_up, grad_down = spread_hidden(info, near_f + tuple(far_f))
    qa, qb, pa, pb, more, own_q, pos, grad_up, grad_down = sync(qa, qb, pa, pb, more, own_q, pos, grad_up, grad_down)

    sums = sums + more
    more = links.swap_z(sums, 2)
    near_q = (own_q, qa, qb, second(qa))
    near_p = (pos, pa, pb, second(pa))
    far_q = tuple(core(v) for v in near_q)
    far_p = tuple(core(v) for v in near_p)
    total_sums = sums + more
    pos_sum = spread_pos(info, near_p + far_p)
    grad_query_t, grad_key_t, grad_value_t, grad_out, grad_query_b, grad_value_b, grad_up_b = spread_query(
        info, near_q + far_q, gw
    )
    return (
        out_words,
        out_ents,
        grad_words,
        grad_ents,
        pos_sum,
        jnp.swapaxes(grad_query_t, 1, 2),
        grad_query_b,
        grad_key_t.T,
        grad_value_t.T,
        grad_value_b[0],
        grad_out,
        total_sums[5],
        total_sums[3],
        total_sums[4],
        grad_up,
        grad_up_b[0],
        grad_down,
        total_sums[2],
        total_sums[0],
        total_sums[1],
    )


def solution(mesh):
    rows = P(("dp", "tensor"), None)
    last = P(None, "tensor")
    placed = (
        P("dp", None),
        P("dp", None),
        P("dp", None, None),
        P("dp", None),
        P("dp", None),
        P(),
        P(None, None, "tensor"),
        last,
        last,
        last,
        P("tensor"),
        P("tensor", None),
        P(),
        P(),
        P(),
        last,
        P("tensor"),
        P("tensor", None),
        P(),
        P(),
        P(),
        rows,
        rows,
    )
    return jax.shard_map(
        shards,
        mesh=mesh,
        in_specs=placed,
        out_specs=(
            rows,
            rows,
            rows,
            rows,
            P(),
            P(None, None, "tensor"),
            last,
            last,
            last,
            P("tensor"),
            P("tensor", None),
            P(),
            P(),
            P(),
            last,
            P("tensor"),
            P("tensor", None),
            P(),
            P(),
            P(),
        ),
        check_vma=False,
    )
```

```python
from functools import partial

import jax
import jax.numpy as jnp
from jax import lax
from jax.experimental import pallas as pl
from jax.experimental.pallas import tpu as pltpu
from jax.sharding import PartitionSpec as P

HEAD_DIM = 64
SCALE = HEAD_DIM**-0.5
norm_epsilon = 1e-12
F32 = jnp.float32
BF16 = jnp.bfloat16
NT = (((1,), (1,)), ((), ()))
TN = (((0,), (0,)), ((), ()))
ERFC_STEP = 0.35
ERFC_POLY = (
    0.1396196249207051,
    0.13989555693599826,
    0.11957015144655456,
    0.10661400019997494,
    -0.025870835326937874,
    0.16337919550284652,
    -0.25954764983005574,
    0.14589250699009862,
    -0.029552569422939476,
)
TILE = 16
VMEM = pl.BlockSpec(memory_space=pltpu.VMEM)
SMEM = pl.BlockSpec(memory_space=pltpu.SMEM)
HBM = pl.BlockSpec(memory_space=pltpu.HBM)
DMA = pltpu.SemaphoreType.DMA


def mm(a, b):
    return jnp.dot(a, b, preferred_element_type=F32)


def mm_nt(a, b):
    return lax.dot_general(a, b, NT, preferred_element_type=F32)


def mm_tn(a, b):
    return lax.dot_general(a, b, TN, preferred_element_type=F32)


def params(mib):
    return pltpu.CompilerParams(vmem_limit_bytes=mib << 20)


def cost(gflop, mbytes):
    return pl.CostEstimate(
        flops=int(gflop * 1e9), bytes_accessed=int(mbytes * 1e6), transcendentals=0
    )


def shape(dims, kind):
    return jax.ShapeDtypeStruct(dims, kind)


def far(values):
    return tuple(pltpu.with_memory_space_constraint(v, pltpu.HBM) for v in values)


def far_shape(dims, kind):
    return pltpu.HBM(dims, kind)


def start(pairs, sem):
    copies = [pltpu.make_async_copy(source, target, sem) for source, target in pairs]
    for copy in copies:
        copy.start()
    return copies


def wait(copies):
    for copy in copies:
        copy.wait()


def rows_at(first, size):
    return pl.ds(pl.multiple_of(first, TILE), size)


def place(pieces, info_ref, unit, targets, skip=0):
    part, first = info_ref[2], info_ref[3]
    second = 3 - first
    pairs = []
    for piece, code in zip(pieces, (0, first, second, 3, 4, 4 + second, 4 + first, 7)):
        row = lax.bitwise_xor(part, jnp.int32(code)) * unit
        for t, target in enumerate(targets):
            pairs.append((piece.at[pl.ds(skip + t * unit, unit)], target.at[rows_at(row, unit)]))
    return pairs


def blocks_out(sources, info_ref, send_ref, near_ref, pass_ref):
    part, first = info_ref[2], info_ref[3]
    second = 3 - first
    keep = (0, second, first, 3)
    send = (4, 4 + first, 4 + second, 7)
    total = sum(unit for _, unit in sources)
    pairs = []
    for i in range(4):
        done = 0
        for source, unit in sources:
            other = lax.bitwise_xor(part, jnp.int32(send[i])) * unit
            mine = lax.bitwise_xor(part, jnp.int32(keep[i])) * unit
            to = near_ref if i < 2 else pass_ref
            pairs.append((source.at[rows_at(other, unit)], send_ref.at[pl.ds(i * total + done, unit)]))
            pairs.append((source.at[rows_at(mine, unit)], to.at[pl.ds((i % 2) * total + done, unit)]))
            done += unit
    return pairs


def own_parts(query_ref, key_ref, value_ref, out_ref):
    return (query_ref.at[0], query_ref.at[1], key_ref, value_ref, query_ref.at[2], query_ref.at[3], out_ref)


def spare_rows(qb_ref, vb_ref, ub_ref, spare):
    qb = qb_ref[...].astype(F32)
    none = jnp.zeros((1, qb.shape[1]), F32)
    first = jnp.concatenate([qb[0:1], qb[1:2], none, vb_ref[...].astype(F32)], 1)
    second = jnp.concatenate([qb[2:3], qb[3:4], none, none], 1)
    row = lax.broadcasted_iota(jnp.int32, (spare, first.shape[1]), 0)
    rows = jnp.where(row == 0, first, jnp.where(row == 1, second, jnp.where(row == 2, ub_ref[...].astype(F32), 0.0)))
    return rows.astype(BF16)


def pack_kernel(
    gw, info_ref, qb_ref, vb_ref, ub_ref, query_ref, key_ref, value_ref, ow_ref, up_ref, down_ref,
    piece_ref, ffn_ref, w_s, f_s, sem,
):
    part = info_ref[2]
    size = piece_ref.shape[0]
    low = lax.div(part * size, jnp.int32(gw))
    copies = []
    for i, ref in enumerate(own_parts(query_ref, key_ref, value_ref, ow_ref)):
        needed = jnp.logical_or(low == i, low + 1 == i)
        copies.append((needed, pltpu.make_async_copy(ref, w_s.at[pl.ds(i * gw, gw)], sem.at[0])))
    for needed, copy in copies:
        pl.when(needed)(copy.start)
    unit = f_s.shape[0] // 2
    ffn = start(
        [(v.at[rows_at(part * unit, unit)], f_s.at[pl.ds(i * unit, unit)]) for i, v in enumerate((up_ref, down_ref))],
        sem.at[1],
    )
    w_s[7 * gw :] = spare_rows(qb_ref, vb_ref, ub_ref, w_s.shape[0] - 7 * gw)
    for needed, copy in copies:
        pl.when(needed)(copy.wait)
    piece = start([(w_s.at[rows_at(part * size, size)], piece_ref)], sem.at[2])
    wait(ffn)
    last = start([(f_s, ffn_ref)], sem.at[3])
    wait(piece)
    wait(last)


def pack(info, biases, own, up_w, down_w, rows):
    gw, width = own[1].shape
    unit = up_w.shape[0] // 8
    return pl.pallas_call(
        partial(pack_kernel, gw),
        in_specs=[SMEM] + [VMEM] * 3 + [HBM] * 6,
        out_specs=[HBM] * 2,
        out_shape=(far_shape((rows // 8, width), BF16), far_shape((2 * unit, width), BF16)),
        scratch_shapes=[pltpu.VMEM((rows, width), BF16), pltpu.VMEM((2 * unit, width), BF16), DMA((4,))],
        compiler_params=params(4),
        cost_estimate=cost(0.01, 3),
        name="pack",
    )(info, *biases, *far(own + (up_w, down_w)))


def start_kernel(info_ref, words_ref, ents_ref, spans_ref, table_ref, bias_ref, low_ref, resid_ref, w_s, e_s, t_s, sem):
    words, count = w_s.shape[0], e_s.shape[0]
    z = info_ref[0]
    ents = start(
        [(ents_ref.at[rows_at(z * count, count)], e_s), (table_ref, t_s)],
        sem.at[0],
    )
    reads = start([(words_ref.at[rows_at(z * words, words)], w_s)], sem.at[1])
    spans = spans_ref[z]
    begin = spans[:, 0:1]
    end = spans[:, 1:2]
    position = lax.broadcasted_iota(jnp.int32, (count, words), 1)
    inside = jnp.where(jnp.logical_and(position >= begin, position < end), 1.0, 0.0).astype(BF16)
    share = 1.0 / (end - begin).astype(F32)
    out_b = bias_ref[...].astype(F32)
    wait(ents)
    rows = e_s[...].astype(F32) + mm(inside, t_s[...]) * share
    low_ref[words:] = rows.astype(BF16)
    resid_ref[words:] = rows + out_b
    wait(reads)
    low_ref[:words] = w_s[...]
    resid_ref[:words] = w_s[...].astype(F32) + out_b


def start_rows(info, word_in, entity_in, spans, table, out_b, words, ents):
    width = word_in.shape[1]
    total = words + ents
    return pl.pallas_call(
        start_kernel,
        in_specs=[SMEM, HBM, HBM, VMEM, HBM, VMEM],
        out_specs=[VMEM] * 2,
        out_shape=(shape((total, width), BF16), shape((total, width), F32)),
        scratch_shapes=[
            pltpu.VMEM((words, width), BF16),
            pltpu.VMEM((ents, width), BF16),
            pltpu.VMEM(table.shape, BF16),
            DMA((2,)),
        ],
        compiler_params=params(6),
        cost_estimate=cost(0.5, 6),
        name="start_rows",
    )(info, *far((word_in, entity_in)), spans, *far((table,)), out_b)


def split_heads(words, gw, heads, pw_ref, pe_ref, qw_s, qe_s, k_s, v_s):
    half = 2 * gw
    for h in range(heads):
        o = h * HEAD_DIM
        e = o + HEAD_DIM
        qw_s[h, :words] = pw_ref[:, o:e] * SCALE
        qw_s[h, words:] = pe_ref[:, half + o : half + e] * SCALE
        qe_s[h, :words] = pw_ref[:, gw + o : gw + e] * SCALE
        qe_s[h, words:] = pe_ref[:, half + gw + o : half + gw + e] * SCALE
        k_s[h, :words] = pw_ref[:, half + o : half + e]
        k_s[h, words:] = pe_ref[:, o:e]
        v_s[h, :words] = pw_ref[:, half + gw + o : half + gw + e]
        v_s[h, words:] = pe_ref[:, gw + o : gw + e]


def attend_kernel(words, gw, heads, count, info_ref, rows_ref, acc_ref, *refs):
    own = count == 4
    small, refs = (refs[:3], refs[3:]) if own else ((), refs)
    pieces = refs[:count]
    pw_ref, pe_ref, ctx_ref, lt_ref, bias_ref, out_ref, w_s, pw_s, pe_s, ctx_s, qw_s, qe_s, k_s, v_s, sem = refs[count:]
    half = 2 * gw
    if own:
        reads = start([(v, w_s.at[pl.ds(i * gw, gw)]) for i, v in enumerate(own_parts(*pieces))], sem.at[0])
        w_s[7 * gw :] = spare_rows(*small, w_s.shape[0] - 7 * gw)
        wait(reads)
    else:
        wait(start(place(pieces, info_ref, w_s.shape[0] // 8, (w_s,)), sem.at[0]))
    rows_b = w_s[7 * gw : 7 * gw + TILE]
    bias_ref[...] = rows_b
    rows_b = rows_b.astype(F32)
    bias_e = jnp.concatenate([rows_b[0:1, half:], rows_b[1:2, :half]], 1)
    pw_s[...] = (mm_nt(rows_ref[:words], w_s[: 4 * gw]) + rows_b[0:1]).astype(BF16)
    pe_s[...] = (mm_nt(rows_ref[words:], w_s[half : 6 * gw]) + bias_e).astype(BF16)
    saves = start([(pw_s, pw_ref), (pe_s, pe_ref)], sem.at[1])
    split_heads(words, gw, heads, pw_s, pe_s, qw_s, qe_s, k_s, v_s)
    block = 128

    def step(qb, carry):
        rows = pl.ds(pl.multiple_of(qb * block, block), block)
        parts = []
        for h in range(heads):
            sw = mm_nt(qw_s[h, rows], k_s[h, :words])
            se = mm_nt(qe_s[h, rows], k_s[h, words:])
            top = jnp.maximum(jnp.max(sw, 1, keepdims=True), jnp.max(se, 1, keepdims=True))
            ew = jnp.exp(sw - top)
            ee = jnp.exp(se - top)
            total = jnp.sum(ew, 1, keepdims=True) + jnp.sum(ee, 1, keepdims=True)
            parts.append(
                (mm(ew.astype(BF16), v_s[h, :words]) + mm(ee.astype(BF16), v_s[h, words:])) * (1.0 / total)
            )
            logt = top + jnp.log(total)
            lt_ref[h : h + 1, rows] = jnp.broadcast_to(logt, (block, block)).T[0:1]
        ctx_s[rows, :] = jnp.concatenate(parts, 1).astype(BF16)
        return carry

    lax.fori_loop(0, rows_ref.shape[0] // block, step, 0, unroll=True)
    last = start([(ctx_s, ctx_ref)], sem.at[2])
    out_ref[...] = acc_ref[...] + mm(ctx_s[...], w_s[6 * gw : 7 * gw])
    wait(saves)
    wait(last)


def attend(info, rows_low, acc, pieces, words, heads, rows, small=()):
    total, width = rows_low.shape
    ents = total - words
    gw = heads * HEAD_DIM
    count = len(pieces)
    return pl.pallas_call(
        partial(attend_kernel, words, gw, heads, count),
        in_specs=[SMEM] + [VMEM] * (2 + len(small)) + [HBM] * count,
        out_specs=[HBM] * 3 + [VMEM] * 3,
        out_shape=(
            far_shape((words, 4 * gw), BF16),
            far_shape((ents, 4 * gw), BF16),
            far_shape((total, gw), BF16),
            shape((8, total), F32),
            shape((TILE, width), BF16),
            shape((total, width), F32),
        ),
        scratch_shapes=[
            pltpu.VMEM((rows, width), BF16),
            pltpu.VMEM((words, 4 * gw), BF16),
            pltpu.VMEM((ents, 4 * gw), BF16),
            pltpu.VMEM((total, gw), BF16),
        ]
        + [pltpu.VMEM((heads, total, HEAD_DIM), BF16) for _ in range(4)]
        + [DMA((3,))],
        input_output_aliases={2: 5},
        compiler_params=params(16),
        cost_estimate=cost(8, 6),
        name="attend_own" if small else "attend_far",
    )(info, rows_low, acc, *small, *far(pieces))


def gelu_pair(x):
    size = jnp.abs(x)
    t = 1.0 / (1.0 + ERFC_STEP * size)
    poly = jnp.full_like(x, ERFC_POLY[-1])
    for c in ERFC_POLY[-2::-1]:
        poly = poly * t + c
    bell = jnp.exp(x * x * -0.5)
    tail = poly * t * bell
    below = jnp.where(x >= 0, 1.0 - tail, tail)
    return x * below, below + x * (bell * 0.3989422804014327)


def norm_parts(values):
    centered = values - jnp.mean(values, 1, keepdims=True)
    inv = lax.rsqrt(jnp.mean(centered * centered, 1, keepdims=True) + norm_epsilon)
    return centered * inv, inv


def hidden_kernel(n, info_ref, attended_ref, vec_ref, wm_ref, em_ref, cw_ref, ce_ref, *refs):
    bias_refs, refs = refs[:n], refs[n:]
    up_own, down_own = refs[:2]
    pieces, refs = (refs[2:10], refs[10:18]), refs[18:]
    turn_ref, at_ref, slope_ref, up_s, down_s, ow_ref, oe_ref, mixed_ref, grad_ref, sums_ref, low_ref, acc_s, b_s, sem = refs
    total, width = attended_ref.shape
    unit = width // 8
    reads = [start([(up_own, up_s.at[0]), (down_own, down_s.at[0])], sem.at[0])]
    for r in range(1, n):
        held, skip = pieces[r // 3], 2 * unit * ((r - 1) % 2)
        reads.append(start(place(held, info_ref, unit, (up_s.at[r], down_s.at[r]), skip), sem.at[r]))
    for r in range(n):
        b_s[r] = bias_refs[r][2:3].astype(F32)
    scaled, _ = norm_parts(attended_ref[...])
    normed = scaled * vec_ref[0:1].astype(F32) + vec_ref[1:2].astype(F32)
    low = normed.astype(BF16)
    low_ref[...] = low
    turn_ref[...] = low.T
    acc_s[...] = normed + vec_ref[2:3].astype(F32)
    block = 128

    def group(r):
        for lo in range(0, total, block):
            pre = mm(low_ref[lo : lo + block], up_s[r]) + b_s[r]
            value, slope = gelu_pair(pre)
            slope_ref[r, lo : lo + block] = slope
            value = value.astype(BF16)
            at_ref[r, :, lo : lo + block] = value.T
            acc_s[lo : lo + block] += mm(value, down_s[r])

    for r in range(n):
        wait(reads[r])
        group(r)

    words = cw_ref.shape[0]
    z = info_ref[0]
    scaled, inv = norm_parts(acc_s[...])
    gain = vec_ref[3:4].astype(F32)
    output = scaled * gain + vec_ref[4:5].astype(F32)
    ow_ref[...] = output[:words].astype(BF16)
    oe_ref[...] = output[words:].astype(BF16)

    def column(ref, size):
        return jnp.broadcast_to(ref[pl.ds(z, 1), :].astype(F32), (128, size)).T[:, 0:1]

    cot = jnp.concatenate(
        [
            column(wm_ref, words) * cw_ref[...].astype(F32),
            column(em_ref, total - words) * ce_ref[...].astype(F32),
        ],
        0,
    )
    grad, grad_gain, grad_shift = norm_backward(cot, scaled, inv, gain)
    grad_ref[...] = grad
    mixed_ref[...] = grad.astype(BF16)
    sums_ref[0:1] = grad_gain
    sums_ref[1:2] = grad_shift
    sums_ref[2:3] = jnp.sum(grad, 0, keepdims=True)
    sums_ref[3:] = jnp.zeros((5, width), F32)


def hidden(info, attended, vec, word_mask, entity_mask, cot_words, cot_ents, biases, own, pieces):
    total, width = attended.shape
    n = len(biases)
    return pl.pallas_call(
        partial(hidden_kernel, n),
        in_specs=[SMEM] + [VMEM] * (6 + n) + [HBM] * (2 + len(pieces)),
        out_specs=[VMEM] * 10,
        out_shape=(
            shape((width, total), BF16),
            shape((n, width, total), BF16),
            shape((n, total, width), F32),
            shape((n, width, width), BF16),
            shape((n, width, width), BF16),
            shape(cot_words.shape, BF16),
            shape(cot_ents.shape, BF16),
            shape((total, width), BF16),
            shape((total, width), F32),
            shape((8, width), F32),
        ),
        scratch_shapes=[
            pltpu.VMEM((total, width), BF16),
            pltpu.VMEM((total, width), F32),
            pltpu.VMEM((n, 1, width), F32),
            DMA((n,)),
        ],
        compiler_params=params(18),
        cost_estimate=cost(22, 20),
        name="hidden",
    )(info, attended, vec, word_mask, entity_mask, cot_words, cot_ents, *biases, *far(own), *far(pieces))


def norm_backward(grad_in, scaled, inv_std, gain_row):
    grad_gain = jnp.sum(grad_in * scaled, axis=0, keepdims=True)
    grad_shift = jnp.sum(grad_in, axis=0, keepdims=True)
    grad_scaled = grad_in * gain_row
    mean_first = jnp.mean(grad_scaled, axis=1, keepdims=True)
    mean_second = jnp.mean(grad_scaled * scaled, axis=1, keepdims=True)
    return inv_std * (grad_scaled - mean_first - scaled * mean_second), grad_gain, grad_shift


def hidden_back_kernel(
    pair, info_ref, low_ref, at_ref, slope_ref, turn_ref, up_ref, down_ref, acc_ref,
    send_ref, near_ref, pass_ref, out_ref, b_ref, *refs,
):
    full, sem = refs[:-1], refs[-1]
    unit = turn_ref.shape[0] // 8
    low = low_ref[...]
    out_ref[...] = acc_ref[...]
    for k, r in enumerate(pair):
        grad_down = mm(at_ref[r], low).astype(BF16)
        for i in range(8):
            full[k][(2 * i + 1) * unit : (2 * i + 2) * unit] = grad_down[i * unit : (i + 1) * unit]
        pre_low = (mm_nt(low, down_ref[r]) * slope_ref[r]).astype(BF16)
        grad_up = mm(turn_ref[...], pre_low).astype(BF16)
        for i in range(8):
            full[k][2 * i * unit : (2 * i + 1) * unit] = grad_up[i * unit : (i + 1) * unit]
        b_ref[8 * k : 8 * k + 8] = jnp.broadcast_to(jnp.sum(pre_low.astype(F32), 0, keepdims=True), (8, b_ref.shape[1]))
        out_ref[...] += mm_nt(pre_low, up_ref[r])
    wait(start(blocks_out([(f, 2 * unit) for f in full], info_ref, send_ref, near_ref, pass_ref), sem))


def hidden_back(info, pair, mixed_low, act_t, slope, normed_t, up, down, acc):
    total, width = mixed_low.shape
    k = len(pair)
    return pl.pallas_call(
        partial(hidden_back_kernel, pair),
        in_specs=[SMEM] + [VMEM] * 7,
        out_specs=[HBM] * 3 + [VMEM] * 2,
        out_shape=(
            far_shape((k * width, width), BF16),
            far_shape((k * width // 2, width), BF16),
            far_shape((k * width // 2, width), BF16),
            shape((total, width), F32),
            shape((8 * k, width), F32),
        ),
        scratch_shapes=[pltpu.VMEM((2 * width, width), BF16) for _ in pair] + [DMA],
        input_output_aliases={7: 3},
        compiler_params=params(12),
        cost_estimate=cost(7 * k, 8 * k),
        name="hidden_back",
    )(info, mixed_low, act_t, slope, normed_t, up, down, acc)


def norm_back_kernel(attended_ref, grad_ref, vec_ref, sums_ref, out_ref, low_ref, all_ref):
    scaled, inv = norm_parts(attended_ref[...])
    grad, grad_gain, grad_shift = norm_backward(grad_ref[...], scaled, inv, vec_ref[0:1].astype(F32))
    out_ref[...] = grad
    low_ref[...] = grad.astype(BF16)
    all_ref[...] = sums_ref[...]
    all_ref[3:4] = grad_gain
    all_ref[4:5] = grad_shift
    all_ref[5:6] = jnp.sum(grad, 0, keepdims=True)


def norm_back(attended, grad, vec, sums):
    total, width = attended.shape
    return pl.pallas_call(
        norm_back_kernel,
        in_specs=[VMEM] * 4,
        out_specs=[VMEM] * 3,
        out_shape=(shape((total, width), F32), shape((total, width), BF16), shape((8, width), F32)),
        input_output_aliases={1: 0},
        compiler_params=params(8),
        cost_estimate=cost(2, 6),
        name="norm_back",
    )(attended, grad, vec, sums)


def attend_back_kernel(words, gw, heads, final, count, info_ref, rows_ref, lt_ref, low_ref, up_ref, acc_ref, *refs):
    pw_ref, pe_ref, ctx_ref = refs[:3]
    pieces, refs = refs[3 : 3 + count], refs[3 + count :]
    if final:
        spans_ref, send_ref, near_ref, pass_ref, words_ref, ents_ref, pos_s, *refs = refs
    else:
        send_ref, near_ref, pass_ref, out_ref, *refs = refs
    (
        w_s, pw_s, pe_s, ctx_s, qw_s, qe_s, k_s, v_s, dc_s, p_s, ds_s, dpw_s, dpe_s, full_s, sem,
    ) = refs
    half = 2 * gw
    total = rows_ref.shape[0]
    size = w_s.shape[0] // 8
    saved = start([(pw_ref, pw_s), (pe_ref, pe_s)], sem.at[0])
    if count == 4:
        reads = start([(v, w_s.at[pl.ds(i * gw, gw)]) for i, v in enumerate(own_parts(*pieces))], sem.at[1])
    else:
        reads = start(place(pieces, info_ref, size, (w_s,)), sem.at[1])
    last = start([(ctx_ref, ctx_s)], sem.at[2])
    wait(saved)
    split_heads(words, gw, heads, pw_s, pe_s, qw_s, qe_s, k_s, v_s)
    wait(reads)
    grad_ctx = mm_nt(low_ref[...], w_s[6 * gw : 7 * gw]).astype(BF16)
    for h in range(heads):
        dc_s[h] = grad_ctx[:, h * HEAD_DIM : (h + 1) * HEAD_DIM]
    wait(last)
    full_s[6 * gw : 7 * gw] = mm_tn(ctx_s[...], low_ref[...]).astype(BF16)
    for h in range(heads):
        o = h * HEAD_DIM
        e = o + HEAD_DIM
        logt = lt_ref[h : h + 1]
        pw = jnp.exp(mm_nt(k_s[h, :words], qw_s[h]) - logt)
        pe = jnp.exp(mm_nt(k_s[h, words:], qe_s[h]) - logt)
        gw_ = mm_nt(v_s[h, :words], dc_s[h])
        ge_ = mm_nt(v_s[h, words:], dc_s[h])
        p_s[:words] = pw.astype(BF16)
        p_s[words:] = pe.astype(BF16)
        dot = jnp.sum(pw * gw_, 0, keepdims=True) + jnp.sum(pe * ge_, 0, keepdims=True)
        ds_s[:words] = (pw * (gw_ - dot)).astype(BF16)
        ds_s[words:] = (pe * (ge_ - dot)).astype(BF16)
        dv = mm(p_s[...], dc_s[h]).astype(BF16)
        dkw = mm(ds_s[:words], qw_s[h]).astype(BF16)
        dke = mm(ds_s[words:], qe_s[h]).astype(BF16)
        dqw = (mm_tn(ds_s[:words], k_s[h, :words]) * SCALE).astype(BF16)
        dqe = (mm_tn(ds_s[words:], k_s[h, words:]) * SCALE).astype(BF16)
        dpw_s[:, o:e] = dqw[:words]
        dpw_s[:, gw + o : gw + e] = dqe[:words]
        dpw_s[:, half + o : half + e] = dkw
        dpw_s[:, half + gw + o : half + gw + e] = dv[:words]
        dpe_s[:, o:e] = dke
        dpe_s[:, gw + o : gw + e] = dv[words:]
        dpe_s[:, half + o : half + e] = dqw[words:]
        dpe_s[:, half + gw + o : half + gw + e] = dqe[words:]
    dpw = dpw_s[...]
    dpe = dpe_s[...]
    rows_w = rows_ref[:words]
    rows_e = rows_ref[words:]
    full_s[:half] = mm_tn(dpw[:, :half], rows_w).astype(BF16)
    full_s[half : 2 * half] = (mm_tn(dpw[:, half:], rows_w) + mm_tn(dpe[:, :half], rows_e)).astype(BF16)
    full_s[2 * half : 3 * half] = mm_tn(dpe[:, half:], rows_e).astype(BF16)
    sw = jnp.sum(dpw.astype(F32), 0, keepdims=True)
    se = jnp.sum(dpe.astype(F32), 0, keepdims=True)
    sum_a = jnp.concatenate([sw[:, :half], sw[:, half:] + se[:, :half]], 1)
    sum_b = jnp.concatenate([se[:, half:], jnp.zeros((1, half), F32)], 1)
    spare = w_s.shape[0] - 7 * gw
    row = lax.broadcasted_iota(jnp.int32, (spare, 2 * half), 0)
    sums = jnp.where(row == 0, sum_a, jnp.where(row == 1, sum_b, jnp.where(row == 2, up_ref[0:1], 0.0)))
    full_s[7 * gw :] = sums.astype(BF16)
    if final:
        grad = acc_ref[words:] + mm(dpe, w_s[half : 3 * half])
        ents_ref[...] = grad
        spans = spans_ref[info_ref[0]]
        begin = spans[:, 0:1]
        end = spans[:, 1:2]
        position = lax.broadcasted_iota(jnp.int32, (total - words, words), 1)
        inside = jnp.where(jnp.logical_and(position >= begin, position < end), 1.0, 0.0).astype(BF16)
        scaled = grad * (1.0 / (end - begin).astype(F32))
        high = scaled.astype(BF16)
        rest = (scaled - high.astype(F32)).astype(BF16)
        pos_s[...] = (mm_tn(inside, high) + mm_tn(inside, rest)).astype(BF16)
        sources = [(full_s, size), (pos_s, words // 8)]
        writes = start(blocks_out(sources, info_ref, send_ref, near_ref, pass_ref), sem.at[3])
        words_ref[...] = acc_ref[:words] + mm(dpw, w_s[: 2 * half])
    else:
        writes = start(blocks_out([(full_s, size)], info_ref, send_ref, near_ref, pass_ref), sem.at[3])
        out_ref[:words] = acc_ref[:words] + mm(dpw, w_s[: 2 * half])
        out_ref[words:] = acc_ref[words:] + mm(dpe, w_s[half : 3 * half])
    wait(writes)


def attend_back(info, rows_low, saved, low, up_sums, acc, pieces, words, heads, rows, spans=None):
    total, width = rows_low.shape
    pw, pe, ctx, lt = saved
    ents = total - words
    gw = heads * HEAD_DIM
    count = len(pieces)
    final = spans is not None
    moved = rows + words if final else rows
    grads = (shape((words, width), F32), shape((ents, width), F32)) if final else (shape((total, width), F32),)
    return pl.pallas_call(
        partial(attend_back_kernel, words, gw, heads, final, count),
        in_specs=[SMEM] + [VMEM] * 5 + [HBM] * (3 + count) + [VMEM] * final,
        out_specs=[HBM] * 3 + [VMEM] * len(grads),
        out_shape=(
            far_shape((moved // 2, width), BF16),
            far_shape((moved // 4, width), BF16),
            far_shape((moved // 4, width), BF16),
        )
        + grads,
        scratch_shapes=[pltpu.VMEM((words, width), BF16)] * final
        + [
            pltpu.VMEM((rows, width), BF16),
            pltpu.VMEM((words, 4 * gw), BF16),
            pltpu.VMEM((ents, 4 * gw), BF16),
            pltpu.VMEM((total, gw), BF16),
        ]
        + [pltpu.VMEM((heads, total, HEAD_DIM), BF16) for _ in range(5)]
        + [
            pltpu.VMEM((total, total), BF16),
            pltpu.VMEM((total, total), BF16),
            pltpu.VMEM((words, 4 * gw), BF16),
            pltpu.VMEM((ents, 4 * gw), BF16),
            pltpu.VMEM((rows, width), BF16),
            DMA((4,)),
        ],
        input_output_aliases={} if final else {5: 3},
        compiler_params=params(24),
        cost_estimate=cost(11, 8),
        name="attend_back",
    )(info, rows_low, lt, low, up_sums, acc, *far((pw, pe, ctx)), *far(pieces), *((spans,) if final else ()))


def spread_query_kernel(info_ref, *refs):
    pieces = refs[:8]
    query_ref, key_ref, value_ref, out_ref, qb_ref, vb_ref, ub_ref, s, sem = refs[8:]
    wait(start(place(pieces, info_ref, s.shape[0] // 8, (s,)), sem))
    gw = key_ref.shape[0]
    for i, k in ((0, 0), (1, 1), (2, 4), (3, 5)):
        query_ref[i] = s[k * gw : (k + 1) * gw].astype(F32)
    key_ref[...] = s[2 * gw : 3 * gw].astype(F32)
    value_ref[...] = s[3 * gw : 4 * gw].astype(F32)
    out_ref[...] = s[6 * gw : 7 * gw].astype(F32)
    rows = s[7 * gw : 7 * gw + TILE].astype(F32)
    qb_ref[0:1] = rows[0:1, :gw]
    qb_ref[1:2] = rows[0:1, gw : 2 * gw]
    qb_ref[2:3] = rows[1:2, :gw]
    qb_ref[3:4] = rows[1:2, gw : 2 * gw]
    vb_ref[...] = rows[0:1, 3 * gw :]
    ub_ref[...] = rows[2:3]


def spread_query(info, pieces, gw):
    unit, width = pieces[0].shape
    flat = shape((gw, width), F32)
    return pl.pallas_call(
        spread_query_kernel,
        in_specs=[SMEM] + [HBM] * 8,
        out_specs=[VMEM] * 7,
        out_shape=(
            shape((4, gw, width), F32), flat, flat, flat,
            shape((4, gw), F32), shape((1, gw), F32), shape((1, width), F32),
        ),
        scratch_shapes=[pltpu.VMEM((8 * unit, width), BF16), DMA],
        compiler_params=params(8),
        cost_estimate=cost(0.5, 7),
        name="spread_query",
    )(info, *far(pieces))


def spread_hidden_kernel(info_ref, *refs):
    pieces = refs[:8]
    up_ref, down_ref, up_s, down_s, sem = refs[8:]
    wait(start(place(pieces, info_ref, up_ref.shape[0] // 8, (up_s, down_s)), sem))
    up_ref[...] = up_s[...].astype(F32)
    down_ref[...] = down_s[...].astype(F32)


def spread_hidden(info, pieces):
    rows, width = pieces[0].shape
    out = shape((4 * rows, width), F32)
    return pl.pallas_call(
        spread_hidden_kernel,
        in_specs=[SMEM] + [HBM] * 8,
        out_specs=[VMEM] * 2,
        out_shape=(out, out),
        scratch_shapes=[pltpu.VMEM((4 * rows, width), BF16)] * 2 + [DMA],
        compiler_params=params(9),
        cost_estimate=cost(0.5, 7),
        name="spread_hidden",
    )(info, *far(pieces))


def spread_pos_kernel(info_ref, *refs):
    pieces = refs[:8]
    pos_ref, s, sem = refs[8:]
    wait(start(place(pieces, info_ref, s.shape[0] // 8, (s,)), sem))
    pos_ref[...] = s[...].astype(F32)


def spread_pos(info, pieces):
    rows, width = pieces[0].shape
    return pl.pallas_call(
        spread_pos_kernel,
        in_specs=[SMEM] + [HBM] * 8,
        out_specs=VMEM,
        out_shape=shape((8 * rows, width), F32),
        scratch_shapes=[pltpu.VMEM((8 * rows, width), BF16), DMA],
        compiler_params=params(4),
        cost_estimate=cost(0.5, 3),
        name="spread_pos",
    )(info, *far(pieces))


class Links:
    def __init__(self):
        self.dp = lax.axis_size("dp")
        self.ring = lax.axis_size("tensor")
        dp_index = lax.axis_index("dp")
        self.z = lax.axis_index("tensor")
        self.core = dp_index % 2
        self.bits = (self.dp // 2).bit_length() - 1
        self.bit = [(dp_index // (2 << k)) % 2 for k in range(self.bits)]

    def shift_z(self, v, by):
        n = self.ring
        return lax.ppermute(v, "tensor", [(i, (i + by) % n) for i in range(n)])

    def swap_z(self, v, mask):
        return lax.ppermute(v, "tensor", [(i, i ^ mask) for i in range(self.ring)])

    def swap(self, v, code):
        return lax.ppermute(v, "dp", [(i, i ^ code) for i in range(self.dp)])

    def swap_core(self, v):
        return self.swap(v, 1)

    def first(self, v):
        return lax.ppermute(v, "dp", [(i, i ^ (4 if i % 2 else 2)) for i in range(self.dp)])

    def second(self, v):
        return lax.ppermute(v, "dp", [(i, i ^ (2 if i % 2 else 4)) for i in range(self.dp)])


def after(value, *others):
    return lax.optimization_barrier((value,) + others)[0]


def sync(*values):
    return lax.optimization_barrier(values)


def add_low(*parts):
    total = parts[0].astype(F32)
    for part in parts[1:]:
        total = total + part.astype(F32)
    return total.astype(BF16)


class Blocks:
    def __init__(self, links, send, near, far):
        self.links, self.send, self.near, self.far = links, send, near, far
        self.unit = near.shape[0] // 2

    def one(self):
        return add_low(self.far, self.got[2 * self.unit :])

    def two(self):
        u = self.unit
        return add_low(self.near[u:], self.got[u : 2 * u], self.a[u:])

    def rest(self, low, high, *more):
        value = add_low(self.near[low:high], self.got[low:high], self.a[low:high], self.b[low:high], *more)
        for j in range(2, self.links.bits):
            value = add_low(value, self.links.swap(value, 2 << j))
        return value


def shards(
    word_in,
    entity_in,
    entity_spans,
    word_mask,
    entity_mask,
    pos_table,
    query_w,
    query_b,
    key_w,
    value_w,
    value_b,
    out_w,
    out_b,
    norm1_gain,
    norm1_bias,
    up_w,
    up_b,
    down_w,
    down_b,
    norm2_gain,
    norm2_bias,
    cot_words,
    cot_entities,
):
    links = Links()
    n = links.ring
    z = links.z
    words = cot_words.shape[0]
    ents = cot_entities.shape[0]
    width = word_in.shape[1]
    gw = key_w.shape[1]
    heads = gw // HEAD_DIM
    rows = -(-(7 * gw + 3) // (8 * TILE)) * 8 * TILE
    part = 4 * links.core + 2 * links.bit[0] + links.bit[1]
    info = jnp.stack([z, links.core, part, 2 - links.core]).astype(jnp.int32)

    small = (query_b, value_b[None], up_b[None])
    own = (jnp.swapaxes(query_w, 1, 2), key_w.T, value_w.T, out_w)
    piece_q, piece_f = pack(info, small, own, up_w, down_w, rows)
    first, second, core, shift = links.first, links.second, links.swap_core, links.shift_z
    rows_low, acc = start_rows(info, word_in, entity_in, entity_spans, pos_table, out_b[None], words, ents)
    saved = [None] * n
    biases = [None] * n

    def attend_one(r, acc, pieces, small=()):
        pw, pe, ctx, lt, biases[r], acc = attend(info, rows_low, acc, pieces, words, heads, rows, small)
        saved[r] = (pw, pe, ctx, lt)
        return acc

    v1, v3 = shift(piece_q, 1), shift(piece_q, 3)
    acc, piece_f = sync(acc, piece_f)
    f1, f3 = shift(piece_f, 1), shift(piece_f, 3)
    acc = attend_one(0, acc, own, small)
    acc, v1, v3 = sync(acc, v1, v3)
    a1, b1, v2 = first(v1), second(v1), shift(v1, 1)
    acc, v1, a1, b1, v3, f1, f3 = sync(acc, v1, a1, b1, v3, f1, f3)
    c1, kv, ka, kb, a3, b3 = second(a1), core(v1), core(a1), core(b1), first(v3), second(v3)
    acc, c1, kv, ka, kb, v2, f1, v3 = sync(acc, c1, kv, ka, kb, v2, f1, v3)
    kc, f2 = core(c1), shift(f1, 1)
    acc, kc, a3, b3, v2, f3 = sync(acc, kc, a3, b3, v2, f3)
    group_1 = (v1, a1, b1, c1, kv, ka, kb, kc)

    c3, a2, b2, ag, bg = second(a3), first(v2), second(v2), first(f3), second(f3)
    acc = attend_one(1, acc, group_1)
    acc, c3, a2, b2, ag, bg, f1, f2 = sync(acc, c3, a2, b2, ag, bg, f1, f2)
    kv, ka, kb, kc = core(v3), core(a3), core(b3), core(c3)
    far_f = jnp.concatenate([f1, f2], 0)
    acc, kv, ka, kb, kc, far_f, a2, ag, v2 = sync(acc, kv, ka, kb, kc, far_f, a2, ag, v2)
    group_3 = (v3, a3, b3, c3, kv, ka, kb, kc)

    c2, cg, af, kv, ka = second(a2), second(ag), first(far_f), core(v2), core(a2)
    acc = attend_one(3, acc, group_3)
    acc, c2, cg, af, kv, ka, b2, far_f = sync(acc, c2, cg, af, kv, ka, b2, far_f)
    kb, kc = core(b2), core(c2)
    acc, kb, kc, far_f, af, f3, ag, bg = sync(acc, kb, kc, far_f, af, f3, ag, bg)
    group_2 = (v2, a2, b2, c2, kv, ka, kb, kc)

    bf, cf, kv_g, ka_g, kb_g = second(far_f), second(af), core(f3), core(ag), core(bg)
    acc = attend_one(2, acc, group_2)
    acc, bf, cf, kv_g, ka_g, kb_g, cg, af, far_f = sync(acc, bf, cf, kv_g, ka_g, kb_g, cg, af, far_f)
    attended = acc
    ffn_pieces = (
        far_f, af, bf, cf, core(far_f), core(af), core(bf), core(cf), f3, ag, bg, cg, kv_g, ka_g, kb_g, core(cg)
    )
    query_groups = (own, group_1, group_2, group_3)

    vec = jnp.stack([norm1_gain, norm1_bias, down_b, norm2_gain, norm2_bias] + [down_b] * 3)
    normed_t, act_t, slope, up, down, out_words, out_ents, mixed_low, acc, sums = hidden(
        info, attended, vec, word_mask, entity_mask, cot_words, cot_entities, biases, (up_w, down_w), ffn_pieces
    )

    size = width // 4
    unit = rows // 8
    up_sums = [None] * n

    def ffn_blocks(group, acc):
        send, near, rest, acc, up_sum = hidden_back(info, group, mixed_low, act_t, slope, normed_t, up, down, acc)
        for k, r in enumerate(group):
            up_sums[r] = up_sum[8 * k : 8 * k + 8]
        return Blocks(links, send, near, rest), acc

    def back(r, acc, spans=None):
        send, near, rest, *acc = attend_back(
            info, rows_low, saved[r], attended_low, up_sums[r], acc, query_groups[r], words, heads, rows, spans
        )
        return Blocks(links, send, near, rest), *acc

    fa, acc = ffn_blocks((2, 1), acc)
    fa.got = core(fa.send)
    fb, acc = ffn_blocks((3,), acc)
    acc, fa.got = sync(acc, fa.got)
    acc, one_a = sync(acc, fa.one())

    fa.a, fb.got = first(one_a), core(fb.send)
    fc, acc = ffn_blocks((0,), acc)
    acc, fb.got = sync(acc, fb.got)
    one_b = fb.one()
    fc.got = core(fc.send)
    acc, attended_low, sums = norm_back(attended, acc, vec, sums)
    more = core(sums)
    acc, one_b, sums, more, fc.got = sync(acc, one_b, sums, more, fc.got)
    acc, one_c, sums = sync(acc, fc.one(), sums + more)

    fb.a, fc.a, more = first(one_b), first(one_c), links.swap(sums, 2)
    q1, acc = back(2, acc)
    acc, fa.a, fb.a, fc.a, more = sync(acc, fa.a, fb.a, fc.a, more)
    q1.got = core(q1.send)
    acc, two_a, two_b, two_c, sums, q1.got = sync(acc, fa.two(), fb.two(), fc.two(), sums + more, q1.got)
    acc, one_1 = sync(acc, q1.one())

    fa.b, fb.b, fc.b, q1.a, more = second(two_a), second(two_b), second(two_c), first(one_1), links.swap(sums, 4)
    q2, acc = back(1, acc)
    acc, fa.b, fb.b, fc.b, q1.a, more = sync(acc, fa.b, fb.b, fc.b, q1.a, more)
    q2.got = core(q2.send)
    sums = sums + more
    for j in range(2, links.bits):
        sums = sums + links.swap(sums, 2 << j)
    acc, r2, r1, r3, two_1, q2.got, sums = sync(
        acc, fa.rest(0, size), fa.rest(size, 2 * size), fb.rest(0, size), q1.two(), q2.got, sums
    )
    acc, one_2 = sync(acc, q2.one())

    z2, z1, z3, q1.b, q2.a = shift(r2, -2), shift(r1, -1), shift(r3, -3), second(two_1), first(one_2)
    q3, acc = back(3, acc)
    acc, z2, z1, z3, q1.b, q2.a = sync(acc, z2, z1, z3, q1.b, q2.a)
    q3.got = core(q3.send)
    acc, own_f, value_1, two_2, q3.got = sync(
        acc, fc.rest(0, size, z1, z2, z3), q1.rest(0, unit), q2.two(), q3.got
    )
    acc, one_3 = sync(acc, q3.one())

    y1, ga, gb, q2.b, q3.a = shift(value_1, -2), first(own_f), second(own_f), second(two_2), first(one_3)
    q4, grad_words, grad_ents = back(0, acc, entity_spans)
    q4.send, y1, ga, gb, q2.b, q3.a, sums = sync(q4.send, y1, ga, gb, q2.b, q3.a, sums)

    q4.got = core(q4.send)
    y2, q3.b, gc = shift(q2.rest(0, unit), -1), second(q3.two()), second(ga)
    q4.a = first(q4.one())
    q4.a, q3.b, y2, gc, own_f, ga, gb, sums = sync(q4.a, q3.b, y2, gc, own_f, ga, gb, sums)

    y3, q4.b = shift(q3.rest(0, unit), -3), second(q4.two())
    near_f = (own_f, ga, gb, gc)
    far_f = tuple(core(v) for v in near_f)
    q4.b, y3, sums, *far_f = sync(q4.b, y3, sums, *far_f)

    pos = q4.rest(unit, unit + words // 8)
    own_q = q4.rest(0, unit, y1, y2, y3)
    p1, p2, p3 = (links.swap_z(pos, mask) for mask in (1, 2, 3))
    qa, qb = first(own_q), second(own_q)
    grad_up, grad_down = spread_hidden(info, near_f + tuple(far_f))
    p1, p2, p3, qa, qb, own_q, pos, sums, grad_up, grad_down = sync(
        p1, p2, p3, qa, qb, own_q, pos, sums, grad_up, grad_down
    )

    pos = ((pos.astype(F32) + p1.astype(F32)) + (p2.astype(F32) + p3.astype(F32))).astype(BF16)
    pa, pb, qc, more = first(pos), second(pos), second(qa), links.swap_z(sums, 1)
    kv, ka, kb = core(own_q), core(qa), core(qb)
    pa, pb, qc, more, kv, ka, kb, pos = sync(pa, pb, qc, more, kv, ka, kb, pos)
    sums = sums + more
    pc, more, kc = second(pa), links.swap_z(sums, 2), core(qc)
    kp = tuple(core(v) for v in (pos, pa, pb))
    grad_query_t, grad_key_t, grad_value_t, grad_out, grad_query_b, grad_value_b, grad_up_b = spread_query(
        info, (own_q, qa, qb, qc, kv, ka, kb, kc), gw
    )
    total_sums = sums + more
    grad_query_t, pc, *kp = sync(grad_query_t, pc, *kp)
    pos_sum = spread_pos(info, (pos, pa, pb, pc, *kp, core(pc)))
    return (
        out_words,
        out_ents,
        grad_words,
        grad_ents,
        pos_sum,
        jnp.swapaxes(grad_query_t, 1, 2),
        grad_query_b,
        grad_key_t.T,
        grad_value_t.T,
        grad_value_b[0],
        grad_out,
        total_sums[5],
        total_sums[3],
        total_sums[4],
        grad_up,
        grad_up_b[0],
        grad_down,
        total_sums[2],
        total_sums[0],
        total_sums[1],
    )


def solution(mesh):
    rows = P(("dp", "tensor"), None)
    last = P(None, "tensor")
    placed = (
        P("dp", None),
        P("dp", None),
        P("dp", None, None),
        P("dp", None),
        P("dp", None),
        P(),
        P(None, None, "tensor"),
        last,
        last,
        last,
        P("tensor"),
        P("tensor", None),
        P(),
        P(),
        P(),
        last,
        P("tensor"),
        P("tensor", None),
        P(),
        P(),
        P(),
        rows,
        rows,
    )
    return jax.shard_map(
        shards,
        mesh=mesh,
        in_specs=placed,
        out_specs=(
            rows,
            rows,
            rows,
            rows,
            P(),
            P(None, None, "tensor"),
            last,
            last,
            last,
            P("tensor"),
            P("tensor", None),
            P(),
            P(),
            P(),
            last,
            P("tensor"),
            P("tensor", None),
            P(),
            P(),
            P(),
        ),
        check_vma=False,
    )
```

```python
from functools import partial

import jax
import jax.numpy as jnp
from jax import lax
from jax.experimental import pallas as pl
from jax.experimental.pallas import tpu as pltpu
from jax.sharding import PartitionSpec as P

HEAD_DIM = 64
SCALE = HEAD_DIM**-0.5
norm_epsilon = 1e-12
F32 = jnp.float32
BF16 = jnp.bfloat16
NT = (((1,), (1,)), ((), ()))
TN = (((0,), (0,)), ((), ()))
ERFC_STEP = 0.35
ERFC_POLY = (
    0.1396196249207051,
    0.13989555693599826,
    0.11957015144655456,
    0.10661400019997494,
    -0.025870835326937874,
    0.16337919550284652,
    -0.25954764983005574,
    0.14589250699009862,
    -0.029552569422939476,
)
TILE = 16
VMEM = pl.BlockSpec(memory_space=pltpu.VMEM)
SMEM = pl.BlockSpec(memory_space=pltpu.SMEM)
HBM = pl.BlockSpec(memory_space=pltpu.HBM)
DMA = pltpu.SemaphoreType.DMA


def mm(a, b):
    return jnp.dot(a, b, preferred_element_type=F32)


def mm_nt(a, b):
    return lax.dot_general(a, b, NT, preferred_element_type=F32)


def mm_tn(a, b):
    return lax.dot_general(a, b, TN, preferred_element_type=F32)


def params(mib):
    return pltpu.CompilerParams(vmem_limit_bytes=mib << 20)


def cost(gflop, mbytes):
    return pl.CostEstimate(
        flops=int(gflop * 1e9), bytes_accessed=int(mbytes * 1e6), transcendentals=0
    )


def shape(dims, kind):
    return jax.ShapeDtypeStruct(dims, kind)


def far(values):
    return tuple(pltpu.with_memory_space_constraint(v, pltpu.HBM) for v in values)


def far_shape(dims, kind):
    return pltpu.HBM(dims, kind)


def start(pairs, sem):
    copies = [pltpu.make_async_copy(source, target, sem) for source, target in pairs]
    for copy in copies:
        copy.start()
    return copies


def wait(copies):
    for copy in copies:
        copy.wait()


def rows_at(first, size):
    return pl.ds(pl.multiple_of(first, TILE), size)


def place(pieces, info_ref, unit, targets, skip=0):
    part, first = info_ref[2], info_ref[3]
    second = 3 - first
    pairs = []
    for piece, code in zip(pieces, (0, first, second, 3, 4, 4 + second, 4 + first, 7)):
        row = lax.bitwise_xor(part, jnp.int32(code)) * unit
        for t, target in enumerate(targets):
            pairs.append((piece.at[pl.ds(skip + t * unit, unit)], target.at[rows_at(row, unit)]))
    return pairs


def blocks_out(sources, info_ref, send_ref, near_ref, pass_ref):
    part, first = info_ref[2], info_ref[3]
    second = 3 - first
    keep = (0, second, first, 3)
    send = (4, 4 + first, 4 + second, 7)
    total = sum(unit for _, unit in sources)
    pairs = []
    for i in range(4):
        done = 0
        for source, unit in sources:
            other = lax.bitwise_xor(part, jnp.int32(send[i])) * unit
            mine = lax.bitwise_xor(part, jnp.int32(keep[i])) * unit
            to = near_ref if i < 2 else pass_ref
            pairs.append((source.at[rows_at(other, unit)], send_ref.at[pl.ds(i * total + done, unit)]))
            pairs.append((source.at[rows_at(mine, unit)], to.at[pl.ds((i % 2) * total + done, unit)]))
            done += unit
    return pairs


def own_parts(query_ref, key_ref, value_ref, out_ref):
    return (query_ref.at[0], query_ref.at[1], key_ref, value_ref, query_ref.at[2], query_ref.at[3], out_ref)


def spare_rows(qb_ref, vb_ref, ub_ref, spare):
    qb = qb_ref[...].astype(F32)
    none = jnp.zeros((1, qb.shape[1]), F32)
    first = jnp.concatenate([qb[0:1], qb[1:2], none, vb_ref[...].astype(F32)], 1)
    second = jnp.concatenate([qb[2:3], qb[3:4], none, none], 1)
    row = lax.broadcasted_iota(jnp.int32, (spare, first.shape[1]), 0)
    rows = jnp.where(row == 0, first, jnp.where(row == 1, second, jnp.where(row == 2, ub_ref[...].astype(F32), 0.0)))
    return rows.astype(BF16)


def pack_kernel(
    gw, info_ref, qb_ref, vb_ref, ub_ref, query_ref, key_ref, value_ref, ow_ref, up_ref, down_ref,
    piece_ref, ffn_ref, w_s, f_s, sem,
):
    part = info_ref[2]
    size = piece_ref.shape[0]
    low = lax.div(part * size, jnp.int32(gw))
    copies = []
    for i, ref in enumerate(own_parts(query_ref, key_ref, value_ref, ow_ref)):
        needed = jnp.logical_or(low == i, low + 1 == i)
        copies.append((needed, pltpu.make_async_copy(ref, w_s.at[pl.ds(i * gw, gw)], sem.at[0])))
    for needed, copy in copies:
        pl.when(needed)(copy.start)
    unit = f_s.shape[0] // 2
    ffn = start(
        [(v.at[rows_at(part * unit, unit)], f_s.at[pl.ds(i * unit, unit)]) for i, v in enumerate((up_ref, down_ref))],
        sem.at[1],
    )
    w_s[7 * gw :] = spare_rows(qb_ref, vb_ref, ub_ref, w_s.shape[0] - 7 * gw)
    for needed, copy in copies:
        pl.when(needed)(copy.wait)
    piece = start([(w_s.at[rows_at(part * size, size)], piece_ref)], sem.at[2])
    wait(ffn)
    last = start([(f_s, ffn_ref)], sem.at[3])
    wait(piece)
    wait(last)


def pack(info, biases, own, up_w, down_w, rows):
    gw, width = own[1].shape
    unit = up_w.shape[0] // 8
    return pl.pallas_call(
        partial(pack_kernel, gw),
        in_specs=[SMEM] + [VMEM] * 3 + [HBM] * 6,
        out_specs=[HBM] * 2,
        out_shape=(far_shape((rows // 8, width), BF16), far_shape((2 * unit, width), BF16)),
        scratch_shapes=[pltpu.VMEM((rows, width), BF16), pltpu.VMEM((2 * unit, width), BF16), DMA((4,))],
        compiler_params=params(4),
        cost_estimate=cost(0.01, 3),
        name="pack",
    )(info, *biases, *far(own + (up_w, down_w)))


def start_kernel(info_ref, words_ref, ents_ref, spans_ref, table_ref, bias_ref, low_ref, resid_ref, w_s, e_s, t_s, sem):
    words, count = w_s.shape[0], e_s.shape[0]
    z = info_ref[0]
    ents = start(
        [(ents_ref.at[rows_at(z * count, count)], e_s), (table_ref, t_s)],
        sem.at[0],
    )
    reads = start([(words_ref.at[rows_at(z * words, words)], w_s)], sem.at[1])
    spans = spans_ref[z]
    begin = spans[:, 0:1]
    end = spans[:, 1:2]
    position = lax.broadcasted_iota(jnp.int32, (count, words), 1)
    inside = jnp.where(jnp.logical_and(position >= begin, position < end), 1.0, 0.0).astype(BF16)
    share = 1.0 / (end - begin).astype(F32)
    out_b = bias_ref[...].astype(F32)
    wait(ents)
    rows = e_s[...].astype(F32) + mm(inside, t_s[...]) * share
    low_ref[words:] = rows.astype(BF16)
    resid_ref[words:] = rows + out_b
    wait(reads)
    low_ref[:words] = w_s[...]
    resid_ref[:words] = w_s[...].astype(F32) + out_b


def start_rows(info, word_in, entity_in, spans, table, out_b, words, ents):
    width = word_in.shape[1]
    total = words + ents
    return pl.pallas_call(
        start_kernel,
        in_specs=[SMEM, HBM, HBM, VMEM, HBM, VMEM],
        out_specs=[VMEM] * 2,
        out_shape=(shape((total, width), BF16), shape((total, width), F32)),
        scratch_shapes=[
            pltpu.VMEM((words, width), BF16),
            pltpu.VMEM((ents, width), BF16),
            pltpu.VMEM(table.shape, BF16),
            DMA((2,)),
        ],
        compiler_params=params(6),
        cost_estimate=cost(0.5, 6),
        name="start_rows",
    )(info, *far((word_in, entity_in)), spans, *far((table,)), out_b)


def split_heads(words, gw, heads, pw_ref, pe_ref, qw_s, qe_s, k_s, v_s):
    half = 2 * gw
    for h in range(heads):
        o = h * HEAD_DIM
        e = o + HEAD_DIM
        qw_s[h, :words] = pw_ref[:, o:e] * SCALE
        qw_s[h, words:] = pe_ref[:, half + o : half + e] * SCALE
        qe_s[h, :words] = pw_ref[:, gw + o : gw + e] * SCALE
        qe_s[h, words:] = pe_ref[:, half + gw + o : half + gw + e] * SCALE
        k_s[h, :words] = pw_ref[:, half + o : half + e]
        k_s[h, words:] = pe_ref[:, o:e]
        v_s[h, :words] = pw_ref[:, half + gw + o : half + gw + e]
        v_s[h, words:] = pe_ref[:, gw + o : gw + e]


def attend_kernel(words, gw, heads, count, info_ref, rows_ref, acc_ref, *refs):
    own = count == 4
    small, refs = (refs[:3], refs[3:]) if own else ((), refs)
    pieces = refs[:count]
    pw_ref, pe_ref, ctx_ref, lt_ref, bias_ref, out_ref, w_s, pw_s, pe_s, ctx_s, qw_s, qe_s, k_s, v_s, sem = refs[count:]
    half = 2 * gw
    if own:
        reads = start([(v, w_s.at[pl.ds(i * gw, gw)]) for i, v in enumerate(own_parts(*pieces))], sem.at[0])
        w_s[7 * gw :] = spare_rows(*small, w_s.shape[0] - 7 * gw)
        wait(reads)
    else:
        wait(start(place(pieces, info_ref, w_s.shape[0] // 8, (w_s,)), sem.at[0]))
    rows_b = w_s[7 * gw : 7 * gw + TILE]
    bias_ref[...] = rows_b
    rows_b = rows_b.astype(F32)
    bias_e = jnp.concatenate([rows_b[0:1, half:], rows_b[1:2, :half]], 1)
    pw_s[...] = (mm_nt(rows_ref[:words], w_s[: 4 * gw]) + rows_b[0:1]).astype(BF16)
    pe_s[...] = (mm_nt(rows_ref[words:], w_s[half : 6 * gw]) + bias_e).astype(BF16)
    saves = start([(pw_s, pw_ref), (pe_s, pe_ref)], sem.at[1])
    split_heads(words, gw, heads, pw_s, pe_s, qw_s, qe_s, k_s, v_s)
    block = 128

    def step(qb, carry):
        rows = pl.ds(pl.multiple_of(qb * block, block), block)
        parts = []
        for h in range(heads):
            sw = mm_nt(qw_s[h, rows], k_s[h, :words])
            se = mm_nt(qe_s[h, rows], k_s[h, words:])
            top = jnp.maximum(jnp.max(sw, 1, keepdims=True), jnp.max(se, 1, keepdims=True))
            ew = jnp.exp(sw - top)
            ee = jnp.exp(se - top)
            total = jnp.sum(ew, 1, keepdims=True) + jnp.sum(ee, 1, keepdims=True)
            parts.append(
                (mm(ew.astype(BF16), v_s[h, :words]) + mm(ee.astype(BF16), v_s[h, words:])) * (1.0 / total)
            )
            logt = top + jnp.log(total)
            lt_ref[h : h + 1, rows] = jnp.broadcast_to(logt, (block, block)).T[0:1]
        ctx_s[rows, :] = jnp.concatenate(parts, 1).astype(BF16)
        return carry

    lax.fori_loop(0, rows_ref.shape[0] // block, step, 0, unroll=True)
    last = start([(ctx_s, ctx_ref)], sem.at[2])
    out_ref[...] = acc_ref[...] + mm(ctx_s[...], w_s[6 * gw : 7 * gw])
    wait(saves)
    wait(last)


def attend(info, rows_low, acc, pieces, words, heads, rows, small=()):
    total, width = rows_low.shape
    ents = total - words
    gw = heads * HEAD_DIM
    count = len(pieces)
    return pl.pallas_call(
        partial(attend_kernel, words, gw, heads, count),
        in_specs=[SMEM] + [VMEM] * (2 + len(small)) + [HBM] * count,
        out_specs=[HBM] * 3 + [VMEM] * 3,
        out_shape=(
            far_shape((words, 4 * gw), BF16),
            far_shape((ents, 4 * gw), BF16),
            far_shape((total, gw), BF16),
            shape((8, total), F32),
            shape((TILE, width), BF16),
            shape((total, width), F32),
        ),
        scratch_shapes=[
            pltpu.VMEM((rows, width), BF16),
            pltpu.VMEM((words, 4 * gw), BF16),
            pltpu.VMEM((ents, 4 * gw), BF16),
            pltpu.VMEM((total, gw), BF16),
        ]
        + [pltpu.VMEM((heads, total, HEAD_DIM), BF16) for _ in range(4)]
        + [DMA((3,))],
        input_output_aliases={2: 5},
        compiler_params=params(16),
        cost_estimate=cost(8, 6),
        name="attend_own" if small else "attend_far",
    )(info, rows_low, acc, *small, *far(pieces))


def gelu_pair(x):
    size = jnp.abs(x)
    t = 1.0 / (1.0 + ERFC_STEP * size)
    poly = jnp.full_like(x, ERFC_POLY[-1])
    for c in ERFC_POLY[-2::-1]:
        poly = poly * t + c
    bell = jnp.exp(x * x * -0.5)
    tail = poly * t * bell
    below = jnp.where(x >= 0, 1.0 - tail, tail)
    return x * below, below + x * (bell * 0.3989422804014327)


def norm_parts(values):
    centered = values - jnp.mean(values, 1, keepdims=True)
    inv = lax.rsqrt(jnp.mean(centered * centered, 1, keepdims=True) + norm_epsilon)
    return centered * inv, inv


def hidden_kernel(n, info_ref, attended_ref, vec_ref, wm_ref, em_ref, cw_ref, ce_ref, *refs):
    bias_refs, refs = refs[:n], refs[n:]
    up_own, down_own = refs[:2]
    pieces, refs = (refs[2:10], refs[10:18]), refs[18:]
    turn_ref, at_ref, slope_ref, up_s, down_s, ow_ref, oe_ref, mixed_ref, grad_ref, sums_ref, low_ref, acc_s, b_s, sem = refs
    total, width = attended_ref.shape
    unit = width // 8
    reads = [start([(up_own, up_s.at[0]), (down_own, down_s.at[0])], sem.at[0])]
    for r in range(1, n):
        held, skip = pieces[r // 3], 2 * unit * ((r - 1) % 2)
        reads.append(start(place(held, info_ref, unit, (up_s.at[r], down_s.at[r]), skip), sem.at[r]))
    for r in range(n):
        b_s[r] = bias_refs[r][2:3].astype(F32)
    scaled, _ = norm_parts(attended_ref[...])
    normed = scaled * vec_ref[0:1].astype(F32) + vec_ref[1:2].astype(F32)
    low = normed.astype(BF16)
    low_ref[...] = low
    turn_ref[...] = low.T
    acc_s[...] = normed + vec_ref[2:3].astype(F32)
    block = 128

    def group(r):
        for lo in range(0, total, block):
            pre = mm(low_ref[lo : lo + block], up_s[r]) + b_s[r]
            value, slope = gelu_pair(pre)
            slope_ref[r, lo : lo + block] = slope
            value = value.astype(BF16)
            at_ref[r, :, lo : lo + block] = value.T
            acc_s[lo : lo + block] += mm(value, down_s[r])

    for r in range(n):
        wait(reads[r])
        group(r)

    words = cw_ref.shape[0]
    z = info_ref[0]
    scaled, inv = norm_parts(acc_s[...])
    gain = vec_ref[3:4].astype(F32)
    output = scaled * gain + vec_ref[4:5].astype(F32)
    ow_ref[...] = output[:words].astype(BF16)
    oe_ref[...] = output[words:].astype(BF16)

    def column(ref, size):
        return jnp.broadcast_to(ref[pl.ds(z, 1), :].astype(F32), (128, size)).T[:, 0:1]

    cot = jnp.concatenate(
        [
            column(wm_ref, words) * cw_ref[...].astype(F32),
            column(em_ref, total - words) * ce_ref[...].astype(F32),
        ],
        0,
    )
    grad, grad_gain, grad_shift = norm_backward(cot, scaled, inv, gain)
    grad_ref[...] = grad
    mixed_ref[...] = grad.astype(BF16)
    sums_ref[0:1] = grad_gain
    sums_ref[1:2] = grad_shift
    sums_ref[2:3] = jnp.sum(grad, 0, keepdims=True)
    sums_ref[3:] = jnp.zeros((5, width), F32)


def hidden(info, attended, vec, word_mask, entity_mask, cot_words, cot_ents, biases, own, pieces):
    total, width = attended.shape
    n = len(biases)
    return pl.pallas_call(
        partial(hidden_kernel, n),
        in_specs=[SMEM] + [VMEM] * (6 + n) + [HBM] * (2 + len(pieces)),
        out_specs=[VMEM] * 10,
        out_shape=(
            shape((width, total), BF16),
            shape((n, width, total), BF16),
            shape((n, total, width), F32),
            shape((n, width, width), BF16),
            shape((n, width, width), BF16),
            shape(cot_words.shape, BF16),
            shape(cot_ents.shape, BF16),
            shape((total, width), BF16),
            shape((total, width), F32),
            shape((8, width), F32),
        ),
        scratch_shapes=[
            pltpu.VMEM((total, width), BF16),
            pltpu.VMEM((total, width), F32),
            pltpu.VMEM((n, 1, width), F32),
            DMA((n,)),
        ],
        compiler_params=params(18),
        cost_estimate=cost(22, 20),
        name="hidden",
    )(info, attended, vec, word_mask, entity_mask, cot_words, cot_ents, *biases, *far(own), *far(pieces))


def norm_backward(grad_in, scaled, inv_std, gain_row):
    grad_gain = jnp.sum(grad_in * scaled, axis=0, keepdims=True)
    grad_shift = jnp.sum(grad_in, axis=0, keepdims=True)
    grad_scaled = grad_in * gain_row
    mean_first = jnp.mean(grad_scaled, axis=1, keepdims=True)
    mean_second = jnp.mean(grad_scaled * scaled, axis=1, keepdims=True)
    return inv_std * (grad_scaled - mean_first - scaled * mean_second), grad_gain, grad_shift


def hidden_back_kernel(
    pair, info_ref, low_ref, at_ref, slope_ref, turn_ref, up_ref, down_ref, acc_ref,
    send_ref, near_ref, pass_ref, out_ref, b_ref, *refs,
):
    full, sem = refs[:-1], refs[-1]
    unit = turn_ref.shape[0] // 8
    low = low_ref[...]
    out_ref[...] = acc_ref[...]
    for k, r in enumerate(pair):
        grad_down = mm(at_ref[r], low).astype(BF16)
        for i in range(8):
            full[k][(2 * i + 1) * unit : (2 * i + 2) * unit] = grad_down[i * unit : (i + 1) * unit]
        pre_low = (mm_nt(low, down_ref[r]) * slope_ref[r]).astype(BF16)
        grad_up = mm(turn_ref[...], pre_low).astype(BF16)
        for i in range(8):
            full[k][2 * i * unit : (2 * i + 1) * unit] = grad_up[i * unit : (i + 1) * unit]
        b_ref[8 * k : 8 * k + 8] = jnp.broadcast_to(jnp.sum(pre_low.astype(F32), 0, keepdims=True), (8, b_ref.shape[1]))
        out_ref[...] += mm_nt(pre_low, up_ref[r])
    wait(start(blocks_out([(f, 2 * unit) for f in full], info_ref, send_ref, near_ref, pass_ref), sem))


def hidden_back(info, pair, mixed_low, act_t, slope, normed_t, up, down, acc):
    total, width = mixed_low.shape
    k = len(pair)
    return pl.pallas_call(
        partial(hidden_back_kernel, pair),
        in_specs=[SMEM] + [VMEM] * 7,
        out_specs=[HBM] * 3 + [VMEM] * 2,
        out_shape=(
            far_shape((k * width, width), BF16),
            far_shape((k * width // 2, width), BF16),
            far_shape((k * width // 2, width), BF16),
            shape((total, width), F32),
            shape((8 * k, width), F32),
        ),
        scratch_shapes=[pltpu.VMEM((2 * width, width), BF16) for _ in pair] + [DMA],
        input_output_aliases={7: 3},
        compiler_params=params(12),
        cost_estimate=cost(7 * k, 8 * k),
        name="hidden_back",
    )(info, mixed_low, act_t, slope, normed_t, up, down, acc)


def norm_back_kernel(attended_ref, grad_ref, vec_ref, sums_ref, out_ref, low_ref, all_ref):
    scaled, inv = norm_parts(attended_ref[...])
    grad, grad_gain, grad_shift = norm_backward(grad_ref[...], scaled, inv, vec_ref[0:1].astype(F32))
    out_ref[...] = grad
    low_ref[...] = grad.astype(BF16)
    all_ref[...] = sums_ref[...]
    all_ref[3:4] = grad_gain
    all_ref[4:5] = grad_shift
    all_ref[5:6] = jnp.sum(grad, 0, keepdims=True)


def norm_back(attended, grad, vec, sums):
    total, width = attended.shape
    return pl.pallas_call(
        norm_back_kernel,
        in_specs=[VMEM] * 4,
        out_specs=[VMEM] * 3,
        out_shape=(shape((total, width), F32), shape((total, width), BF16), shape((8, width), F32)),
        input_output_aliases={1: 0},
        compiler_params=params(8),
        cost_estimate=cost(2, 6),
        name="norm_back",
    )(attended, grad, vec, sums)


def attend_back_kernel(words, gw, heads, final, count, info_ref, rows_ref, lt_ref, low_ref, up_ref, acc_ref, *refs):
    pw_ref, pe_ref, ctx_ref = refs[:3]
    pieces, refs = refs[3 : 3 + count], refs[3 + count :]
    if final:
        spans_ref, sums_ref, send_ref, near_ref, pass_ref, words_ref, ents_ref, pos_s, *refs = refs
    else:
        send_ref, near_ref, pass_ref, out_ref, *refs = refs
    (
        w_s, pw_s, pe_s, ctx_s, qw_s, qe_s, k_s, v_s, dc_s, p_s, ds_s, dpw_s, dpe_s, full_s, sem,
    ) = refs
    half = 2 * gw
    total = rows_ref.shape[0]
    size = w_s.shape[0] // 8
    saved = start([(pw_ref, pw_s), (pe_ref, pe_s)], sem.at[0])
    if count == 4:
        reads = start([(v, w_s.at[pl.ds(i * gw, gw)]) for i, v in enumerate(own_parts(*pieces))], sem.at[1])
    else:
        reads = start(place(pieces, info_ref, size, (w_s,)), sem.at[1])
    last = start([(ctx_ref, ctx_s)], sem.at[2])
    wait(saved)
    split_heads(words, gw, heads, pw_s, pe_s, qw_s, qe_s, k_s, v_s)
    wait(reads)
    grad_ctx = mm_nt(low_ref[...], w_s[6 * gw : 7 * gw]).astype(BF16)
    for h in range(heads):
        dc_s[h] = grad_ctx[:, h * HEAD_DIM : (h + 1) * HEAD_DIM]
    wait(last)
    full_s[6 * gw : 7 * gw] = mm_tn(ctx_s[...], low_ref[...]).astype(BF16)
    for h in range(heads):
        o = h * HEAD_DIM
        e = o + HEAD_DIM
        logt = lt_ref[h : h + 1]
        pw = jnp.exp(mm_nt(k_s[h, :words], qw_s[h]) - logt)
        pe = jnp.exp(mm_nt(k_s[h, words:], qe_s[h]) - logt)
        gw_ = mm_nt(v_s[h, :words], dc_s[h])
        ge_ = mm_nt(v_s[h, words:], dc_s[h])
        p_s[:words] = pw.astype(BF16)
        p_s[words:] = pe.astype(BF16)
        dot = jnp.sum(pw * gw_, 0, keepdims=True) + jnp.sum(pe * ge_, 0, keepdims=True)
        ds_s[:words] = (pw * (gw_ - dot)).astype(BF16)
        ds_s[words:] = (pe * (ge_ - dot)).astype(BF16)
        dv = mm(p_s[...], dc_s[h]).astype(BF16)
        dkw = mm(ds_s[:words], qw_s[h]).astype(BF16)
        dke = mm(ds_s[words:], qe_s[h]).astype(BF16)
        dqw = (mm_tn(ds_s[:words], k_s[h, :words]) * SCALE).astype(BF16)
        dqe = (mm_tn(ds_s[words:], k_s[h, words:]) * SCALE).astype(BF16)
        dpw_s[:, o:e] = dqw[:words]
        dpw_s[:, gw + o : gw + e] = dqe[:words]
        dpw_s[:, half + o : half + e] = dkw
        dpw_s[:, half + gw + o : half + gw + e] = dv[:words]
        dpe_s[:, o:e] = dke
        dpe_s[:, gw + o : gw + e] = dv[words:]
        dpe_s[:, half + o : half + e] = dqw[words:]
        dpe_s[:, half + gw + o : half + gw + e] = dqe[words:]
    dpw = dpw_s[...]
    dpe = dpe_s[...]
    rows_w = rows_ref[:words]
    rows_e = rows_ref[words:]
    full_s[:half] = mm_tn(dpw[:, :half], rows_w).astype(BF16)
    full_s[half : 2 * half] = (mm_tn(dpw[:, half:], rows_w) + mm_tn(dpe[:, :half], rows_e)).astype(BF16)
    full_s[2 * half : 3 * half] = mm_tn(dpe[:, half:], rows_e).astype(BF16)
    sw = jnp.sum(dpw.astype(F32), 0, keepdims=True)
    se = jnp.sum(dpe.astype(F32), 0, keepdims=True)
    sum_a = jnp.concatenate([sw[:, :half], sw[:, half:] + se[:, :half]], 1)
    sum_b = jnp.concatenate([se[:, half:], jnp.zeros((1, half), F32)], 1)
    spare = w_s.shape[0] - 7 * gw
    row = lax.broadcasted_iota(jnp.int32, (spare, 2 * half), 0)
    sums = jnp.where(row == 0, sum_a, jnp.where(row == 1, sum_b, jnp.where(row == 2, up_ref[0:1], 0.0)))
    full_s[7 * gw :] = sums.astype(BF16)
    if final:
        grad = acc_ref[words:] + mm(dpe, w_s[half : 3 * half])
        ents_ref[...] = grad
        spans = spans_ref[info_ref[0]]
        begin = spans[:, 0:1]
        end = spans[:, 1:2]
        position = lax.broadcasted_iota(jnp.int32, (total - words, words), 1)
        inside = jnp.where(jnp.logical_and(position >= begin, position < end), 1.0, 0.0).astype(BF16)
        scaled = grad * (1.0 / (end - begin).astype(F32))
        high = scaled.astype(BF16)
        rest = (scaled - high.astype(F32)).astype(BF16)
        pos = (mm_tn(inside, high) + mm_tn(inside, rest)).astype(BF16)
        unit = words // 8
        step = unit + TILE
        for i in range(8):
            pos_s[i * step : i * step + unit] = pos[i * unit : (i + 1) * unit]
            if i:
                pos_s[i * step + unit : (i + 1) * step] = jnp.zeros((TILE, pos.shape[1]), BF16)
        sums = sums_ref[...]
        pos_s[unit:step] = jnp.concatenate([sums, jnp.zeros_like(sums)], 0).astype(BF16)
        sources = [(full_s, size), (pos_s, step)]
        writes = start(blocks_out(sources, info_ref, send_ref, near_ref, pass_ref), sem.at[3])
        words_ref[...] = acc_ref[:words] + mm(dpw, w_s[: 2 * half])
    else:
        writes = start(blocks_out([(full_s, size)], info_ref, send_ref, near_ref, pass_ref), sem.at[3])
        out_ref[:words] = acc_ref[:words] + mm(dpw, w_s[: 2 * half])
        out_ref[words:] = acc_ref[words:] + mm(dpe, w_s[half : 3 * half])
    wait(writes)


def attend_back(info, rows_low, saved, low, up_sums, acc, pieces, words, heads, rows, spans=None, sums=None):
    total, width = rows_low.shape
    pw, pe, ctx, lt = saved
    ents = total - words
    gw = heads * HEAD_DIM
    count = len(pieces)
    final = spans is not None
    extra = words + 8 * TILE
    moved = rows + extra if final else rows
    grads = (shape((words, width), F32), shape((ents, width), F32)) if final else (shape((total, width), F32),)
    return pl.pallas_call(
        partial(attend_back_kernel, words, gw, heads, final, count),
        in_specs=[SMEM] + [VMEM] * 5 + [HBM] * (3 + count) + [VMEM] * (2 * final),
        out_specs=[HBM] * 3 + [VMEM] * len(grads),
        out_shape=(
            far_shape((moved // 2, width), BF16),
            far_shape((moved // 4, width), BF16),
            far_shape((moved // 4, width), BF16),
        )
        + grads,
        scratch_shapes=[pltpu.VMEM((extra, width), BF16)] * final
        + [
            pltpu.VMEM((rows, width), BF16),
            pltpu.VMEM((words, 4 * gw), BF16),
            pltpu.VMEM((ents, 4 * gw), BF16),
            pltpu.VMEM((total, gw), BF16),
        ]
        + [pltpu.VMEM((heads, total, HEAD_DIM), BF16) for _ in range(5)]
        + [
            pltpu.VMEM((total, total), BF16),
            pltpu.VMEM((total, total), BF16),
            pltpu.VMEM((words, 4 * gw), BF16),
            pltpu.VMEM((ents, 4 * gw), BF16),
            pltpu.VMEM((rows, width), BF16),
            DMA((4,)),
        ],
        input_output_aliases={} if final else {5: 3},
        compiler_params=params(24),
        cost_estimate=cost(11, 8),
        name="attend_back",
    )(info, rows_low, lt, low, up_sums, acc, *far((pw, pe, ctx)), *far(pieces), *((spans, sums) if final else ()))


def spread_query_kernel(info_ref, *refs):
    pieces = refs[:8]
    query_ref, key_ref, value_ref, out_ref, qb_ref, vb_ref, ub_ref, s, sem = refs[8:]
    wait(start(place(pieces, info_ref, s.shape[0] // 8, (s,)), sem))
    gw = key_ref.shape[0]
    for i, k in ((0, 0), (1, 1), (2, 4), (3, 5)):
        query_ref[i] = s[k * gw : (k + 1) * gw].astype(F32)
    key_ref[...] = s[2 * gw : 3 * gw].astype(F32)
    value_ref[...] = s[3 * gw : 4 * gw].astype(F32)
    out_ref[...] = s[6 * gw : 7 * gw].astype(F32)
    rows = s[7 * gw : 7 * gw + TILE].astype(F32)
    qb_ref[0:1] = rows[0:1, :gw]
    qb_ref[1:2] = rows[0:1, gw : 2 * gw]
    qb_ref[2:3] = rows[1:2, :gw]
    qb_ref[3:4] = rows[1:2, gw : 2 * gw]
    vb_ref[...] = rows[0:1, 3 * gw :]
    ub_ref[...] = rows[2:3]


def spread_query(info, pieces, gw):
    unit, width = pieces[0].shape
    flat = shape((gw, width), F32)
    return pl.pallas_call(
        spread_query_kernel,
        in_specs=[SMEM] + [HBM] * 8,
        out_specs=[VMEM] * 7,
        out_shape=(
            shape((4, gw, width), F32), flat, flat, flat,
            shape((4, gw), F32), shape((1, gw), F32), shape((1, width), F32),
        ),
        scratch_shapes=[pltpu.VMEM((8 * unit, width), BF16), DMA],
        compiler_params=params(8),
        cost_estimate=cost(0.5, 7),
        name="spread_query",
    )(info, *far(pieces))


def spread_hidden_kernel(info_ref, *refs):
    pieces = refs[:8]
    up_ref, down_ref, up_s, down_s, sem = refs[8:]
    wait(start(place(pieces, info_ref, up_ref.shape[0] // 8, (up_s, down_s)), sem))
    up_ref[...] = up_s[...].astype(F32)
    down_ref[...] = down_s[...].astype(F32)


def spread_hidden(info, pieces):
    rows, width = pieces[0].shape
    out = shape((4 * rows, width), F32)
    return pl.pallas_call(
        spread_hidden_kernel,
        in_specs=[SMEM] + [HBM] * 8,
        out_specs=[VMEM] * 2,
        out_shape=(out, out),
        scratch_shapes=[pltpu.VMEM((4 * rows, width), BF16)] * 2 + [DMA],
        compiler_params=params(9),
        cost_estimate=cost(0.5, 7),
        name="spread_hidden",
    )(info, *far(pieces))


def spread_pos_kernel(info_ref, *refs):
    pieces = refs[:8]
    pos_ref, sums_ref, s, sem = refs[8:]
    step = s.shape[0] // 8
    unit = step - TILE
    wait(start(place(pieces, info_ref, step, (s,)), sem))
    for i in range(8):
        pos_ref[i * unit : (i + 1) * unit] = s[i * step : i * step + unit].astype(F32)
    sums_ref[...] = s[unit:step].astype(F32)[:8]


def spread_pos(info, pieces):
    rows, width = pieces[0].shape
    return pl.pallas_call(
        spread_pos_kernel,
        in_specs=[SMEM] + [HBM] * 8,
        out_specs=[VMEM] * 2,
        out_shape=(shape((8 * (rows - TILE), width), F32), shape((8, width), F32)),
        scratch_shapes=[pltpu.VMEM((8 * rows, width), BF16), DMA],
        compiler_params=params(5),
        cost_estimate=cost(0.5, 3),
        name="spread_pos",
    )(info, *far(pieces))


class Links:
    def __init__(self):
        self.dp = lax.axis_size("dp")
        self.ring = lax.axis_size("tensor")
        dp_index = lax.axis_index("dp")
        self.z = lax.axis_index("tensor")
        self.core = dp_index % 2
        self.bits = (self.dp // 2).bit_length() - 1
        self.bit = [(dp_index // (2 << k)) % 2 for k in range(self.bits)]

    def shift_z(self, v, by):
        n = self.ring
        return lax.ppermute(v, "tensor", [(i, (i + by) % n) for i in range(n)])

    def swap_z(self, v, mask):
        return lax.ppermute(v, "tensor", [(i, i ^ mask) for i in range(self.ring)])

    def swap(self, v, code):
        return lax.ppermute(v, "dp", [(i, i ^ code) for i in range(self.dp)])

    def swap_core(self, v):
        return self.swap(v, 1)

    def first(self, v):
        return lax.ppermute(v, "dp", [(i, i ^ (4 if i % 2 else 2)) for i in range(self.dp)])

    def second(self, v):
        return lax.ppermute(v, "dp", [(i, i ^ (2 if i % 2 else 4)) for i in range(self.dp)])


def after(value, *others):
    return lax.optimization_barrier((value,) + others)[0]


def sync(*values):
    return lax.optimization_barrier(values)


def add_low(*parts):
    total = parts[0].astype(F32)
    for part in parts[1:]:
        total = total + part.astype(F32)
    return total.astype(BF16)


class Blocks:
    def __init__(self, links, send, near, far):
        self.links, self.send, self.near, self.far = links, send, near, far
        self.unit = near.shape[0] // 2

    def one(self):
        return add_low(self.far, self.got[2 * self.unit :])

    def two(self):
        u = self.unit
        return add_low(self.near[u:], self.got[u : 2 * u], self.a[u:])

    def rest(self, low, high, *more):
        value = add_low(self.near[low:high], self.got[low:high], self.a[low:high], self.b[low:high], *more)
        for j in range(2, self.links.bits):
            value = add_low(value, self.links.swap(value, 2 << j))
        return value


def shards(
    word_in,
    entity_in,
    entity_spans,
    word_mask,
    entity_mask,
    pos_table,
    query_w,
    query_b,
    key_w,
    value_w,
    value_b,
    out_w,
    out_b,
    norm1_gain,
    norm1_bias,
    up_w,
    up_b,
    down_w,
    down_b,
    norm2_gain,
    norm2_bias,
    cot_words,
    cot_entities,
):
    links = Links()
    n = links.ring
    z = links.z
    words = cot_words.shape[0]
    ents = cot_entities.shape[0]
    width = word_in.shape[1]
    gw = key_w.shape[1]
    heads = gw // HEAD_DIM
    rows = -(-(7 * gw + 3) // (8 * TILE)) * 8 * TILE
    part = 4 * links.core + 2 * links.bit[0] + links.bit[1]
    info = jnp.stack([z, links.core, part, 2 - links.core]).astype(jnp.int32)

    small = (query_b, value_b[None], up_b[None])
    own = (jnp.swapaxes(query_w, 1, 2), key_w.T, value_w.T, out_w)
    piece_q, piece_f = pack(info, small, own, up_w, down_w, rows)
    first, second, core, shift = links.first, links.second, links.swap_core, links.shift_z
    rows_low, acc = start_rows(info, word_in, entity_in, entity_spans, pos_table, out_b[None], words, ents)
    saved = [None] * n
    biases = [None] * n

    def attend_one(r, acc, pieces, small=()):
        pw, pe, ctx, lt, biases[r], acc = attend(info, rows_low, acc, pieces, words, heads, rows, small)
        saved[r] = (pw, pe, ctx, lt)
        return acc

    v1, v3 = shift(piece_q, 1), shift(piece_q, 3)
    acc, piece_f = sync(acc, piece_f)
    f1, f3 = shift(piece_f, 1), shift(piece_f, 3)
    acc = attend_one(0, acc, own, small)
    acc, v1, v3 = sync(acc, v1, v3)
    a1, b1, v2 = first(v1), second(v1), shift(v1, 1)
    acc, v1, a1, b1, v3, f1, f3 = sync(acc, v1, a1, b1, v3, f1, f3)
    c1, kv, ka, kb, a3, b3 = second(a1), core(v1), core(a1), core(b1), first(v3), second(v3)
    acc, c1, kv, ka, kb, v2, f1, v3 = sync(acc, c1, kv, ka, kb, v2, f1, v3)
    kc, f2 = core(c1), shift(f1, 1)
    acc, kc, a3, b3, v2, f3 = sync(acc, kc, a3, b3, v2, f3)
    group_1 = (v1, a1, b1, c1, kv, ka, kb, kc)

    c3, a2, b2, ag, bg = second(a3), first(v2), second(v2), first(f3), second(f3)
    acc = attend_one(1, acc, group_1)
    acc, c3, a2, b2, ag, bg, f1, f2 = sync(acc, c3, a2, b2, ag, bg, f1, f2)
    kv, ka, kb, kc = core(v3), core(a3), core(b3), core(c3)
    far_f = jnp.concatenate([f1, f2], 0)
    acc, kv, ka, kb, kc, far_f, a2, ag, v2 = sync(acc, kv, ka, kb, kc, far_f, a2, ag, v2)
    group_3 = (v3, a3, b3, c3, kv, ka, kb, kc)

    c2, cg, af, kv, ka = second(a2), second(ag), first(far_f), core(v2), core(a2)
    acc = attend_one(3, acc, group_3)
    acc, c2, cg, af, kv, ka, b2, far_f = sync(acc, c2, cg, af, kv, ka, b2, far_f)
    kb, kc = core(b2), core(c2)
    acc, kb, kc, far_f, af, f3, ag, bg = sync(acc, kb, kc, far_f, af, f3, ag, bg)
    group_2 = (v2, a2, b2, c2, kv, ka, kb, kc)

    bf, cf, kv_g, ka_g, kb_g = second(far_f), second(af), core(f3), core(ag), core(bg)
    acc = attend_one(2, acc, group_2)
    acc, bf, cf, kv_g, ka_g, kb_g, cg, af, far_f = sync(acc, bf, cf, kv_g, ka_g, kb_g, cg, af, far_f)
    attended = acc
    ffn_pieces = (
        far_f, af, bf, cf, core(far_f), core(af), core(bf), core(cf), f3, ag, bg, cg, kv_g, ka_g, kb_g, core(cg)
    )
    query_groups = (own, group_1, group_2, group_3)

    vec = jnp.stack([norm1_gain, norm1_bias, down_b, norm2_gain, norm2_bias] + [down_b] * 3)
    normed_t, act_t, slope, up, down, out_words, out_ents, mixed_low, acc, sums = hidden(
        info, attended, vec, word_mask, entity_mask, cot_words, cot_entities, biases, (up_w, down_w), ffn_pieces
    )

    size = width // 4
    unit = rows // 8
    up_sums = [None] * n

    def ffn_blocks(group, acc):
        send, near, rest, acc, up_sum = hidden_back(info, group, mixed_low, act_t, slope, normed_t, up, down, acc)
        for k, r in enumerate(group):
            up_sums[r] = up_sum[8 * k : 8 * k + 8]
        return Blocks(links, send, near, rest), acc

    def back(r, acc, *last):
        send, near, rest, *acc = attend_back(
            info, rows_low, saved[r], attended_low, up_sums[r], acc, query_groups[r], words, heads, rows, *last
        )
        return Blocks(links, send, near, rest), *acc

    fa, acc = ffn_blocks((2, 1), acc)
    fa.got = core(fa.send)
    fb, acc = ffn_blocks((3, 0), acc)
    acc, fa.got = sync(acc, fa.got)
    acc, one_a = sync(acc, fa.one())

    fa.a, fb.got = first(one_a), core(fb.send)
    acc, attended_low, sums = norm_back(attended, acc, vec, sums)
    acc, fb.got = sync(acc, fb.got)
    acc, one_b = sync(acc, fb.one())

    fb.a = first(one_b)
    q1, acc = back(2, acc)
    acc, q1.send, fa.a, fb.a = sync(acc, q1.send, fa.a, fb.a)
    q1.got = core(q1.send)
    acc, two_a, two_b, q1.got = sync(acc, fa.two(), fb.two(), q1.got)
    acc, one_1 = sync(acc, q1.one())

    fa.b, fb.b, q1.a = second(two_a), second(two_b), first(one_1)
    q2, acc = back(1, acc)
    acc, q2.send, fa.b, fb.b, q1.a = sync(acc, q2.send, fa.b, fb.b, q1.a)
    q2.got = core(q2.send)
    acc, r2, r3, two_1, q2.got = sync(acc, fa.rest(0, size), fb.rest(0, size), q1.two(), q2.got)
    acc, one_2 = sync(acc, q2.one())

    z2, z3, q1.b, q2.a = shift(r2, -1), shift(r3, -3), second(two_1), first(one_2)
    q3, acc = back(3, acc)
    acc, q3.send, z2, z3, q1.b, q2.a = sync(acc, q3.send, z2, z3, q1.b, q2.a)
    q3.got = core(q3.send)
    acc, r1, value_2, two_2, q3.got = sync(acc, fa.rest(size, 2 * size, z2), q1.rest(0, unit), q2.two(), q3.got)
    acc, one_3 = sync(acc, q3.one())

    z1, y2, q2.b, q3.a = shift(r1, -1), shift(value_2, -1), second(two_2), first(one_3)
    q4, grad_words, grad_ents = back(0, acc, entity_spans, sums)
    q4.send, z1, y2, q2.b, q3.a = sync(q4.send, z1, y2, q2.b, q3.a)

    q4.got = core(q4.send)
    y1, q3.b = shift(q2.rest(0, unit, y2), -1), second(q3.two())
    own_f = fb.rest(size, 2 * size, z1, z3)
    q4.a, ga = first(q4.one()), first(own_f)
    q4.a, q3.b, y1, ga, own_f = sync(q4.a, q3.b, y1, ga, own_f)

    q4.b, y3, gb, gc = second(q4.two()), shift(q3.rest(0, unit), -3), second(own_f), second(ga)
    q4.b, y3, gb, gc, own_f, ga = sync(q4.b, y3, gb, gc, own_f, ga)

    pos = q4.rest(unit, q4.unit)
    own_q = q4.rest(0, unit, y1, y3)
    p1, p2, p3 = (links.swap_z(pos, mask) for mask in (1, 2, 3))
    qa, qb = first(own_q), second(own_q)
    p1, p2, p3, qa, qb, own_q, pos, own_f, ga, gb, gc = sync(p1, p2, p3, qa, qb, own_q, pos, own_f, ga, gb, gc)

    pos = ((pos.astype(F32) + p1.astype(F32)) + (p2.astype(F32) + p3.astype(F32))).astype(BF16)
    pa, pb, qc, kf, kg = first(pos), second(pos), second(qa), core(own_f), core(ga)
    pa, pb, qc, kf, kg, pos, own_q, qa, qb, gb, gc = sync(pa, pb, qc, kf, kg, pos, own_q, qa, qb, gb, gc)
    pc, kh, ki, kv, ka = second(pa), core(gb), core(gc), core(own_q), core(qa)
    pc, kh, ki, kv, ka, qb, qc, pos, pa, pb = sync(pc, kh, ki, kv, ka, qb, qc, pos, pa, pb)
    kb, kc = core(qb), core(qc)
    kp = tuple(core(v) for v in (pos, pa, pb, pc))
    grad_up, grad_down = spread_hidden(info, (own_f, ga, gb, gc, kf, kg, kh, ki))
    kb, kc, grad_up, grad_down, *kp = sync(kb, kc, grad_up, grad_down, *kp)
    grad_query_t, grad_key_t, grad_value_t, grad_out, grad_query_b, grad_value_b, grad_up_b = spread_query(
        info, (own_q, qa, qb, qc, kv, ka, kb, kc), gw
    )
    pos_sum, total_sums = spread_pos(info, (pos, pa, pb, pc, *kp))
    return (
        out_words,
        out_ents,
        grad_words,
        grad_ents,
        pos_sum,
        jnp.swapaxes(grad_query_t, 1, 2),
        grad_query_b,
        grad_key_t.T,
        grad_value_t.T,
        grad_value_b[0],
        grad_out,
        total_sums[5],
        total_sums[3],
        total_sums[4],
        grad_up,
        grad_up_b[0],
        grad_down,
        total_sums[2],
        total_sums[0],
        total_sums[1],
    )


def solution(mesh):
    rows = P(("dp", "tensor"), None)
    last = P(None, "tensor")
    placed = (
        P("dp", None),
        P("dp", None),
        P("dp", None, None),
        P("dp", None),
        P("dp", None),
        P(),
        P(None, None, "tensor"),
        last,
        last,
        last,
        P("tensor"),
        P("tensor", None),
        P(),
        P(),
        P(),
        last,
        P("tensor"),
        P("tensor", None),
        P(),
        P(),
        P(),
        rows,
        rows,
    )
    return jax.shard_map(
        shards,
        mesh=mesh,
        in_specs=placed,
        out_specs=(
            rows,
            rows,
            rows,
            rows,
            P(),
            P(None, None, "tensor"),
            last,
            last,
            last,
            P("tensor"),
            P("tensor", None),
            P(),
            P(),
            P(),
            last,
            P("tensor"),
            P("tensor", None),
            P(),
            P(),
            P(),
        ),
        check_vma=False,
    )
```

```python
from functools import partial

import jax
import jax.numpy as jnp
from jax import lax
from jax.experimental import pallas as pl
from jax.experimental.pallas import tpu as pltpu
from jax.sharding import PartitionSpec as P

HEAD_DIM = 64
SCALE = HEAD_DIM**-0.5
norm_epsilon = 1e-12
F32 = jnp.float32
BF16 = jnp.bfloat16
NT = (((1,), (1,)), ((), ()))
TN = (((0,), (0,)), ((), ()))
ERFC_STEP = 0.35
ERFC_POLY = (
    0.1396196249207051,
    0.13989555693599826,
    0.11957015144655456,
    0.10661400019997494,
    -0.025870835326937874,
    0.16337919550284652,
    -0.25954764983005574,
    0.14589250699009862,
    -0.029552569422939476,
)
TILE = 16
VMEM = pl.BlockSpec(memory_space=pltpu.VMEM)
SMEM = pl.BlockSpec(memory_space=pltpu.SMEM)
HBM = pl.BlockSpec(memory_space=pltpu.HBM)
DMA = pltpu.SemaphoreType.DMA


def mm(a, b):
    return jnp.dot(a, b, preferred_element_type=F32)


def mm_nt(a, b):
    return lax.dot_general(a, b, NT, preferred_element_type=F32)


def mm_tn(a, b):
    return lax.dot_general(a, b, TN, preferred_element_type=F32)


def params(mib):
    return pltpu.CompilerParams(vmem_limit_bytes=mib << 20)


def cost(gflop, mbytes):
    return pl.CostEstimate(
        flops=int(gflop * 1e9), bytes_accessed=int(mbytes * 1e6), transcendentals=0
    )


def shape(dims, kind):
    return jax.ShapeDtypeStruct(dims, kind)


def far(values):
    return tuple(pltpu.with_memory_space_constraint(v, pltpu.HBM) for v in values)


def far_shape(dims, kind):
    return pltpu.HBM(dims, kind)


def start(pairs, sem):
    copies = [pltpu.make_async_copy(source, target, sem) for source, target in pairs]
    for copy in copies:
        copy.start()
    return copies


def wait(copies):
    for copy in copies:
        copy.wait()


def rows_at(first, size):
    return pl.ds(pl.multiple_of(first, TILE), size)


def place(pieces, info_ref, unit, targets, skip=0):
    part, first = info_ref[2], info_ref[3]
    second = 3 - first
    pairs = []
    for piece, code in zip(pieces, (0, first, second, 3, 4, 4 + second, 4 + first, 7)):
        row = lax.bitwise_xor(part, jnp.int32(code)) * unit
        ref, begin = piece if isinstance(piece, tuple) else (piece, skip)
        for t, target in enumerate(targets):
            pairs.append((ref.at[pl.ds(begin + t * unit, unit)], target.at[rows_at(row, unit)]))
    return pairs


def blocks_out(sources, info_ref, send_ref, near_ref, pass_ref):
    part, first = info_ref[2], info_ref[3]
    second = 3 - first
    keep = (0, second, first, 3)
    send = (4, 4 + first, 4 + second, 7)
    total = sum(unit for _, unit in sources)
    pairs = []
    for i in range(4):
        done = 0
        for source, unit in sources:
            other = lax.bitwise_xor(part, jnp.int32(send[i])) * unit
            mine = lax.bitwise_xor(part, jnp.int32(keep[i])) * unit
            to = near_ref if i < 2 else pass_ref
            pairs.append((source.at[rows_at(other, unit)], send_ref.at[pl.ds(i * total + done, unit)]))
            pairs.append((source.at[rows_at(mine, unit)], to.at[pl.ds((i % 2) * total + done, unit)]))
            done += unit
    return pairs


def own_parts(query_ref, key_ref, value_ref, out_ref):
    return (query_ref.at[0], query_ref.at[1], key_ref, value_ref, query_ref.at[2], query_ref.at[3], out_ref)


def spare_rows(qb_ref, vb_ref, ub_ref, spare):
    qb = qb_ref[...].astype(F32)
    none = jnp.zeros((1, qb.shape[1]), F32)
    first = jnp.concatenate([qb[0:1], qb[1:2], none, vb_ref[...].astype(F32)], 1)
    second = jnp.concatenate([qb[2:3], qb[3:4], none, none], 1)
    row = lax.broadcasted_iota(jnp.int32, (spare, first.shape[1]), 0)
    rows = jnp.where(row == 0, first, jnp.where(row == 1, second, jnp.where(row == 2, ub_ref[...].astype(F32), 0.0)))
    return rows.astype(BF16)


def pack_kernel(
    gw, info_ref, qb_ref, vb_ref, ub_ref, query_ref, key_ref, value_ref, ow_ref, up_ref, down_ref,
    piece_ref, ffn_ref, w_s, f_s, sem,
):
    part = info_ref[2]
    size = piece_ref.shape[0]
    low = lax.div(part * size, jnp.int32(gw))
    copies = []
    for i, ref in enumerate(own_parts(query_ref, key_ref, value_ref, ow_ref)):
        needed = jnp.logical_or(low == i, low + 1 == i)
        copies.append((needed, pltpu.make_async_copy(ref, w_s.at[pl.ds(i * gw, gw)], sem.at[0])))
    for needed, copy in copies:
        pl.when(needed)(copy.start)
    unit = f_s.shape[0] // 2
    ffn = start(
        [(v.at[rows_at(part * unit, unit)], f_s.at[pl.ds(i * unit, unit)]) for i, v in enumerate((up_ref, down_ref))],
        sem.at[1],
    )
    w_s[7 * gw :] = spare_rows(qb_ref, vb_ref, ub_ref, w_s.shape[0] - 7 * gw)
    for needed, copy in copies:
        pl.when(needed)(copy.wait)
    piece = start([(w_s.at[rows_at(part * size, size)], piece_ref)], sem.at[2])
    wait(ffn)
    last = start([(f_s, ffn_ref)], sem.at[3])
    wait(piece)
    wait(last)


def pack(info, biases, own, up_w, down_w, rows):
    gw, width = own[1].shape
    unit = up_w.shape[0] // 8
    return pl.pallas_call(
        partial(pack_kernel, gw),
        in_specs=[SMEM] + [VMEM] * 3 + [HBM] * 6,
        out_specs=[HBM] * 2,
        out_shape=(far_shape((rows // 8, width), BF16), far_shape((2 * unit, width), BF16)),
        scratch_shapes=[pltpu.VMEM((rows, width), BF16), pltpu.VMEM((2 * unit, width), BF16), DMA((4,))],
        compiler_params=params(4),
        cost_estimate=cost(0.01, 3),
        name="pack",
    )(info, *biases, *far(own + (up_w, down_w)))


def start_kernel(info_ref, words_ref, ents_ref, spans_ref, table_ref, bias_ref, low_ref, resid_ref, w_s, e_s, t_s, sem):
    words, count = w_s.shape[0], e_s.shape[0]
    z = info_ref[0]
    ents = start(
        [(ents_ref.at[rows_at(z * count, count)], e_s), (table_ref, t_s)],
        sem.at[0],
    )
    reads = start([(words_ref.at[rows_at(z * words, words)], w_s)], sem.at[1])
    spans = spans_ref[z]
    begin = spans[:, 0:1]
    end = spans[:, 1:2]
    position = lax.broadcasted_iota(jnp.int32, (count, words), 1)
    inside = jnp.where(jnp.logical_and(position >= begin, position < end), 1.0, 0.0).astype(BF16)
    share = 1.0 / (end - begin).astype(F32)
    out_b = bias_ref[...].astype(F32)
    wait(ents)
    rows = e_s[...].astype(F32) + mm(inside, t_s[...]) * share
    low_ref[words:] = rows.astype(BF16)
    resid_ref[words:] = rows + out_b
    wait(reads)
    low_ref[:words] = w_s[...]
    resid_ref[:words] = w_s[...].astype(F32) + out_b


def start_rows(info, word_in, entity_in, spans, table, out_b, words, ents):
    width = word_in.shape[1]
    total = words + ents
    return pl.pallas_call(
        start_kernel,
        in_specs=[SMEM, HBM, HBM, VMEM, HBM, VMEM],
        out_specs=[VMEM] * 2,
        out_shape=(shape((total, width), BF16), shape((total, width), F32)),
        scratch_shapes=[
            pltpu.VMEM((words, width), BF16),
            pltpu.VMEM((ents, width), BF16),
            pltpu.VMEM(table.shape, BF16),
            DMA((2,)),
        ],
        compiler_params=params(6),
        cost_estimate=cost(0.5, 6),
        name="start_rows",
    )(info, *far((word_in, entity_in)), spans, *far((table,)), out_b)


def split_heads(words, gw, heads, pw_ref, pe_ref, qw_s, qe_s, k_s, v_s):
    half = 2 * gw
    for h in range(heads):
        o = h * HEAD_DIM
        e = o + HEAD_DIM
        qw_s[h, :words] = pw_ref[:, o:e] * SCALE
        qw_s[h, words:] = pe_ref[:, half + o : half + e] * SCALE
        qe_s[h, :words] = pw_ref[:, gw + o : gw + e] * SCALE
        qe_s[h, words:] = pe_ref[:, half + gw + o : half + gw + e] * SCALE
        k_s[h, :words] = pw_ref[:, half + o : half + e]
        k_s[h, words:] = pe_ref[:, o:e]
        v_s[h, :words] = pw_ref[:, half + gw + o : half + gw + e]
        v_s[h, words:] = pe_ref[:, gw + o : gw + e]


def attend_kernel(words, gw, heads, count, info_ref, rows_ref, acc_ref, *refs):
    own = count == 4
    small, refs = (refs[:3], refs[3:]) if own else ((), refs)
    pieces = refs[:count]
    pw_ref, pe_ref, ctx_ref, lt_ref, bias_ref, out_ref, w_s, pw_s, pe_s, ctx_s, qw_s, qe_s, k_s, v_s, sem = refs[count:]
    half = 2 * gw
    if own:
        reads = start([(v, w_s.at[pl.ds(i * gw, gw)]) for i, v in enumerate(own_parts(*pieces))], sem.at[0])
        w_s[7 * gw :] = spare_rows(*small, w_s.shape[0] - 7 * gw)
        wait(reads)
    else:
        wait(start(place(pieces, info_ref, w_s.shape[0] // 8, (w_s,)), sem.at[0]))
    rows_b = w_s[7 * gw : 7 * gw + TILE]
    bias_ref[...] = rows_b
    rows_b = rows_b.astype(F32)
    bias_e = jnp.concatenate([rows_b[0:1, half:], rows_b[1:2, :half]], 1)
    pw_s[...] = (mm_nt(rows_ref[:words], w_s[: 4 * gw]) + rows_b[0:1]).astype(BF16)
    pe_s[...] = (mm_nt(rows_ref[words:], w_s[half : 6 * gw]) + bias_e).astype(BF16)
    saves = start([(pw_s, pw_ref), (pe_s, pe_ref)], sem.at[1])
    split_heads(words, gw, heads, pw_s, pe_s, qw_s, qe_s, k_s, v_s)
    block = 128

    def step(qb, carry):
        rows = pl.ds(pl.multiple_of(qb * block, block), block)
        parts = []
        for h in range(heads):
            sw = mm_nt(qw_s[h, rows], k_s[h, :words])
            se = mm_nt(qe_s[h, rows], k_s[h, words:])
            top = jnp.maximum(jnp.max(sw, 1, keepdims=True), jnp.max(se, 1, keepdims=True))
            ew = jnp.exp(sw - top)
            ee = jnp.exp(se - top)
            total = jnp.sum(ew, 1, keepdims=True) + jnp.sum(ee, 1, keepdims=True)
            parts.append(
                (mm(ew.astype(BF16), v_s[h, :words]) + mm(ee.astype(BF16), v_s[h, words:])) * (1.0 / total)
            )
            logt = top + jnp.log(total)
            lt_ref[h : h + 1, rows] = jnp.broadcast_to(logt, (block, block)).T[0:1]
        ctx_s[rows, :] = jnp.concatenate(parts, 1).astype(BF16)
        return carry

    lax.fori_loop(0, rows_ref.shape[0] // block, step, 0, unroll=True)
    last = start([(ctx_s, ctx_ref)], sem.at[2])
    out_ref[...] = acc_ref[...] + mm(ctx_s[...], w_s[6 * gw : 7 * gw])
    wait(saves)
    wait(last)


def attend(info, rows_low, acc, pieces, words, heads, rows, small=()):
    total, width = rows_low.shape
    ents = total - words
    gw = heads * HEAD_DIM
    count = len(pieces)
    return pl.pallas_call(
        partial(attend_kernel, words, gw, heads, count),
        in_specs=[SMEM] + [VMEM] * (2 + len(small)) + [HBM] * count,
        out_specs=[HBM] * 3 + [VMEM] * 3,
        out_shape=(
            far_shape((words, 4 * gw), BF16),
            far_shape((ents, 4 * gw), BF16),
            far_shape((total, gw), BF16),
            shape((8, total), F32),
            shape((TILE, width), BF16),
            shape((total, width), F32),
        ),
        scratch_shapes=[
            pltpu.VMEM((rows, width), BF16),
            pltpu.VMEM((words, 4 * gw), BF16),
            pltpu.VMEM((ents, 4 * gw), BF16),
            pltpu.VMEM((total, gw), BF16),
        ]
        + [pltpu.VMEM((heads, total, HEAD_DIM), BF16) for _ in range(4)]
        + [DMA((3,))],
        input_output_aliases={2: 5},
        compiler_params=params(16),
        cost_estimate=cost(8, 6),
        name="attend_own" if small else "attend_far",
    )(info, rows_low, acc, *small, *far(pieces))


def gelu_pair(x):
    size = jnp.abs(x)
    t = 1.0 / (1.0 + ERFC_STEP * size)
    poly = jnp.full_like(x, ERFC_POLY[-1])
    for c in ERFC_POLY[-2::-1]:
        poly = poly * t + c
    bell = jnp.exp(x * x * -0.5)
    tail = poly * t * bell
    below = jnp.where(x >= 0, 1.0 - tail, tail)
    return x * below, below + x * (bell * 0.3989422804014327)


def norm_parts(values):
    centered = values - jnp.mean(values, 1, keepdims=True)
    inv = lax.rsqrt(jnp.mean(centered * centered, 1, keepdims=True) + norm_epsilon)
    return centered * inv, inv


def hidden_kernel(n, info_ref, attended_ref, vec_ref, wm_ref, em_ref, cw_ref, ce_ref, *refs):
    bias_refs, refs = refs[:n], refs[n:]
    up_own, down_own = refs[:2]
    pieces, refs = (refs[2:10], refs[10:18]), refs[18:]
    turn_ref, at_ref, slope_ref, up_s, down_s, ow_ref, oe_ref, mixed_ref, grad_ref, sums_ref, low_ref, acc_s, b_s, sem = refs
    total, width = attended_ref.shape
    unit = width // 8
    reads = [start([(up_own, up_s.at[0]), (down_own, down_s.at[0])], sem.at[0])]
    for r in range(1, n):
        held, skip = pieces[r // 3], 2 * unit * ((r - 1) % 2)
        reads.append(start(place(held, info_ref, unit, (up_s.at[r], down_s.at[r]), skip), sem.at[r]))
    for r in range(n):
        b_s[r] = bias_refs[r][2:3].astype(F32)
    scaled, _ = norm_parts(attended_ref[...])
    normed = scaled * vec_ref[0:1].astype(F32) + vec_ref[1:2].astype(F32)
    low = normed.astype(BF16)
    low_ref[...] = low
    turn_ref[...] = low.T
    acc_s[...] = normed + vec_ref[2:3].astype(F32)
    block = 128

    def group(r):
        for lo in range(0, total, block):
            pre = mm(low_ref[lo : lo + block], up_s[r]) + b_s[r]
            value, slope = gelu_pair(pre)
            slope_ref[r, lo : lo + block] = slope
            value = value.astype(BF16)
            at_ref[r, :, lo : lo + block] = value.T
            acc_s[lo : lo + block] += mm(value, down_s[r])

    for r in range(n):
        wait(reads[r])
        group(r)

    words = cw_ref.shape[0]
    z = info_ref[0]
    scaled, inv = norm_parts(acc_s[...])
    gain = vec_ref[3:4].astype(F32)
    output = scaled * gain + vec_ref[4:5].astype(F32)
    ow_ref[...] = output[:words].astype(BF16)
    oe_ref[...] = output[words:].astype(BF16)

    def column(ref, size):
        return jnp.broadcast_to(ref[pl.ds(z, 1), :].astype(F32), (128, size)).T[:, 0:1]

    cot = jnp.concatenate(
        [
            column(wm_ref, words) * cw_ref[...].astype(F32),
            column(em_ref, total - words) * ce_ref[...].astype(F32),
        ],
        0,
    )
    grad, grad_gain, grad_shift = norm_backward(cot, scaled, inv, gain)
    grad_ref[...] = grad
    mixed_ref[...] = grad.astype(BF16)
    sums_ref[0:1] = grad_gain
    sums_ref[1:2] = grad_shift
    sums_ref[2:3] = jnp.sum(grad, 0, keepdims=True)
    sums_ref[3:] = jnp.zeros((5, width), F32)


def hidden(info, attended, vec, word_mask, entity_mask, cot_words, cot_ents, biases, own, pieces):
    total, width = attended.shape
    n = len(biases)
    return pl.pallas_call(
        partial(hidden_kernel, n),
        in_specs=[SMEM] + [VMEM] * (6 + n) + [HBM] * (2 + len(pieces)),
        out_specs=[VMEM] * 10,
        out_shape=(
            shape((width, total), BF16),
            shape((n, width, total), BF16),
            shape((n, total, width), F32),
            shape((n, width, width), BF16),
            shape((n, width, width), BF16),
            shape(cot_words.shape, BF16),
            shape(cot_ents.shape, BF16),
            shape((total, width), BF16),
            shape((total, width), F32),
            shape((8, width), F32),
        ),
        scratch_shapes=[
            pltpu.VMEM((total, width), BF16),
            pltpu.VMEM((total, width), F32),
            pltpu.VMEM((n, 1, width), F32),
            DMA((n,)),
        ],
        compiler_params=params(18),
        cost_estimate=cost(22, 20),
        name="hidden",
    )(info, attended, vec, word_mask, entity_mask, cot_words, cot_ents, *biases, *far(own), *far(pieces))


def norm_backward(grad_in, scaled, inv_std, gain_row):
    grad_gain = jnp.sum(grad_in * scaled, axis=0, keepdims=True)
    grad_shift = jnp.sum(grad_in, axis=0, keepdims=True)
    grad_scaled = grad_in * gain_row
    mean_first = jnp.mean(grad_scaled, axis=1, keepdims=True)
    mean_second = jnp.mean(grad_scaled * scaled, axis=1, keepdims=True)
    return inv_std * (grad_scaled - mean_first - scaled * mean_second), grad_gain, grad_shift


def hidden_back_kernel(
    pair, info_ref, low_ref, at_ref, slope_ref, turn_ref, up_ref, down_ref, acc_ref,
    send_ref, near_ref, pass_ref, out_ref, b_ref, *refs,
):
    full, sem = refs[:-1], refs[-1]
    unit = turn_ref.shape[0] // 8
    low = low_ref[...]
    out_ref[...] = acc_ref[...]
    for k, r in enumerate(pair):
        grad_down = mm(at_ref[r], low).astype(BF16)
        for i in range(8):
            full[k][(2 * i + 1) * unit : (2 * i + 2) * unit] = grad_down[i * unit : (i + 1) * unit]
        pre_low = (mm_nt(low, down_ref[r]) * slope_ref[r]).astype(BF16)
        grad_up = mm(turn_ref[...], pre_low).astype(BF16)
        for i in range(8):
            full[k][2 * i * unit : (2 * i + 1) * unit] = grad_up[i * unit : (i + 1) * unit]
        b_ref[8 * k : 8 * k + 8] = jnp.broadcast_to(jnp.sum(pre_low.astype(F32), 0, keepdims=True), (8, b_ref.shape[1]))
        out_ref[...] += mm_nt(pre_low, up_ref[r])
    wait(start(blocks_out([(f, 2 * unit) for f in full], info_ref, send_ref, near_ref, pass_ref), sem))


def hidden_back(info, pair, mixed_low, act_t, slope, normed_t, up, down, acc):
    total, width = mixed_low.shape
    k = len(pair)
    return pl.pallas_call(
        partial(hidden_back_kernel, pair),
        in_specs=[SMEM] + [VMEM] * 7,
        out_specs=[HBM] * 3 + [VMEM] * 2,
        out_shape=(
            far_shape((k * width, width), BF16),
            far_shape((k * width // 2, width), BF16),
            far_shape((k * width // 2, width), BF16),
            shape((total, width), F32),
            shape((8 * k, width), F32),
        ),
        scratch_shapes=[pltpu.VMEM((2 * width, width), BF16) for _ in pair] + [DMA],
        input_output_aliases={7: 3},
        compiler_params=params(12),
        cost_estimate=cost(7 * k, 8 * k),
        name="hidden_back",
    )(info, mixed_low, act_t, slope, normed_t, up, down, acc)


def norm_back_kernel(attended_ref, grad_ref, vec_ref, sums_ref, out_ref, low_ref, all_ref):
    scaled, inv = norm_parts(attended_ref[...])
    grad, grad_gain, grad_shift = norm_backward(grad_ref[...], scaled, inv, vec_ref[0:1].astype(F32))
    out_ref[...] = grad
    low_ref[...] = grad.astype(BF16)
    all_ref[...] = sums_ref[...]
    all_ref[3:4] = grad_gain
    all_ref[4:5] = grad_shift
    all_ref[5:6] = jnp.sum(grad, 0, keepdims=True)


def norm_back(attended, grad, vec, sums):
    total, width = attended.shape
    return pl.pallas_call(
        norm_back_kernel,
        in_specs=[VMEM] * 4,
        out_specs=[VMEM] * 3,
        out_shape=(shape((total, width), F32), shape((total, width), BF16), shape((8, width), F32)),
        input_output_aliases={1: 0},
        compiler_params=params(8),
        cost_estimate=cost(2, 6),
        name="norm_back",
    )(attended, grad, vec, sums)


def attend_back_kernel(words, gw, heads, final, count, info_ref, rows_ref, lt_ref, low_ref, up_ref, acc_ref, *refs):
    pw_ref, pe_ref, ctx_ref = refs[:3]
    pieces, refs = refs[3 : 3 + count], refs[3 + count :]
    if final:
        spans_ref, sums_ref, send_ref, near_ref, pass_ref, words_ref, ents_ref, pos_s, *refs = refs
    else:
        send_ref, near_ref, pass_ref, out_ref, *refs = refs
    (
        w_s, pw_s, pe_s, ctx_s, qw_s, qe_s, k_s, v_s, dc_s, p_s, ds_s, dpw_s, dpe_s, full_s, sem,
    ) = refs
    half = 2 * gw
    total = rows_ref.shape[0]
    size = w_s.shape[0] // 8
    saved = start([(pw_ref, pw_s), (pe_ref, pe_s)], sem.at[0])
    if count == 4:
        reads = start([(v, w_s.at[pl.ds(i * gw, gw)]) for i, v in enumerate(own_parts(*pieces))], sem.at[1])
    else:
        reads = start(place(pieces, info_ref, size, (w_s,)), sem.at[1])
    last = start([(ctx_ref, ctx_s)], sem.at[2])
    wait(saved)
    split_heads(words, gw, heads, pw_s, pe_s, qw_s, qe_s, k_s, v_s)
    wait(reads)
    grad_ctx = mm_nt(low_ref[...], w_s[6 * gw : 7 * gw]).astype(BF16)
    for h in range(heads):
        dc_s[h] = grad_ctx[:, h * HEAD_DIM : (h + 1) * HEAD_DIM]
    wait(last)
    full_s[6 * gw : 7 * gw] = mm_tn(ctx_s[...], low_ref[...]).astype(BF16)
    for h in range(heads):
        o = h * HEAD_DIM
        e = o + HEAD_DIM
        logt = lt_ref[h : h + 1]
        pw = jnp.exp(mm_nt(k_s[h, :words], qw_s[h]) - logt)
        pe = jnp.exp(mm_nt(k_s[h, words:], qe_s[h]) - logt)
        gw_ = mm_nt(v_s[h, :words], dc_s[h])
        ge_ = mm_nt(v_s[h, words:], dc_s[h])
        p_s[:words] = pw.astype(BF16)
        p_s[words:] = pe.astype(BF16)
        dot = jnp.sum(pw * gw_, 0, keepdims=True) + jnp.sum(pe * ge_, 0, keepdims=True)
        ds_s[:words] = (pw * (gw_ - dot)).astype(BF16)
        ds_s[words:] = (pe * (ge_ - dot)).astype(BF16)
        dv = mm(p_s[...], dc_s[h]).astype(BF16)
        dkw = mm(ds_s[:words], qw_s[h]).astype(BF16)
        dke = mm(ds_s[words:], qe_s[h]).astype(BF16)
        dqw = (mm_tn(ds_s[:words], k_s[h, :words]) * SCALE).astype(BF16)
        dqe = (mm_tn(ds_s[words:], k_s[h, words:]) * SCALE).astype(BF16)
        dpw_s[:, o:e] = dqw[:words]
        dpw_s[:, gw + o : gw + e] = dqe[:words]
        dpw_s[:, half + o : half + e] = dkw
        dpw_s[:, half + gw + o : half + gw + e] = dv[:words]
        dpe_s[:, o:e] = dke
        dpe_s[:, gw + o : gw + e] = dv[words:]
        dpe_s[:, half + o : half + e] = dqw[words:]
        dpe_s[:, half + gw + o : half + gw + e] = dqe[words:]
    dpw = dpw_s[...]
    dpe = dpe_s[...]
    rows_w = rows_ref[:words]
    rows_e = rows_ref[words:]
    full_s[:half] = mm_tn(dpw[:, :half], rows_w).astype(BF16)
    full_s[half : 2 * half] = (mm_tn(dpw[:, half:], rows_w) + mm_tn(dpe[:, :half], rows_e)).astype(BF16)
    full_s[2 * half : 3 * half] = mm_tn(dpe[:, half:], rows_e).astype(BF16)
    sw = jnp.sum(dpw.astype(F32), 0, keepdims=True)
    se = jnp.sum(dpe.astype(F32), 0, keepdims=True)
    sum_a = jnp.concatenate([sw[:, :half], sw[:, half:] + se[:, :half]], 1)
    sum_b = jnp.concatenate([se[:, half:], jnp.zeros((1, half), F32)], 1)
    spare = w_s.shape[0] - 7 * gw
    row = lax.broadcasted_iota(jnp.int32, (spare, 2 * half), 0)
    sums = jnp.where(row == 0, sum_a, jnp.where(row == 1, sum_b, jnp.where(row == 2, up_ref[0:1], 0.0)))
    full_s[7 * gw :] = sums.astype(BF16)
    if final:
        grad = acc_ref[words:] + mm(dpe, w_s[half : 3 * half])
        ents_ref[...] = grad
        spans = spans_ref[info_ref[0]]
        begin = spans[:, 0:1]
        end = spans[:, 1:2]
        position = lax.broadcasted_iota(jnp.int32, (total - words, words), 1)
        inside = jnp.where(jnp.logical_and(position >= begin, position < end), 1.0, 0.0).astype(BF16)
        scaled = grad * (1.0 / (end - begin).astype(F32))
        high = scaled.astype(BF16)
        rest = (scaled - high.astype(F32)).astype(BF16)
        pos = (mm_tn(inside, high) + mm_tn(inside, rest)).astype(BF16)
        unit = words // 8
        step = unit + TILE
        for i in range(8):
            pos_s[i * step : i * step + unit] = pos[i * unit : (i + 1) * unit]
            if i:
                pos_s[i * step + unit : (i + 1) * step] = jnp.zeros((TILE, pos.shape[1]), BF16)
        sums = sums_ref[...]
        pos_s[unit:step] = jnp.concatenate([sums, jnp.zeros_like(sums)], 0).astype(BF16)
        sources = [(full_s, size), (pos_s, step)]
        writes = start(blocks_out(sources, info_ref, send_ref, near_ref, pass_ref), sem.at[3])
        words_ref[...] = acc_ref[:words] + mm(dpw, w_s[: 2 * half])
    else:
        writes = start(blocks_out([(full_s, size)], info_ref, send_ref, near_ref, pass_ref), sem.at[3])
        out_ref[:words] = acc_ref[:words] + mm(dpw, w_s[: 2 * half])
        out_ref[words:] = acc_ref[words:] + mm(dpe, w_s[half : 3 * half])
    wait(writes)


def attend_back(info, rows_low, saved, low, up_sums, acc, pieces, words, heads, rows, spans=None, sums=None):
    total, width = rows_low.shape
    pw, pe, ctx, lt = saved
    ents = total - words
    gw = heads * HEAD_DIM
    count = len(pieces)
    final = spans is not None
    extra = words + 8 * TILE
    moved = rows + extra if final else rows
    grads = (shape((words, width), F32), shape((ents, width), F32)) if final else (shape((total, width), F32),)
    return pl.pallas_call(
        partial(attend_back_kernel, words, gw, heads, final, count),
        in_specs=[SMEM] + [VMEM] * 5 + [HBM] * (3 + count) + [VMEM] * (2 * final),
        out_specs=[HBM] * 3 + [VMEM] * len(grads),
        out_shape=(
            far_shape((moved // 2, width), BF16),
            far_shape((moved // 4, width), BF16),
            far_shape((moved // 4, width), BF16),
        )
        + grads,
        scratch_shapes=[pltpu.VMEM((extra, width), BF16)] * final
        + [
            pltpu.VMEM((rows, width), BF16),
            pltpu.VMEM((words, 4 * gw), BF16),
            pltpu.VMEM((ents, 4 * gw), BF16),
            pltpu.VMEM((total, gw), BF16),
        ]
        + [pltpu.VMEM((heads, total, HEAD_DIM), BF16) for _ in range(5)]
        + [
            pltpu.VMEM((total, total), BF16),
            pltpu.VMEM((total, total), BF16),
            pltpu.VMEM((words, 4 * gw), BF16),
            pltpu.VMEM((ents, 4 * gw), BF16),
            pltpu.VMEM((rows, width), BF16),
            DMA((4,)),
        ],
        input_output_aliases={} if final else {5: 3},
        compiler_params=params(24),
        cost_estimate=cost(11, 8),
        name="attend_back",
    )(info, rows_low, lt, low, up_sums, acc, *far((pw, pe, ctx)), *far(pieces), *((spans, sums) if final else ()))


def spread_query_kernel(info_ref, *refs):
    pieces = refs[:8]
    query_ref, key_ref, value_ref, out_ref, qb_ref, vb_ref, ub_ref, s, sem = refs[8:]
    wait(start(place(pieces, info_ref, s.shape[0] // 8, (s,)), sem))
    gw = key_ref.shape[0]
    for i, k in ((0, 0), (1, 1), (2, 4), (3, 5)):
        query_ref[i] = s[k * gw : (k + 1) * gw].astype(F32)
    key_ref[...] = s[2 * gw : 3 * gw].astype(F32)
    value_ref[...] = s[3 * gw : 4 * gw].astype(F32)
    out_ref[...] = s[6 * gw : 7 * gw].astype(F32)
    rows = s[7 * gw : 7 * gw + TILE].astype(F32)
    qb_ref[0:1] = rows[0:1, :gw]
    qb_ref[1:2] = rows[0:1, gw : 2 * gw]
    qb_ref[2:3] = rows[1:2, :gw]
    qb_ref[3:4] = rows[1:2, gw : 2 * gw]
    vb_ref[...] = rows[0:1, 3 * gw :]
    ub_ref[...] = rows[2:3]


def spread_query(info, pieces, gw):
    unit, width = pieces[0].shape
    flat = shape((gw, width), F32)
    return pl.pallas_call(
        spread_query_kernel,
        in_specs=[SMEM] + [HBM] * 8,
        out_specs=[VMEM] * 7,
        out_shape=(
            shape((4, gw, width), F32), flat, flat, flat,
            shape((4, gw), F32), shape((1, gw), F32), shape((1, width), F32),
        ),
        scratch_shapes=[pltpu.VMEM((8 * unit, width), BF16), DMA],
        compiler_params=params(8),
        cost_estimate=cost(0.5, 7),
        name="spread_query",
    )(info, *far(pieces))


def spread_hidden_kernel(info_ref, *refs):
    up_ref, down_ref, up_s, down_s, sem = refs[5:]
    unit = up_ref.shape[0] // 8
    pieces = refs[:4] + tuple((refs[4], 2 * unit * i) for i in range(4))
    wait(start(place(pieces, info_ref, unit, (up_s, down_s)), sem))
    up_ref[...] = up_s[...].astype(F32)
    down_ref[...] = down_s[...].astype(F32)


def spread_hidden(info, pieces):
    rows, width = pieces[0].shape
    out = shape((4 * rows, width), F32)
    return pl.pallas_call(
        spread_hidden_kernel,
        in_specs=[SMEM] + [HBM] * 5,
        out_specs=[VMEM] * 2,
        out_shape=(out, out),
        scratch_shapes=[pltpu.VMEM((4 * rows, width), BF16)] * 2 + [DMA],
        compiler_params=params(9),
        cost_estimate=cost(0.5, 7),
        name="spread_hidden",
    )(info, *far(pieces))


def spread_pos_kernel(info_ref, *refs):
    pieces = refs[:8]
    pos_ref, sums_ref, s, sem = refs[8:]
    step = s.shape[0] // 8
    unit = step - TILE
    wait(start(place(pieces, info_ref, step, (s,)), sem))
    for i in range(8):
        pos_ref[i * unit : (i + 1) * unit] = s[i * step : i * step + unit].astype(F32)
    sums_ref[...] = s[unit:step].astype(F32)[:8]


def spread_pos(info, pieces):
    rows, width = pieces[0].shape
    return pl.pallas_call(
        spread_pos_kernel,
        in_specs=[SMEM] + [HBM] * 8,
        out_specs=[VMEM] * 2,
        out_shape=(shape((8 * (rows - TILE), width), F32), shape((8, width), F32)),
        scratch_shapes=[pltpu.VMEM((8 * rows, width), BF16), DMA],
        compiler_params=params(5),
        cost_estimate=cost(0.5, 3),
        name="spread_pos",
    )(info, *far(pieces))


class Links:
    def __init__(self):
        self.dp = lax.axis_size("dp")
        self.ring = lax.axis_size("tensor")
        dp_index = lax.axis_index("dp")
        self.z = lax.axis_index("tensor")
        self.core = dp_index % 2
        self.bits = (self.dp // 2).bit_length() - 1
        self.bit = [(dp_index // (2 << k)) % 2 for k in range(self.bits)]

    def shift_z(self, v, by):
        n = self.ring
        return lax.ppermute(v, "tensor", [(i, (i + by) % n) for i in range(n)])

    def swap_z(self, v, mask):
        return lax.ppermute(v, "tensor", [(i, i ^ mask) for i in range(self.ring)])

    def swap(self, v, code):
        return lax.ppermute(v, "dp", [(i, i ^ code) for i in range(self.dp)])

    def swap_core(self, v):
        return self.swap(v, 1)

    def first(self, v):
        return lax.ppermute(v, "dp", [(i, i ^ (4 if i % 2 else 2)) for i in range(self.dp)])

    def second(self, v):
        return lax.ppermute(v, "dp", [(i, i ^ (2 if i % 2 else 4)) for i in range(self.dp)])


def after(value, *others):
    return lax.optimization_barrier((value,) + others)[0]


def sync(*values):
    return lax.optimization_barrier(values)


def add_low(*parts):
    total = parts[0].astype(F32)
    for part in parts[1:]:
        total = total + part.astype(F32)
    return total.astype(BF16)


class Blocks:
    def __init__(self, links, send, near, far):
        self.links, self.send, self.near, self.far = links, send, near, far
        self.unit = near.shape[0] // 2

    def one(self):
        return add_low(self.far, self.got[2 * self.unit :])

    def two(self):
        u = self.unit
        return add_low(self.near[u:], self.got[u : 2 * u], self.a[u:])

    def rest(self, low, high, *more):
        value = add_low(self.near[low:high], self.got[low:high], self.a[low:high], self.b[low:high], *more)
        for j in range(2, self.links.bits):
            value = add_low(value, self.links.swap(value, 2 << j))
        return value


def shards(
    word_in,
    entity_in,
    entity_spans,
    word_mask,
    entity_mask,
    pos_table,
    query_w,
    query_b,
    key_w,
    value_w,
    value_b,
    out_w,
    out_b,
    norm1_gain,
    norm1_bias,
    up_w,
    up_b,
    down_w,
    down_b,
    norm2_gain,
    norm2_bias,
    cot_words,
    cot_entities,
):
    links = Links()
    n = links.ring
    z = links.z
    words = cot_words.shape[0]
    ents = cot_entities.shape[0]
    width = word_in.shape[1]
    gw = key_w.shape[1]
    heads = gw // HEAD_DIM
    rows = -(-(7 * gw + 3) // (8 * TILE)) * 8 * TILE
    part = 4 * links.core + 2 * links.bit[0] + links.bit[1]
    info = jnp.stack([z, links.core, part, 2 - links.core]).astype(jnp.int32)

    small = (query_b, value_b[None], up_b[None])
    own = (jnp.swapaxes(query_w, 1, 2), key_w.T, value_w.T, out_w)
    piece_q, piece_f = pack(info, small, own, up_w, down_w, rows)
    first, second, core, shift = links.first, links.second, links.swap_core, links.shift_z
    rows_low, acc = start_rows(info, word_in, entity_in, entity_spans, pos_table, out_b[None], words, ents)
    saved = [None] * n
    biases = [None] * n

    def attend_one(r, acc, pieces, small=()):
        pw, pe, ctx, lt, biases[r], acc = attend(info, rows_low, acc, pieces, words, heads, rows, small)
        saved[r] = (pw, pe, ctx, lt)
        return acc

    v1, v3 = shift(piece_q, 1), shift(piece_q, 3)
    acc, piece_f = sync(acc, piece_f)
    f1, f3 = shift(piece_f, 1), shift(piece_f, 3)
    acc = attend_one(0, acc, own, small)
    acc, v1, v3 = sync(acc, v1, v3)
    a1, b1, v2 = first(v1), second(v1), shift(v1, 1)
    vec = jnp.stack([norm1_gain, norm1_bias, down_b, norm2_gain, norm2_bias] + [down_b] * 3)
    acc, v1, a1, b1, v3, f1, f3, vec = sync(acc, v1, a1, b1, v3, f1, f3, vec)
    c1, kv, ka, kb, a3, b3 = second(a1), core(v1), core(a1), core(b1), first(v3), second(v3)
    acc, c1, kv, ka, kb, v2, f1, v3 = sync(acc, c1, kv, ka, kb, v2, f1, v3)
    kc, f2 = core(c1), shift(f1, 1)
    acc, kc, a3, b3, v2, f3 = sync(acc, kc, a3, b3, v2, f3)
    group_1 = (v1, a1, b1, c1, kv, ka, kb, kc)

    c3, a2, b2, ag, bg = second(a3), first(v2), second(v2), first(f3), second(f3)
    acc = attend_one(1, acc, group_1)
    acc, c3, a2, b2, ag, bg, f1, f2 = sync(acc, c3, a2, b2, ag, bg, f1, f2)
    kv, ka, kb, kc = core(v3), core(a3), core(b3), core(c3)
    far_f = jnp.concatenate([f1, f2], 0)
    acc, kv, ka, kb, kc, far_f, a2, ag, v2 = sync(acc, kv, ka, kb, kc, far_f, a2, ag, v2)
    group_3 = (v3, a3, b3, c3, kv, ka, kb, kc)

    c2, cg, af, kv, ka = second(a2), second(ag), first(far_f), core(v2), core(a2)
    acc = attend_one(3, acc, group_3)
    acc, c2, cg, af, kv, ka, b2, far_f = sync(acc, c2, cg, af, kv, ka, b2, far_f)
    kb, kc = core(b2), core(c2)
    acc, kb, kc, far_f, af, f3, ag, bg = sync(acc, kb, kc, far_f, af, f3, ag, bg)
    group_2 = (v2, a2, b2, c2, kv, ka, kb, kc)

    bf, cf, kv_g, ka_g, kb_g = second(far_f), second(af), core(f3), core(ag), core(bg)
    acc = attend_one(2, acc, group_2)
    acc, bf, cf, kv_g, ka_g, kb_g, cg, af, far_f = sync(acc, bf, cf, kv_g, ka_g, kb_g, cg, af, far_f)
    attended = acc
    ffn_pieces = (
        far_f, af, bf, cf, core(far_f), core(af), core(bf), core(cf), f3, ag, bg, cg, kv_g, ka_g, kb_g, core(cg)
    )
    query_groups = (own, group_1, group_2, group_3)

    normed_t, act_t, slope, up, down, out_words, out_ents, mixed_low, acc, sums = hidden(
        info, attended, vec, word_mask, entity_mask, cot_words, cot_entities, biases, (up_w, down_w), ffn_pieces
    )

    size = width // 4
    unit = rows // 8
    up_sums = [None] * n

    def ffn_blocks(group, acc):
        send, near, rest, acc, up_sum = hidden_back(info, group, mixed_low, act_t, slope, normed_t, up, down, acc)
        for k, r in enumerate(group):
            up_sums[r] = up_sum[8 * k : 8 * k + 8]
        return Blocks(links, send, near, rest), acc

    def back(r, acc, *last):
        send, near, rest, *acc = attend_back(
            info, rows_low, saved[r], attended_low, up_sums[r], acc, query_groups[r], words, heads, rows, *last
        )
        return Blocks(links, send, near, rest), *acc

    fa, acc = ffn_blocks((2, 1), acc)
    fa.got = core(fa.send)
    fb, acc = ffn_blocks((3,), acc)
    acc, fa.got = sync(acc, fa.got)
    acc, one_a = sync(acc, fa.one())

    fa.a, fb.got = first(one_a), core(fb.send)
    fc, acc = ffn_blocks((0,), acc)
    acc, fb.got = sync(acc, fb.got)
    one_b = fb.one()
    fc.got = core(fc.send)
    acc, attended_low, sums = norm_back(attended, acc, vec, sums)
    acc, one_b, fc.got = sync(acc, one_b, fc.got)
    acc, one_c = sync(acc, fc.one())

    fb.a, fc.a = first(one_b), first(one_c)
    q1, acc = back(2, acc)
    acc, q1.send, fa.a, fb.a, fc.a = sync(acc, q1.send, fa.a, fb.a, fc.a)
    q1.got = core(q1.send)
    acc, two_a, two_b, two_c, q1.got = sync(acc, fa.two(), fb.two(), fc.two(), q1.got)
    acc, one_1 = sync(acc, q1.one())

    fa.b, fb.b, fc.b, q1.a = second(two_a), second(two_b), second(two_c), first(one_1)
    q2, acc = back(1, acc)
    acc, q2.send, fa.b, fb.b, fc.b, q1.a = sync(acc, q2.send, fa.b, fb.b, fc.b, q1.a)
    q2.got = core(q2.send)
    acc, r2, r3, two_1, q2.got = sync(acc, fa.rest(0, size), fb.rest(0, size), q1.two(), q2.got)
    acc, one_2 = sync(acc, q2.one())

    z2, z3, q1.b, q2.a = shift(r2, -1), shift(r3, -3), second(two_1), first(one_2)
    q3, acc = back(3, acc)
    acc, q3.send, z2, z3, q1.b, q2.a = sync(acc, q3.send, z2, z3, q1.b, q2.a)
    q3.got = core(q3.send)
    acc, r1, value_2, two_2, q3.got = sync(acc, fa.rest(size, 2 * size, z2), q1.rest(0, unit), q2.two(), q3.got)
    acc, one_3 = sync(acc, q3.one())

    z1, y2, q2.b, q3.a = shift(r1, -1), shift(value_2, -1), second(two_2), first(one_3)
    q4, grad_words, grad_ents = back(0, acc, entity_spans, sums)
    q4.send, z1, y2, q2.b, q3.a = sync(q4.send, z1, y2, q2.b, q3.a)

    q4.got = core(q4.send)
    y1, q3.b = shift(q2.rest(0, unit, y2), -1), second(q3.two())
    own_f = fc.rest(0, size, z1, z3)
    q4.a, ga = first(q4.one()), first(own_f)
    q4.a, q3.b, y1, ga, own_f = sync(q4.a, q3.b, y1, ga, own_f)

    q4.b, y3, gb, gc = second(q4.two()), shift(q3.rest(0, unit), -3), second(own_f), second(ga)
    q4.b, y3, gb, gc, own_f, ga = sync(q4.b, y3, gb, gc, own_f, ga)

    pos = q4.rest(unit, q4.unit)
    own_q = q4.rest(0, unit, y1, y3)
    p1, p2, p3 = (links.swap_z(pos, mask) for mask in (1, 2, 3))
    near_f = (own_f, ga, gb, gc)
    qa, far_f = first(own_q), core(jnp.concatenate(near_f, 0))
    p1, p2, p3, qa, own_q, pos, far_f = sync(p1, p2, p3, qa, own_q, pos, far_f)

    pos = ((pos.astype(F32) + p1.astype(F32)) + (p2.astype(F32) + p3.astype(F32))).astype(BF16)
    pa, pb, qb, qc = first(pos), second(pos), second(own_q), second(qa)
    grad_up, grad_down = spread_hidden(info, near_f + (far_f,))
    pa, pb, qb, qc, pos, own_q, qa, grad_up, grad_down = sync(pa, pb, qb, qc, pos, own_q, qa, grad_up, grad_down)
    pc, kv, ka, kb, kc = second(pa), core(own_q), core(qa), core(qb), core(qc)
    kv, ka, kb, kc, pos, pa, pb, pc = sync(kv, ka, kb, kc, pos, pa, pb, pc)
    kp = tuple(core(v) for v in (pos, pa, pb, pc))
    grad_query_t, grad_key_t, grad_value_t, grad_out, grad_query_b, grad_value_b, grad_up_b = spread_query(
        info, (own_q, qa, qb, qc, kv, ka, kb, kc), gw
    )
    grad_query_t, *kp = sync(grad_query_t, *kp)
    pos_sum, total_sums = spread_pos(info, (pos, pa, pb, pc, *kp))
    return (
        out_words,
        out_ents,
        grad_words,
        grad_ents,
        pos_sum,
        jnp.swapaxes(grad_query_t, 1, 2),
        grad_query_b,
        grad_key_t.T,
        grad_value_t.T,
        grad_value_b[0],
        grad_out,
        total_sums[5],
        total_sums[3],
        total_sums[4],
        grad_up,
        grad_up_b[0],
        grad_down,
        total_sums[2],
        total_sums[0],
        total_sums[1],
    )


def solution(mesh):
    rows = P(("dp", "tensor"), None)
    last = P(None, "tensor")
    placed = (
        P("dp", None),
        P("dp", None),
        P("dp", None, None),
        P("dp", None),
        P("dp", None),
        P(),
        P(None, None, "tensor"),
        last,
        last,
        last,
        P("tensor"),
        P("tensor", None),
        P(),
        P(),
        P(),
        last,
        P("tensor"),
        P("tensor", None),
        P(),
        P(),
        P(),
        rows,
        rows,
    )
    return jax.shard_map(
        shards,
        mesh=mesh,
        in_specs=placed,
        out_specs=(
            rows,
            rows,
            rows,
            rows,
            P(),
            P(None, None, "tensor"),
            last,
            last,
            last,
            P("tensor"),
            P("tensor", None),
            P(),
            P(),
            P(),
            last,
            P("tensor"),
            P("tensor", None),
            P(),
            P(),
            P(),
        ),
        check_vma=False,
    )
```

```python
from functools import partial

import jax
import jax.numpy as jnp
from jax import lax
from jax.experimental import pallas as pl
from jax.experimental.pallas import tpu as pltpu
from jax.sharding import PartitionSpec as P

HEAD_DIM = 64
SCALE = HEAD_DIM**-0.5
norm_epsilon = 1e-12
F32 = jnp.float32
BF16 = jnp.bfloat16
NT = (((1,), (1,)), ((), ()))
TN = (((0,), (0,)), ((), ()))
ERFC_STEP = 0.35
ERFC_POLY = (
    0.1396196249207051,
    0.13989555693599826,
    0.11957015144655456,
    0.10661400019997494,
    -0.025870835326937874,
    0.16337919550284652,
    -0.25954764983005574,
    0.14589250699009862,
    -0.029552569422939476,
)
TILE = 16
VMEM = pl.BlockSpec(memory_space=pltpu.VMEM)
SMEM = pl.BlockSpec(memory_space=pltpu.SMEM)
HBM = pl.BlockSpec(memory_space=pltpu.HBM)
DMA = pltpu.SemaphoreType.DMA


def mm(a, b):
    return jnp.dot(a, b, preferred_element_type=F32)


def mm_nt(a, b):
    return lax.dot_general(a, b, NT, preferred_element_type=F32)


def mm_tn(a, b):
    return lax.dot_general(a, b, TN, preferred_element_type=F32)


def params(mib):
    return pltpu.CompilerParams(vmem_limit_bytes=mib << 20)


def cost(gflop, mbytes):
    return pl.CostEstimate(
        flops=int(gflop * 1e9), bytes_accessed=int(mbytes * 1e6), transcendentals=0
    )


def shape(dims, kind):
    return jax.ShapeDtypeStruct(dims, kind)


def far(values):
    return tuple(pltpu.with_memory_space_constraint(v, pltpu.HBM) for v in values)


def far_shape(dims, kind):
    return pltpu.HBM(dims, kind)


def start(pairs, sem):
    copies = [pltpu.make_async_copy(source, target, sem) for source, target in pairs]
    for copy in copies:
        copy.start()
    return copies


def wait(copies):
    for copy in copies:
        copy.wait()


def rows_at(first, size):
    return pl.ds(pl.multiple_of(first, TILE), size)


def place(pieces, info_ref, unit, targets, skip=0):
    part, first = info_ref[2], info_ref[3]
    second = 3 - first
    pairs = []
    for piece, code in zip(pieces, (0, first, second, 3, 4, 4 + second, 4 + first, 7)):
        row = lax.bitwise_xor(part, jnp.int32(code)) * unit
        ref, begin = piece if isinstance(piece, tuple) else (piece, skip)
        for t, target in enumerate(targets):
            pairs.append((ref.at[pl.ds(begin + t * unit, unit)], target.at[rows_at(row, unit)]))
    return pairs


def blocks_out(sources, info_ref, send_ref, near_ref, pass_ref):
    part, first = info_ref[2], info_ref[3]
    second = 3 - first
    keep = (0, second, first, 3)
    send = (4, 4 + first, 4 + second, 7)
    total = sum(unit for _, unit in sources)
    pairs = []
    for i in range(4):
        done = 0
        for source, unit in sources:
            other = lax.bitwise_xor(part, jnp.int32(send[i])) * unit
            mine = lax.bitwise_xor(part, jnp.int32(keep[i])) * unit
            to = near_ref if i < 2 else pass_ref
            pairs.append((source.at[rows_at(other, unit)], send_ref.at[pl.ds(i * total + done, unit)]))
            pairs.append((source.at[rows_at(mine, unit)], to.at[pl.ds((i % 2) * total + done, unit)]))
            done += unit
    return pairs


def own_parts(query_ref, key_ref, value_ref, out_ref):
    return (query_ref.at[0], query_ref.at[1], key_ref, value_ref, query_ref.at[2], query_ref.at[3], out_ref)


def spare_rows(qb_ref, vb_ref, ub_ref, spare):
    qb = qb_ref[...].astype(F32)
    none = jnp.zeros((1, qb.shape[1]), F32)
    first = jnp.concatenate([qb[0:1], qb[1:2], none, vb_ref[...].astype(F32)], 1)
    second = jnp.concatenate([qb[2:3], qb[3:4], none, none], 1)
    row = lax.broadcasted_iota(jnp.int32, (spare, first.shape[1]), 0)
    rows = jnp.where(row == 0, first, jnp.where(row == 1, second, jnp.where(row == 2, ub_ref[...].astype(F32), 0.0)))
    return rows.astype(BF16)


def pack_kernel(
    gw, info_ref, qb_ref, vb_ref, ub_ref, query_ref, key_ref, value_ref, ow_ref, up_ref, down_ref,
    piece_ref, ffn_ref, w_s, f_s, sem,
):
    part = info_ref[2]
    size = piece_ref.shape[0]
    low = lax.div(part * size, jnp.int32(gw))
    copies = []
    for i, ref in enumerate(own_parts(query_ref, key_ref, value_ref, ow_ref)):
        needed = jnp.logical_or(low == i, low + 1 == i)
        copies.append((needed, pltpu.make_async_copy(ref, w_s.at[pl.ds(i * gw, gw)], sem.at[0])))
    for needed, copy in copies:
        pl.when(needed)(copy.start)
    unit = f_s.shape[0] // 2
    ffn = start(
        [(v.at[rows_at(part * unit, unit)], f_s.at[pl.ds(i * unit, unit)]) for i, v in enumerate((up_ref, down_ref))],
        sem.at[1],
    )
    w_s[7 * gw :] = spare_rows(qb_ref, vb_ref, ub_ref, w_s.shape[0] - 7 * gw)
    for needed, copy in copies:
        pl.when(needed)(copy.wait)
    piece = start([(w_s.at[rows_at(part * size, size)], piece_ref)], sem.at[2])
    wait(ffn)
    last = start([(f_s, ffn_ref)], sem.at[3])
    wait(piece)
    wait(last)


def pack(info, biases, own, up_w, down_w, rows):
    gw, width = own[1].shape
    unit = up_w.shape[0] // 8
    return pl.pallas_call(
        partial(pack_kernel, gw),
        in_specs=[SMEM] + [VMEM] * 3 + [HBM] * 6,
        out_specs=[HBM] * 2,
        out_shape=(far_shape((rows // 8, width), BF16), far_shape((2 * unit, width), BF16)),
        scratch_shapes=[pltpu.VMEM((rows, width), BF16), pltpu.VMEM((2 * unit, width), BF16), DMA((4,))],
        compiler_params=params(4),
        cost_estimate=cost(0.01, 3),
        name="pack",
    )(info, *biases, *far(own + (up_w, down_w)))


def start_kernel(info_ref, words_ref, ents_ref, spans_ref, table_ref, bias_ref, low_ref, resid_ref, w_s, e_s, t_s, sem):
    words, count = w_s.shape[0], e_s.shape[0]
    z = info_ref[0]
    ents = start(
        [(ents_ref.at[rows_at(z * count, count)], e_s), (table_ref, t_s)],
        sem.at[0],
    )
    reads = start([(words_ref.at[rows_at(z * words, words)], w_s)], sem.at[1])
    spans = spans_ref[z]
    begin = spans[:, 0:1]
    end = spans[:, 1:2]
    position = lax.broadcasted_iota(jnp.int32, (count, words), 1)
    inside = jnp.where(jnp.logical_and(position >= begin, position < end), 1.0, 0.0).astype(BF16)
    share = 1.0 / (end - begin).astype(F32)
    out_b = bias_ref[...].astype(F32)
    wait(ents)
    rows = e_s[...].astype(F32) + mm(inside, t_s[...]) * share
    low_ref[words:] = rows.astype(BF16)
    resid_ref[words:] = rows + out_b
    wait(reads)
    low_ref[:words] = w_s[...]
    resid_ref[:words] = w_s[...].astype(F32) + out_b


def start_rows(info, word_in, entity_in, spans, table, out_b, words, ents):
    width = word_in.shape[1]
    total = words + ents
    return pl.pallas_call(
        start_kernel,
        in_specs=[SMEM, HBM, HBM, VMEM, HBM, VMEM],
        out_specs=[VMEM] * 2,
        out_shape=(shape((total, width), BF16), shape((total, width), F32)),
        scratch_shapes=[
            pltpu.VMEM((words, width), BF16),
            pltpu.VMEM((ents, width), BF16),
            pltpu.VMEM(table.shape, BF16),
            DMA((2,)),
        ],
        compiler_params=params(6),
        cost_estimate=cost(0.5, 6),
        name="start_rows",
    )(info, *far((word_in, entity_in)), spans, *far((table,)), out_b)


def split_heads(words, gw, heads, pw_ref, pe_ref, qw_s, qe_s, k_s, v_s):
    half = 2 * gw
    for h in range(heads):
        o = h * HEAD_DIM
        e = o + HEAD_DIM
        qw_s[h, :words] = pw_ref[:, o:e] * SCALE
        qw_s[h, words:] = pe_ref[:, half + o : half + e] * SCALE
        qe_s[h, :words] = pw_ref[:, gw + o : gw + e] * SCALE
        qe_s[h, words:] = pe_ref[:, half + gw + o : half + gw + e] * SCALE
        k_s[h, :words] = pw_ref[:, half + o : half + e]
        k_s[h, words:] = pe_ref[:, o:e]
        v_s[h, :words] = pw_ref[:, half + gw + o : half + gw + e]
        v_s[h, words:] = pe_ref[:, gw + o : gw + e]


def attend_kernel(words, gw, heads, count, info_ref, rows_ref, acc_ref, *refs):
    own = count == 4
    small, refs = (refs[:3], refs[3:]) if own else ((), refs)
    pieces = refs[:count]
    pw_ref, pe_ref, ctx_ref, lt_ref, bias_ref, out_ref, w_s, pw_s, pe_s, ctx_s, qw_s, qe_s, k_s, v_s, sem = refs[count:]
    half = 2 * gw
    if own:
        reads = start([(v, w_s.at[pl.ds(i * gw, gw)]) for i, v in enumerate(own_parts(*pieces))], sem.at[0])
        w_s[7 * gw :] = spare_rows(*small, w_s.shape[0] - 7 * gw)
        wait(reads)
    else:
        wait(start(place(pieces, info_ref, w_s.shape[0] // 8, (w_s,)), sem.at[0]))
    rows_b = w_s[7 * gw : 7 * gw + TILE]
    bias_ref[...] = rows_b
    rows_b = rows_b.astype(F32)
    bias_e = jnp.concatenate([rows_b[0:1, half:], rows_b[1:2, :half]], 1)
    pw_s[...] = (mm_nt(rows_ref[:words], w_s[: 4 * gw]) + rows_b[0:1]).astype(BF16)
    pe_s[...] = (mm_nt(rows_ref[words:], w_s[half : 6 * gw]) + bias_e).astype(BF16)
    saves = start([(pw_s, pw_ref), (pe_s, pe_ref)], sem.at[1])
    split_heads(words, gw, heads, pw_s, pe_s, qw_s, qe_s, k_s, v_s)
    block = 128

    def step(qb, carry):
        rows = pl.ds(pl.multiple_of(qb * block, block), block)
        parts = []
        for h in range(heads):
            sw = mm_nt(qw_s[h, rows], k_s[h, :words])
            se = mm_nt(qe_s[h, rows], k_s[h, words:])
            top = jnp.maximum(jnp.max(sw, 1, keepdims=True), jnp.max(se, 1, keepdims=True))
            ew = jnp.exp(sw - top)
            ee = jnp.exp(se - top)
            total = jnp.sum(ew, 1, keepdims=True) + jnp.sum(ee, 1, keepdims=True)
            parts.append(
                (mm(ew.astype(BF16), v_s[h, :words]) + mm(ee.astype(BF16), v_s[h, words:])) * (1.0 / total)
            )
            logt = top + jnp.log(total)
            lt_ref[h : h + 1, rows] = jnp.broadcast_to(logt, (block, block)).T[0:1]
        ctx_s[rows, :] = jnp.concatenate(parts, 1).astype(BF16)
        return carry

    lax.fori_loop(0, rows_ref.shape[0] // block, step, 0, unroll=True)
    last = start([(ctx_s, ctx_ref)], sem.at[2])
    out_ref[...] = acc_ref[...] + mm(ctx_s[...], w_s[6 * gw : 7 * gw])
    wait(saves)
    wait(last)


def attend(info, rows_low, acc, pieces, words, heads, rows, small=()):
    total, width = rows_low.shape
    ents = total - words
    gw = heads * HEAD_DIM
    count = len(pieces)
    return pl.pallas_call(
        partial(attend_kernel, words, gw, heads, count),
        in_specs=[SMEM] + [VMEM] * (2 + len(small)) + [HBM] * count,
        out_specs=[HBM] * 3 + [VMEM] * 3,
        out_shape=(
            far_shape((words, 4 * gw), BF16),
            far_shape((ents, 4 * gw), BF16),
            far_shape((total, gw), BF16),
            shape((8, total), F32),
            shape((TILE, width), BF16),
            shape((total, width), F32),
        ),
        scratch_shapes=[
            pltpu.VMEM((rows, width), BF16),
            pltpu.VMEM((words, 4 * gw), BF16),
            pltpu.VMEM((ents, 4 * gw), BF16),
            pltpu.VMEM((total, gw), BF16),
        ]
        + [pltpu.VMEM((heads, total, HEAD_DIM), BF16) for _ in range(4)]
        + [DMA((3,))],
        input_output_aliases={2: 5},
        compiler_params=params(16),
        cost_estimate=cost(8, 6),
        name="attend_own" if small else "attend_far",
    )(info, rows_low, acc, *small, *far(pieces))


def gelu_pair(x):
    size = jnp.abs(x)
    t = 1.0 / (1.0 + ERFC_STEP * size)
    poly = jnp.full_like(x, ERFC_POLY[-1])
    for c in ERFC_POLY[-2::-1]:
        poly = poly * t + c
    bell = jnp.exp(x * x * -0.5)
    tail = poly * t * bell
    below = jnp.where(x >= 0, 1.0 - tail, tail)
    return x * below, below + x * (bell * 0.3989422804014327)


def norm_parts(values):
    centered = values - jnp.mean(values, 1, keepdims=True)
    inv = lax.rsqrt(jnp.mean(centered * centered, 1, keepdims=True) + norm_epsilon)
    return centered * inv, inv


def hidden_kernel(n, info_ref, attended_ref, vec_ref, wm_ref, em_ref, cw_ref, ce_ref, *refs):
    bias_refs, refs = refs[:n], refs[n:]
    up_own, down_own = refs[:2]
    pieces, refs = (refs[2:10], refs[10:18]), refs[18:]
    turn_ref, at_ref, slope_ref, up_s, down_s, ow_ref, oe_ref, mixed_ref, grad_ref, sums_ref, low_ref, acc_s, b_s, sem = refs
    total, width = attended_ref.shape
    unit = width // 8
    reads = [start([(up_own, up_s.at[0]), (down_own, down_s.at[0])], sem.at[0])]
    for r in range(1, n):
        held, skip = pieces[r // 3], 2 * unit * ((r - 1) % 2)
        reads.append(start(place(held, info_ref, unit, (up_s.at[r], down_s.at[r]), skip), sem.at[r]))
    for r in range(n):
        b_s[r] = bias_refs[r][2:3].astype(F32)
    scaled, _ = norm_parts(attended_ref[...])
    normed = scaled * vec_ref[0:1].astype(F32) + vec_ref[1:2].astype(F32)
    low = normed.astype(BF16)
    low_ref[...] = low
    turn_ref[...] = low.T
    acc_s[...] = normed + vec_ref[2:3].astype(F32)
    block = 128

    def group(r):
        for lo in range(0, total, block):
            pre = mm(low_ref[lo : lo + block], up_s[r]) + b_s[r]
            value, slope = gelu_pair(pre)
            slope_ref[r, lo : lo + block] = slope
            value = value.astype(BF16)
            at_ref[r, :, lo : lo + block] = value.T
            acc_s[lo : lo + block] += mm(value, down_s[r])

    for r in range(n):
        wait(reads[r])
        group(r)

    words = cw_ref.shape[0]
    z = info_ref[0]
    scaled, inv = norm_parts(acc_s[...])
    gain = vec_ref[3:4].astype(F32)
    output = scaled * gain + vec_ref[4:5].astype(F32)
    ow_ref[...] = output[:words].astype(BF16)
    oe_ref[...] = output[words:].astype(BF16)

    def column(ref, size):
        return jnp.broadcast_to(ref[pl.ds(z, 1), :].astype(F32), (128, size)).T[:, 0:1]

    cot = jnp.concatenate(
        [
            column(wm_ref, words) * cw_ref[...].astype(F32),
            column(em_ref, total - words) * ce_ref[...].astype(F32),
        ],
        0,
    )
    grad, grad_gain, grad_shift = norm_backward(cot, scaled, inv, gain)
    grad_ref[...] = grad
    mixed_ref[...] = grad.astype(BF16)
    sums_ref[0:1] = grad_gain
    sums_ref[1:2] = grad_shift
    sums_ref[2:3] = jnp.sum(grad, 0, keepdims=True)
    sums_ref[3:] = jnp.zeros((5, width), F32)


def hidden(info, attended, vec, word_mask, entity_mask, cot_words, cot_ents, biases, own, pieces):
    total, width = attended.shape
    n = len(biases)
    return pl.pallas_call(
        partial(hidden_kernel, n),
        in_specs=[SMEM] + [VMEM] * (6 + n) + [HBM] * (2 + len(pieces)),
        out_specs=[VMEM] * 10,
        out_shape=(
            shape((width, total), BF16),
            shape((n, width, total), BF16),
            shape((n, total, width), F32),
            shape((n, width, width), BF16),
            shape((n, width, width), BF16),
            shape(cot_words.shape, BF16),
            shape(cot_ents.shape, BF16),
            shape((total, width), BF16),
            shape((total, width), F32),
            shape((8, width), F32),
        ),
        scratch_shapes=[
            pltpu.VMEM((total, width), BF16),
            pltpu.VMEM((total, width), F32),
            pltpu.VMEM((n, 1, width), F32),
            DMA((n,)),
        ],
        compiler_params=params(18),
        cost_estimate=cost(22, 20),
        name="hidden",
    )(info, attended, vec, word_mask, entity_mask, cot_words, cot_ents, *biases, *far(own), *far(pieces))


def norm_backward(grad_in, scaled, inv_std, gain_row):
    grad_gain = jnp.sum(grad_in * scaled, axis=0, keepdims=True)
    grad_shift = jnp.sum(grad_in, axis=0, keepdims=True)
    grad_scaled = grad_in * gain_row
    mean_first = jnp.mean(grad_scaled, axis=1, keepdims=True)
    mean_second = jnp.mean(grad_scaled * scaled, axis=1, keepdims=True)
    return inv_std * (grad_scaled - mean_first - scaled * mean_second), grad_gain, grad_shift


def hidden_back_kernel(
    pair, info_ref, low_ref, at_ref, slope_ref, turn_ref, up_ref, down_ref, acc_ref,
    send_ref, near_ref, pass_ref, out_ref, b_ref, *refs,
):
    full, sem = refs[:-1], refs[-1]
    unit = turn_ref.shape[0] // 8
    low = low_ref[...]
    out_ref[...] = acc_ref[...]
    for k, r in enumerate(pair):
        grad_down = mm(at_ref[r], low).astype(BF16)
        for i in range(8):
            full[k][(2 * i + 1) * unit : (2 * i + 2) * unit] = grad_down[i * unit : (i + 1) * unit]
        pre_low = (mm_nt(low, down_ref[r]) * slope_ref[r]).astype(BF16)
        grad_up = mm(turn_ref[...], pre_low).astype(BF16)
        for i in range(8):
            full[k][2 * i * unit : (2 * i + 1) * unit] = grad_up[i * unit : (i + 1) * unit]
        b_ref[8 * k : 8 * k + 8] = jnp.broadcast_to(jnp.sum(pre_low.astype(F32), 0, keepdims=True), (8, b_ref.shape[1]))
        out_ref[...] += mm_nt(pre_low, up_ref[r])
    wait(start(blocks_out([(f, 2 * unit) for f in full], info_ref, send_ref, near_ref, pass_ref), sem))


def hidden_back(info, pair, mixed_low, act_t, slope, normed_t, up, down, acc):
    total, width = mixed_low.shape
    k = len(pair)
    return pl.pallas_call(
        partial(hidden_back_kernel, pair),
        in_specs=[SMEM] + [VMEM] * 7,
        out_specs=[HBM] * 3 + [VMEM] * 2,
        out_shape=(
            far_shape((k * width, width), BF16),
            far_shape((k * width // 2, width), BF16),
            far_shape((k * width // 2, width), BF16),
            shape((total, width), F32),
            shape((8 * k, width), F32),
        ),
        scratch_shapes=[pltpu.VMEM((2 * width, width), BF16) for _ in pair] + [DMA],
        input_output_aliases={7: 3},
        compiler_params=params(12),
        cost_estimate=cost(7 * k, 8 * k),
        name="hidden_back",
    )(info, mixed_low, act_t, slope, normed_t, up, down, acc)


def norm_back_kernel(attended_ref, grad_ref, vec_ref, sums_ref, out_ref, low_ref, all_ref):
    scaled, inv = norm_parts(attended_ref[...])
    grad, grad_gain, grad_shift = norm_backward(grad_ref[...], scaled, inv, vec_ref[0:1].astype(F32))
    out_ref[...] = grad
    low_ref[...] = grad.astype(BF16)
    all_ref[...] = sums_ref[...]
    all_ref[3:4] = grad_gain
    all_ref[4:5] = grad_shift
    all_ref[5:6] = jnp.sum(grad, 0, keepdims=True)


def norm_back(attended, grad, vec, sums):
    total, width = attended.shape
    return pl.pallas_call(
        norm_back_kernel,
        in_specs=[VMEM] * 4,
        out_specs=[VMEM] * 3,
        out_shape=(shape((total, width), F32), shape((total, width), BF16), shape((8, width), F32)),
        input_output_aliases={1: 0},
        compiler_params=params(8),
        cost_estimate=cost(2, 6),
        name="norm_back",
    )(attended, grad, vec, sums)


def attend_back_kernel(words, gw, heads, final, count, info_ref, rows_ref, lt_ref, low_ref, up_ref, acc_ref, *refs):
    pw_ref, pe_ref, ctx_ref = refs[:3]
    pieces, refs = refs[3 : 3 + count], refs[3 + count :]
    if final:
        spans_ref, sums_ref, send_ref, near_ref, pass_ref, words_ref, ents_ref, pos_s, *refs = refs
    else:
        send_ref, near_ref, pass_ref, out_ref, *refs = refs
    (
        w_s, pw_s, pe_s, ctx_s, qw_s, qe_s, k_s, v_s, dc_s, p_s, ds_s, dpw_s, dpe_s, full_s, sem,
    ) = refs
    half = 2 * gw
    total = rows_ref.shape[0]
    size = w_s.shape[0] // 8
    saved = start([(pw_ref, pw_s), (pe_ref, pe_s)], sem.at[0])
    if count == 4:
        reads = start([(v, w_s.at[pl.ds(i * gw, gw)]) for i, v in enumerate(own_parts(*pieces))], sem.at[1])
    else:
        reads = start(place(pieces, info_ref, size, (w_s,)), sem.at[1])
    last = start([(ctx_ref, ctx_s)], sem.at[2])
    wait(saved)
    split_heads(words, gw, heads, pw_s, pe_s, qw_s, qe_s, k_s, v_s)
    wait(reads)
    grad_ctx = mm_nt(low_ref[...], w_s[6 * gw : 7 * gw]).astype(BF16)
    for h in range(heads):
        dc_s[h] = grad_ctx[:, h * HEAD_DIM : (h + 1) * HEAD_DIM]
    wait(last)
    full_s[6 * gw : 7 * gw] = mm_tn(ctx_s[...], low_ref[...]).astype(BF16)
    for h in range(heads):
        o = h * HEAD_DIM
        e = o + HEAD_DIM
        logt = lt_ref[h : h + 1]
        pw = jnp.exp(mm_nt(k_s[h, :words], qw_s[h]) - logt)
        pe = jnp.exp(mm_nt(k_s[h, words:], qe_s[h]) - logt)
        gw_ = mm_nt(v_s[h, :words], dc_s[h])
        ge_ = mm_nt(v_s[h, words:], dc_s[h])
        p_s[:words] = pw.astype(BF16)
        p_s[words:] = pe.astype(BF16)
        dot = jnp.sum(pw * gw_, 0, keepdims=True) + jnp.sum(pe * ge_, 0, keepdims=True)
        ds_s[:words] = (pw * (gw_ - dot)).astype(BF16)
        ds_s[words:] = (pe * (ge_ - dot)).astype(BF16)
        dv = mm(p_s[...], dc_s[h]).astype(BF16)
        dkw = mm(ds_s[:words], qw_s[h]).astype(BF16)
        dke = mm(ds_s[words:], qe_s[h]).astype(BF16)
        dqw = (mm_tn(ds_s[:words], k_s[h, :words]) * SCALE).astype(BF16)
        dqe = (mm_tn(ds_s[words:], k_s[h, words:]) * SCALE).astype(BF16)
        dpw_s[:, o:e] = dqw[:words]
        dpw_s[:, gw + o : gw + e] = dqe[:words]
        dpw_s[:, half + o : half + e] = dkw
        dpw_s[:, half + gw + o : half + gw + e] = dv[:words]
        dpe_s[:, o:e] = dke
        dpe_s[:, gw + o : gw + e] = dv[words:]
        dpe_s[:, half + o : half + e] = dqw[words:]
        dpe_s[:, half + gw + o : half + gw + e] = dqe[words:]
    dpw = dpw_s[...]
    dpe = dpe_s[...]
    rows_w = rows_ref[:words]
    rows_e = rows_ref[words:]
    full_s[:half] = mm_tn(dpw[:, :half], rows_w).astype(BF16)
    full_s[half : 2 * half] = (mm_tn(dpw[:, half:], rows_w) + mm_tn(dpe[:, :half], rows_e)).astype(BF16)
    full_s[2 * half : 3 * half] = mm_tn(dpe[:, half:], rows_e).astype(BF16)
    sw = jnp.sum(dpw.astype(F32), 0, keepdims=True)
    se = jnp.sum(dpe.astype(F32), 0, keepdims=True)
    sum_a = jnp.concatenate([sw[:, :half], sw[:, half:] + se[:, :half]], 1)
    sum_b = jnp.concatenate([se[:, half:], jnp.zeros((1, half), F32)], 1)
    spare = w_s.shape[0] - 7 * gw
    row = lax.broadcasted_iota(jnp.int32, (spare, 2 * half), 0)
    sums = jnp.where(row == 0, sum_a, jnp.where(row == 1, sum_b, jnp.where(row == 2, up_ref[0:1], 0.0)))
    full_s[7 * gw :] = sums.astype(BF16)
    if final:
        grad = acc_ref[words:] + mm(dpe, w_s[half : 3 * half])
        ents_ref[...] = grad
        spans = spans_ref[info_ref[0]]
        begin = spans[:, 0:1]
        end = spans[:, 1:2]
        position = lax.broadcasted_iota(jnp.int32, (total - words, words), 1)
        inside = jnp.where(jnp.logical_and(position >= begin, position < end), 1.0, 0.0).astype(BF16)
        scaled = grad * (1.0 / (end - begin).astype(F32))
        high = scaled.astype(BF16)
        rest = (scaled - high.astype(F32)).astype(BF16)
        pos = (mm_tn(inside, high) + mm_tn(inside, rest)).astype(BF16)
        unit = words // 8
        step = unit + TILE
        for i in range(8):
            pos_s[i * step : i * step + unit] = pos[i * unit : (i + 1) * unit]
            if i:
                pos_s[i * step + unit : (i + 1) * step] = jnp.zeros((TILE, pos.shape[1]), BF16)
        sums = sums_ref[...]
        pos_s[unit:step] = jnp.concatenate([sums, jnp.zeros_like(sums)], 0).astype(BF16)
        sources = [(full_s, size), (pos_s, step)]
        writes = start(blocks_out(sources, info_ref, send_ref, near_ref, pass_ref), sem.at[3])
        words_ref[...] = acc_ref[:words] + mm(dpw, w_s[: 2 * half])
    else:
        writes = start(blocks_out([(full_s, size)], info_ref, send_ref, near_ref, pass_ref), sem.at[3])
        out_ref[:words] = acc_ref[:words] + mm(dpw, w_s[: 2 * half])
        out_ref[words:] = acc_ref[words:] + mm(dpe, w_s[half : 3 * half])
    wait(writes)


def attend_back(info, rows_low, saved, low, up_sums, acc, pieces, words, heads, rows, spans=None, sums=None):
    total, width = rows_low.shape
    pw, pe, ctx, lt = saved
    ents = total - words
    gw = heads * HEAD_DIM
    count = len(pieces)
    final = spans is not None
    extra = words + 8 * TILE
    moved = rows + extra if final else rows
    grads = (shape((words, width), F32), shape((ents, width), F32)) if final else (shape((total, width), F32),)
    return pl.pallas_call(
        partial(attend_back_kernel, words, gw, heads, final, count),
        in_specs=[SMEM] + [VMEM] * 5 + [HBM] * (3 + count) + [VMEM] * (2 * final),
        out_specs=[HBM] * 3 + [VMEM] * len(grads),
        out_shape=(
            far_shape((moved // 2, width), BF16),
            far_shape((moved // 4, width), BF16),
            far_shape((moved // 4, width), BF16),
        )
        + grads,
        scratch_shapes=[pltpu.VMEM((extra, width), BF16)] * final
        + [
            pltpu.VMEM((rows, width), BF16),
            pltpu.VMEM((words, 4 * gw), BF16),
            pltpu.VMEM((ents, 4 * gw), BF16),
            pltpu.VMEM((total, gw), BF16),
        ]
        + [pltpu.VMEM((heads, total, HEAD_DIM), BF16) for _ in range(5)]
        + [
            pltpu.VMEM((total, total), BF16),
            pltpu.VMEM((total, total), BF16),
            pltpu.VMEM((words, 4 * gw), BF16),
            pltpu.VMEM((ents, 4 * gw), BF16),
            pltpu.VMEM((rows, width), BF16),
            DMA((4,)),
        ],
        input_output_aliases={} if final else {5: 3},
        compiler_params=params(24),
        cost_estimate=cost(11, 8),
        name="attend_back",
    )(info, rows_low, lt, low, up_sums, acc, *far((pw, pe, ctx)), *far(pieces), *((spans, sums) if final else ()))


def spread_query_kernel(info_ref, *refs):
    pieces = refs[:8]
    query_ref, key_ref, value_ref, out_ref, qb_ref, vb_ref, ub_ref, s, sem = refs[8:]
    wait(start(place(pieces, info_ref, s.shape[0] // 8, (s,)), sem))
    gw = key_ref.shape[0]
    for i, k in ((0, 0), (1, 1), (2, 4), (3, 5)):
        query_ref[i] = s[k * gw : (k + 1) * gw].astype(F32)
    key_ref[...] = s[2 * gw : 3 * gw].astype(F32)
    value_ref[...] = s[3 * gw : 4 * gw].astype(F32)
    out_ref[...] = s[6 * gw : 7 * gw].astype(F32)
    rows = s[7 * gw : 7 * gw + TILE].astype(F32)
    qb_ref[0:1] = rows[0:1, :gw]
    qb_ref[1:2] = rows[0:1, gw : 2 * gw]
    qb_ref[2:3] = rows[1:2, :gw]
    qb_ref[3:4] = rows[1:2, gw : 2 * gw]
    vb_ref[...] = rows[0:1, 3 * gw :]
    ub_ref[...] = rows[2:3]


def spread_query(info, pieces, gw):
    unit, width = pieces[0].shape
    flat = shape((gw, width), F32)
    return pl.pallas_call(
        spread_query_kernel,
        in_specs=[SMEM] + [HBM] * 8,
        out_specs=[VMEM] * 7,
        out_shape=(
            shape((4, gw, width), F32), flat, flat, flat,
            shape((4, gw), F32), shape((1, gw), F32), shape((1, width), F32),
        ),
        scratch_shapes=[pltpu.VMEM((8 * unit, width), BF16), DMA],
        compiler_params=params(8),
        cost_estimate=cost(0.5, 7),
        name="spread_query",
    )(info, *far(pieces))


def spread_hidden_kernel(info_ref, *refs):
    up_ref, down_ref, up_s, down_s, sem = refs[5:]
    unit = up_ref.shape[0] // 8
    pieces = refs[:4] + tuple((refs[4], 2 * unit * i) for i in range(4))
    wait(start(place(pieces, info_ref, unit, (up_s, down_s)), sem))
    up_ref[...] = up_s[...].astype(F32)
    down_ref[...] = down_s[...].astype(F32)


def spread_hidden(info, pieces):
    rows, width = pieces[0].shape
    out = shape((4 * rows, width), F32)
    return pl.pallas_call(
        spread_hidden_kernel,
        in_specs=[SMEM] + [HBM] * 5,
        out_specs=[VMEM] * 2,
        out_shape=(out, out),
        scratch_shapes=[pltpu.VMEM((4 * rows, width), BF16)] * 2 + [DMA],
        compiler_params=params(9),
        cost_estimate=cost(0.5, 7),
        name="spread_hidden",
    )(info, *far(pieces))


def spread_pos_kernel(info_ref, *refs):
    pieces = refs[:8]
    pos_ref, sums_ref, s, sem = refs[8:]
    step = s.shape[0] // 8
    unit = step - TILE
    wait(start(place(pieces, info_ref, step, (s,)), sem))
    for i in range(8):
        pos_ref[i * unit : (i + 1) * unit] = s[i * step : i * step + unit].astype(F32)
    sums_ref[...] = s[unit:step].astype(F32)[:8]


def spread_pos(info, pieces):
    rows, width = pieces[0].shape
    return pl.pallas_call(
        spread_pos_kernel,
        in_specs=[SMEM] + [HBM] * 8,
        out_specs=[VMEM] * 2,
        out_shape=(shape((8 * (rows - TILE), width), F32), shape((8, width), F32)),
        scratch_shapes=[pltpu.VMEM((8 * rows, width), BF16), DMA],
        compiler_params=params(5),
        cost_estimate=cost(0.5, 3),
        name="spread_pos",
    )(info, *far(pieces))


class Links:
    def __init__(self):
        self.dp = lax.axis_size("dp")
        self.ring = lax.axis_size("tensor")
        dp_index = lax.axis_index("dp")
        self.z = lax.axis_index("tensor")
        self.core = dp_index % 2
        self.bits = (self.dp // 2).bit_length() - 1
        self.bit = [(dp_index // (2 << k)) % 2 for k in range(self.bits)]

    def shift_z(self, v, by):
        n = self.ring
        return lax.ppermute(v, "tensor", [(i, (i + by) % n) for i in range(n)])

    def swap_z(self, v, mask):
        return lax.ppermute(v, "tensor", [(i, i ^ mask) for i in range(self.ring)])

    def swap(self, v, code):
        return lax.ppermute(v, "dp", [(i, i ^ code) for i in range(self.dp)])

    def swap_core(self, v):
        return self.swap(v, 1)

    def first(self, v):
        return lax.ppermute(v, "dp", [(i, i ^ (4 if i % 2 else 2)) for i in range(self.dp)])

    def second(self, v):
        return lax.ppermute(v, "dp", [(i, i ^ (2 if i % 2 else 4)) for i in range(self.dp)])


def after(value, *others):
    return lax.optimization_barrier((value,) + others)[0]


def sync(*values):
    return lax.optimization_barrier(values)


def add_low(*parts):
    total = parts[0].astype(F32)
    for part in parts[1:]:
        total = total + part.astype(F32)
    return total.astype(BF16)


class Blocks:
    def __init__(self, links, send, near, far):
        self.links, self.send, self.near, self.far = links, send, near, far
        self.unit = near.shape[0] // 2

    def one(self):
        return add_low(self.far, self.got[2 * self.unit :])

    def two(self):
        u = self.unit
        return add_low(self.near[u:], self.got[u : 2 * u], self.a[u:])

    def rest(self, low, high, *more):
        value = add_low(self.near[low:high], self.got[low:high], self.a[low:high], self.b[low:high], *more)
        for j in range(2, self.links.bits):
            value = add_low(value, self.links.swap(value, 2 << j))
        return value


def shards(
    word_in,
    entity_in,
    entity_spans,
    word_mask,
    entity_mask,
    pos_table,
    query_w,
    query_b,
    key_w,
    value_w,
    value_b,
    out_w,
    out_b,
    norm1_gain,
    norm1_bias,
    up_w,
    up_b,
    down_w,
    down_b,
    norm2_gain,
    norm2_bias,
    cot_words,
    cot_entities,
):
    links = Links()
    n = links.ring
    z = links.z
    words = cot_words.shape[0]
    ents = cot_entities.shape[0]
    width = word_in.shape[1]
    gw = key_w.shape[1]
    heads = gw // HEAD_DIM
    rows = -(-(7 * gw + 3) // (8 * TILE)) * 8 * TILE
    part = 4 * links.core + 2 * links.bit[0] + links.bit[1]
    info = jnp.stack([z, links.core, part, 2 - links.core]).astype(jnp.int32)

    small = (query_b, value_b[None], up_b[None])
    own = (jnp.swapaxes(query_w, 1, 2), key_w.T, value_w.T, out_w)
    piece_q, piece_f = pack(info, small, own, up_w, down_w, rows)
    first, second, core, shift = links.first, links.second, links.swap_core, links.shift_z
    rows_low, acc = start_rows(info, word_in, entity_in, entity_spans, pos_table, out_b[None], words, ents)
    saved = [None] * n
    biases = [None] * n

    def attend_one(r, acc, pieces, small=()):
        pw, pe, ctx, lt, biases[r], acc = attend(info, rows_low, acc, pieces, words, heads, rows, small)
        saved[r] = (pw, pe, ctx, lt)
        return acc

    v1, v3 = shift(piece_q, 1), shift(piece_q, 3)
    acc, piece_f = sync(acc, piece_f)
    f1, f3 = shift(piece_f, 1), shift(piece_f, 3)
    acc = attend_one(0, acc, own, small)
    acc, v1, v3 = sync(acc, v1, v3)
    a1, b1, v2 = first(v1), second(v1), shift(v1, 1)
    vec = jnp.stack([norm1_gain, norm1_bias, down_b, norm2_gain, norm2_bias] + [down_b] * 3)
    acc, v1, a1, b1, v3, f1, f3, vec = sync(acc, v1, a1, b1, v3, f1, f3, vec)
    c1, kv, ka, kb, a3, b3 = second(a1), core(v1), core(a1), core(b1), first(v3), second(v3)
    acc, c1, kv, ka, kb, v2, f1, v3 = sync(acc, c1, kv, ka, kb, v2, f1, v3)
    kc, f2 = core(c1), shift(f1, 1)
    acc, kc, a3, b3, v2, f3 = sync(acc, kc, a3, b3, v2, f3)
    group_1 = (v1, a1, b1, c1, kv, ka, kb, kc)

    c3, a2, b2, ag, bg = second(a3), first(v2), second(v2), first(f3), second(f3)
    acc = attend_one(1, acc, group_1)
    acc, c3, a2, b2, ag, bg, f1, f2 = sync(acc, c3, a2, b2, ag, bg, f1, f2)
    kv, ka, kb, kc = core(v3), core(a3), core(b3), core(c3)
    far_f = jnp.concatenate([f1, f2], 0)
    acc, kv, ka, kb, kc, far_f, a2, ag, v2 = sync(acc, kv, ka, kb, kc, far_f, a2, ag, v2)
    group_3 = (v3, a3, b3, c3, kv, ka, kb, kc)

    c2, cg, af, kv, ka = second(a2), second(ag), first(far_f), core(v2), core(a2)
    acc = attend_one(3, acc, group_3)
    acc, c2, cg, af, kv, ka, b2, far_f = sync(acc, c2, cg, af, kv, ka, b2, far_f)
    kb, kc = core(b2), core(c2)
    acc, kb, kc, far_f, af, f3, ag, bg = sync(acc, kb, kc, far_f, af, f3, ag, bg)
    group_2 = (v2, a2, b2, c2, kv, ka, kb, kc)

    bf, cf, kv_g, ka_g, kb_g = second(far_f), second(af), core(f3), core(ag), core(bg)
    acc = attend_one(2, acc, group_2)
    acc, bf, cf, kv_g, ka_g, kb_g, cg, af, far_f = sync(acc, bf, cf, kv_g, ka_g, kb_g, cg, af, far_f)
    attended = acc
    ffn_pieces = (
        far_f, af, bf, cf, core(far_f), core(af), core(bf), core(cf), f3, ag, bg, cg, kv_g, ka_g, kb_g, core(cg)
    )
    query_groups = (own, group_1, group_2, group_3)

    normed_t, act_t, slope, up, down, out_words, out_ents, mixed_low, acc, sums = hidden(
        info, attended, vec, word_mask, entity_mask, cot_words, cot_entities, biases, (up_w, down_w), ffn_pieces
    )

    size = width // 4
    unit = rows // 8
    up_sums = [None] * n

    def ffn_blocks(group, acc):
        send, near, rest, acc, up_sum = hidden_back(info, group, mixed_low, act_t, slope, normed_t, up, down, acc)
        for k, r in enumerate(group):
            up_sums[r] = up_sum[8 * k : 8 * k + 8]
        return Blocks(links, send, near, rest), acc

    def back(r, acc, *last):
        send, near, rest, *acc = attend_back(
            info, rows_low, saved[r], attended_low, up_sums[r], acc, query_groups[r], words, heads, rows, *last
        )
        return Blocks(links, send, near, rest), *acc

    fa, acc = ffn_blocks((2, 1), acc)
    fa.got = core(fa.send)
    fb, acc = ffn_blocks((3,), acc)
    acc, fa.got = sync(acc, fa.got)
    acc, one_a = sync(acc, fa.one())

    fa.a, fb.got = first(one_a), core(fb.send)
    fc, acc = ffn_blocks((0,), acc)
    acc, fb.got = sync(acc, fb.got)
    one_b = fb.one()
    fc.got = core(fc.send)
    acc, attended_low, sums = norm_back(attended, acc, vec, sums)
    acc, one_b, fc.got = sync(acc, one_b, fc.got)
    acc, one_c = sync(acc, fc.one())

    fb.a, fc.a = first(one_b), first(one_c)
    q1, acc = back(2, acc)
    acc, q1.send, fa.a, fb.a = sync(acc, q1.send, fa.a, fb.a)
    q1.got = core(q1.send)
    acc, two_a, two_b, q1.got = sync(acc, fa.two(), fb.two(), q1.got)
    acc, one_1 = sync(acc, q1.one())

    fa.b, fb.b, q1.a = second(two_a), second(two_b), first(one_1)
    q2, acc = back(1, acc)
    acc, q2.send, fa.b, fb.b, fc.a, q1.a = sync(acc, q2.send, fa.b, fb.b, fc.a, q1.a)
    q2.got = core(q2.send)
    acc, r2, r3, two_c, two_1, q2.got = sync(
        acc, fa.rest(0, size), fb.rest(0, size), fc.two(), q1.two(), q2.got
    )
    acc, one_2 = sync(acc, q2.one())

    z2, z3, q1.b, q2.a, fc.b = shift(r2, -1), shift(r3, -3), second(two_1), first(one_2), second(two_c)
    q3, acc = back(3, acc)
    acc, q3.send, z2, z3, q1.b, q2.a, fc.b = sync(acc, q3.send, z2, z3, q1.b, q2.a, fc.b)
    q3.got = core(q3.send)
    acc, r1, value_2, two_2, q3.got = sync(acc, fa.rest(size, 2 * size, z2), q1.rest(0, unit), q2.two(), q3.got)
    acc, one_3 = sync(acc, q3.one())

    z1, y2, q2.b, q3.a = shift(r1, -1), shift(value_2, -1), second(two_2), first(one_3)
    q4, grad_words, grad_ents = back(0, acc, entity_spans, sums)
    q4.send, z1, y2, q2.b, q3.a = sync(q4.send, z1, y2, q2.b, q3.a)

    q4.got = core(q4.send)
    y1, q3.b = shift(q2.rest(0, unit, y2), -1), second(q3.two())
    own_f = fc.rest(0, size, z1, z3)
    q4.a, ga = first(q4.one()), first(own_f)
    q4.a, q3.b, y1, ga, own_f = sync(q4.a, q3.b, y1, ga, own_f)

    q4.b, y3, gb, gc = second(q4.two()), shift(q3.rest(0, unit), -3), second(own_f), second(ga)
    q4.b, y3, gb, gc, own_f, ga = sync(q4.b, y3, gb, gc, own_f, ga)

    pos = q4.rest(unit, q4.unit)
    own_q = q4.rest(0, unit, y1, y3)
    p1, p2, p3 = (links.swap_z(pos, mask) for mask in (1, 2, 3))
    near_f = (own_f, ga, gb, gc)
    qa, far_f = first(own_q), core(jnp.concatenate(near_f, 0))
    p1, p2, p3, qa, own_q, pos, far_f = sync(p1, p2, p3, qa, own_q, pos, far_f)

    pos = ((pos.astype(F32) + p1.astype(F32)) + (p2.astype(F32) + p3.astype(F32))).astype(BF16)
    pa, pb, qb, qc = first(pos), second(pos), second(own_q), second(qa)
    grad_up, grad_down = spread_hidden(info, near_f + (far_f,))
    pa, pb, qb, qc, pos, own_q, qa, grad_up, grad_down = sync(pa, pb, qb, qc, pos, own_q, qa, grad_up, grad_down)
    pc, kv, ka, kb, kc = second(pa), core(own_q), core(qa), core(qb), core(qc)
    kv, ka, kb, kc, pos, pa, pb, pc = sync(kv, ka, kb, kc, pos, pa, pb, pc)
    kp = tuple(core(v) for v in (pos, pa, pb, pc))
    grad_query_t, grad_key_t, grad_value_t, grad_out, grad_query_b, grad_value_b, grad_up_b = spread_query(
        info, (own_q, qa, qb, qc, kv, ka, kb, kc), gw
    )
    grad_query_t, *kp = sync(grad_query_t, *kp)
    pos_sum, total_sums = spread_pos(info, (pos, pa, pb, pc, *kp))
    return (
        out_words,
        out_ents,
        grad_words,
        grad_ents,
        pos_sum,
        jnp.swapaxes(grad_query_t, 1, 2),
        grad_query_b,
        grad_key_t.T,
        grad_value_t.T,
        grad_value_b[0],
        grad_out,
        total_sums[5],
        total_sums[3],
        total_sums[4],
        grad_up,
        grad_up_b[0],
        grad_down,
        total_sums[2],
        total_sums[0],
        total_sums[1],
    )


def solution(mesh):
    rows = P(("dp", "tensor"), None)
    last = P(None, "tensor")
    placed = (
        P("dp", None),
        P("dp", None),
        P("dp", None, None),
        P("dp", None),
        P("dp", None),
        P(),
        P(None, None, "tensor"),
        last,
        last,
        last,
        P("tensor"),
        P("tensor", None),
        P(),
        P(),
        P(),
        last,
        P("tensor"),
        P("tensor", None),
        P(),
        P(),
        P(),
        rows,
        rows,
    )
    return jax.shard_map(
        shards,
        mesh=mesh,
        in_specs=placed,
        out_specs=(
            rows,
            rows,
            rows,
            rows,
            P(),
            P(None, None, "tensor"),
            last,
            last,
            last,
            P("tensor"),
            P("tensor", None),
            P(),
            P(),
            P(),
            last,
            P("tensor"),
            P("tensor", None),
            P(),
            P(),
            P(),
        ),
        check_vma=False,
    )
```
